32 devices in a mesh: sp: 16 (over z, y, core), flt: 2 (over x).
Axes of the slice: x: 2, y: 2, z: 4, core: 2. Of those that a mesh axis runs over, the one named last changes fastest.
Arguments:
- activations: bfloat16 [32, 16, 8, 256], P('sp', 'flt'), may hold values from -6 to 6
- w_first: bfloat16 [256, 3, 3, 3, 256], P('flt'), may hold values from -0.078125 to 0.078125
- w_second: bfloat16 [256, 3, 3, 3, 256], P('flt'), may hold values from -0.078125 to 0.078125
- cotangent: bfloat16 [16, 8, 4, 256], P('sp', 'flt'), may hold values from -6 to 6
Outputs:
- section_out: float32 [16, 8, 4, 256], P('sp', 'flt')
- grad_input: float32 [32, 16, 8, 256], P('sp', 'flt')
- grad_first: float32 [256, 3, 3, 3, 256], P('flt')
- grad_second: float32 [256, 3, 3, 3, 256], P('flt')
The draws below stay inside these ranges and needn't reach their ends.
All inputs are finite; a program needn't handle non-finite values.
Results may differ from the reference program's by a relative error of at most 0.0045.
Values may be sent and summed in bfloat16 or wider, within the bound.
A program may use at most 64 MiB of HBM per device.

```python
import jax
import jax.numpy as jnp
from jax import lax

C = 256
Z = 8
X = 32
Y = 16


def block_scale(own_key, shape, shards, least, largest):
    def one(axis_at, shards_of):
        draws = jax.random.uniform(jax.random.fold_in(jax.random.fold_in(own_key, 6), axis_at), (shards_of,), jnp.float32, least / len(shards), largest / len(shards))
        return jnp.repeat(jnp.exp(draws), shape[axis_at] // shards_of).reshape((-1,) + (1,) * (len(shape) - axis_at - 1))

    level = one(*shards[0])
    for cut in shards[1:]:
        level = level * one(*cut)
    return level


def gaussian(key, dims, spread, bound, pieces=(), held_as=jnp.bfloat16):
    entries = spread * jax.random.normal(key, dims, jnp.float32)
    if pieces:
        entries = entries * block_scale(key, dims, pieces, -0.22, 0.18)
    return jnp.clip(entries, -bound, bound).astype(held_as)


def setup_inputs(seed: int = 0) -> dict:
    seeds = jax.random.split(jax.random.key(seed), 5)
    return {
        "activations": gaussian(seeds[0], (X, Y, Z, C), 1.0, 6.0, ((0, 16), (1, 2))),
        "w_first": gaussian(seeds[1], (C, 3, 3, 3, C), (27 * C) ** -0.5, 0.078125, ((0, 2),)),
        "w_second": gaussian(seeds[2], (C, 3, 3, 3, C), (27 * C) ** -0.5, 0.078125, ((0, 2),)),
        "cotangent": gaussian(seeds[3], (X // 2, Y // 2, Z // 2, C), 1.0, 6.0, ((0, 16), (1, 2))),
    }


def as_taps(kernel):
    return jnp.transpose(kernel, (1, 2, 3, 4, 0))

def conv_same(field, kernel):
    return lax.conv_general_dilated(field[None].astype(jnp.float32), as_taps(kernel).astype(jnp.float32), (1, 1, 1), ((1, 1), (1, 1), (1, 1)), dimension_numbers=('NDHWC', 'DHWIO', 'NDHWC'), precision=lax.Precision.HIGHEST)[0]

def conv_down(field, kernel):
    return lax.conv_general_dilated(field[None].astype(jnp.float32), as_taps(kernel).astype(jnp.float32), (2, 2, 2), ((1, 0), (1, 0), (1, 0)), dimension_numbers=('NDHWC', 'DHWIO', 'NDHWC'), precision=lax.Precision.HIGHEST)[0]

def silu_slope(value):
    sig = jax.nn.sigmoid(value)
    return sig * (1.0 + value * (1.0 - sig))

def reference(activations, w_first, w_second, cotangent):
    first_pre = conv_same(activations, w_first)
    hidden = jax.nn.silu(first_pre).astype(jnp.bfloat16)
    second_pre = conv_down(hidden, w_second)
    section_out = jax.nn.silu(second_pre)
    second_err = (cotangent.astype(jnp.float32) * silu_slope(second_pre)).astype(jnp.bfloat16)
    unused_two, back_two = jax.vjp(conv_down, hidden.astype(jnp.float32), w_second.astype(jnp.float32))
    hidden_err, grad_second = back_two(second_err.astype(jnp.float32))
    first_err = (hidden_err * silu_slope(first_pre)).astype(jnp.bfloat16)
    unused_one, back_one = jax.vjp(conv_same, activations.astype(jnp.float32), w_first.astype(jnp.float32))
    grad_input, grad_first = back_one(first_err.astype(jnp.float32))
    return (section_out, grad_input, grad_first, grad_second)
```

```python
import functools

import jax
import jax.numpy as jnp
from jax import lax
from jax.experimental import pallas as pl
from jax.experimental.pallas import tpu as pltpu
from jax.sharding import PartitionSpec as P

MESH = pl.DeviceIdType.MESH
VMEM = pl.BlockSpec(memory_space=pltpu.VMEM)
ROOM = 62 * 1024 * 1024


def remote(src, dst, send, recv, place):
    return pltpu.make_async_remote_copy(
        src_ref=src, dst_ref=dst, send_sem=send, recv_sem=recv, device_id=place, device_id_type=MESH
    )


def greet(places):
    barrier = pltpu.get_barrier_semaphore()
    for place in places:
        pl.semaphore_signal(barrier, inc=1, device_id=place, device_id_type=MESH)
    pl.semaphore_wait(barrier, len(places))


def line_kernel(count, own, out, local, recv, send_z, send_y, send_c):
    here, other = lax.axis_index("sp"), lax.axis_index("flt")
    deep = count // 4
    z, y, core = here // 4, (here // 2) % 2, here % 2

    def spot(zz, yy, cc):
        return (zz * 2 + yy) * 2 + cc

    far = [lax.rem(z + step, deep) for step in range(1, deep)]
    to_y = (spot(z, 1 - y, core), other)
    to_c = (spot(z, y, 1 - core), other)
    greet([(spot(zz, y, core), other) for zz in far] + [to_y, to_c])
    sends = []

    def push(src, slot, send, place):
        copy = remote(src, out.at[slot], send, recv.at[slot], place)
        copy.start()
        sends.append(copy)

    def arrived(slot):
        remote(own, out.at[slot], send_y.at[0], recv.at[slot], to_y).wait_recv()

    for n, zz in enumerate(far):
        push(own, here, send_z.at[n], (spot(zz, y, core), other))
    push(own, here, send_y.at[0], to_y)
    push(own, here, send_c.at[0], to_c)
    keep = pltpu.make_async_copy(own, out.at[here], local)
    keep.start()
    for n in range(1, deep):
        slot = spot(lax.rem(z + deep - n, deep), y, core)
        arrived(slot)
        push(out.at[slot], slot, send_y.at[n], to_y)
        push(out.at[slot], slot, send_c.at[n], to_c)
    for n in range(deep):
        slot = spot(lax.rem(z + deep - n, deep), 1 - y, core)
        arrived(slot)
        push(out.at[slot], slot, send_c.at[deep + n], to_c)
    for n in range(deep):
        for yy in (y, 1 - y):
            arrived(spot(lax.rem(z + deep - n, deep), yy, 1 - core))
    keep.wait()
    for copy in sends:
        copy.wait_send()


def gather_line(block, number):
    count = lax.axis_size("sp")
    deep = count // 4
    dma = pltpu.SemaphoreType.DMA
    return pl.pallas_call(
        functools.partial(line_kernel, count),
        out_shape=jax.ShapeDtypeStruct((count,) + block.shape, block.dtype),
        in_specs=[VMEM],
        out_specs=VMEM,
        scratch_shapes=[dma, dma((count,)), dma((max(deep - 1, 1),)), dma((deep,)), dma((2 * deep,))],
        compiler_params=pltpu.CompilerParams(
            collective_id=number, has_side_effects=True, vmem_limit_bytes=ROOM
        ),
    )(block)


def swap_kernel(count, split, *refs):
    kinds = len(split)
    ins, outs = refs[:kinds], refs[kinds : 2 * kinds]
    local, send, recv = refs[2 * kinds :]
    here, me = lax.axis_index("sp"), lax.axis_index("flt")
    peers = [lax.rem(me + step, count) for step in range(1, count)]
    greet([(here, peer) for peer in peers])
    sends, keeps = [], []
    for k in range(kinds):
        for n, peer in enumerate(peers):
            src = ins[k].at[peer] if split[k] else ins[k]
            copy = remote(src, outs[k].at[me], send.at[k, n], recv.at[k, me], (here, peer))
            copy.start()
            sends.append(copy)
        keep = pltpu.make_async_copy(ins[k].at[me] if split[k] else ins[k], outs[k].at[me], local.at[k])
        keep.start()
        keeps.append(keep)
    for k in range(kinds):
        for n, peer in enumerate(peers):
            src = ins[k].at[peer] if split[k] else ins[k]
            remote(src, outs[k].at[peer], send.at[k, n], recv.at[k, peer], (here, peer)).wait_recv()
    for copy in sends:
        copy.wait_send()
    for keep in keeps:
        keep.wait()


def swap(number, *pieces):
    count = lax.axis_size("flt")
    split = tuple(cut for _, cut in pieces)
    arrays = [array for array, _ in pieces]
    dma = pltpu.SemaphoreType.DMA
    shapes = [a.shape if cut else (count,) + a.shape for a, cut in pieces]
    return pl.pallas_call(
        functools.partial(swap_kernel, count, split),
        out_shape=[jax.ShapeDtypeStruct(s, a.dtype) for s, a in zip(shapes, arrays)],
        in_specs=[VMEM] * len(arrays),
        out_specs=[VMEM] * len(arrays),
        scratch_shapes=[
            dma((len(arrays),)),
            dma((len(arrays), max(count - 1, 1))),
            dma((len(arrays), count)),
        ],
        compiler_params=pltpu.CompilerParams(
            collective_id=number, has_side_effects=True, vmem_limit_bytes=ROOM
        ),
    )(*arrays)


def first_kernel(high, wide, x_ref, e_ref, out_ref, moved):
    planes, flat, outs = e_ref.shape
    lane = lax.broadcasted_iota(jnp.int32, (outs, flat), 1)
    row, col = lane // wide, lane % wide
    blank = jnp.zeros((9 * outs, flat), jnp.bfloat16)
    moved[:, 0:flat] = blank
    moved[:, (planes + 1) * flat : (planes + 2) * flat] = blank

    def fill(plane, carry):
        errors = jnp.transpose(e_ref[plane].astype(jnp.float32))
        start = pl.multiple_of((plane + 1) * flat, flat)
        for ky in range(3):
            for kz in range(3):
                by = (ky - 1) * wide + (kz - 1)
                there_y, there_z = row - (ky - 1), col - (kz - 1)
                inside = (there_y >= 0) & (there_y < high) & (there_z >= 0) & (there_z < wide)
                turned_by = pltpu.roll(errors, by % flat, 1) if by else errors
                at = (ky * 3 + kz) * outs
                moved[at : at + outs, pl.ds(start, flat)] = jnp.where(inside, turned_by, 0.0).astype(
                    jnp.bfloat16
                )
        return carry

    lax.fori_loop(0, planes, fill, 0)

    def tap(step, carry):
        kx, ky = step // 3, step % 3
        left = moved[
            pl.ds(pl.multiple_of(ky * 3 * outs, 3 * outs), 3 * outs),
            pl.ds(pl.multiple_of((2 - kx) * flat, flat), planes * flat),
        ]
        out_ref[step] = jnp.dot(left, x_ref[...], preferred_element_type=jnp.float32)
        return carry

    lax.fori_loop(0, 9, tap, 0)


def first_grad(x_cells, errors, high, wide):
    planes, flat, outs = errors.shape
    ins = x_cells.shape[1]
    found = pl.pallas_call(
        functools.partial(first_kernel, high, wide),
        out_shape=jax.ShapeDtypeStruct((9, 3 * outs, ins), jnp.float32),
        in_specs=[VMEM, VMEM],
        out_specs=VMEM,
        scratch_shapes=[pltpu.VMEM((9 * outs, (planes + 2) * flat), jnp.bfloat16)],
        compiler_params=pltpu.CompilerParams(vmem_limit_bytes=ROOM),
        cost_estimate=pl.CostEstimate(
            flops=54 * outs * ins * planes * flat, bytes_accessed=8 * planes * flat * ins, transcendentals=0
        ),
    )(x_cells, errors)
    return jnp.transpose(found.reshape(3, 3, 3, outs, ins), (3, 0, 1, 2, 4))


def second_kernel(high, wide, h_ref, e_ref, out_ref):
    rows, _, flat, ins = h_ref.shape
    cells, outs = e_ref.shape
    errors = jnp.transpose(e_ref[...].astype(jnp.float32))
    lane = lax.broadcasted_iota(jnp.int32, (outs, cells), 1)
    col, line, deep = lane % wide, (lane // wide) % high, lane // flat
    found = {}
    for a in range(2):
        for b in range(2):
            for c in range(2):
                by = a * flat + b * wide + c
                ok = (deep + a < rows) & (line + b < high) & (col + c < wide)
                rolled = pltpu.roll(errors, (cells - by) % cells, 1) if by else errors
                found[a, b, c] = jnp.where(ok, rolled, 0.0).astype(jnp.bfloat16)
    for kx in range(3):
        for ky in range(3):
            for kz in range(3):
                kind = ((kx + 1) % 2 * 2 + (ky + 1) % 2) * 2 + (kz + 1) % 2
                left = found[int(kx == 0), int(ky == 0), int(kz == 0)]
                right = h_ref[:, kind].reshape(cells, ins)
                out_ref[(kx * 3 + ky) * 3 + kz] = jnp.dot(
                    left, right, preferred_element_type=jnp.float32
                )


def second_grad(hidden, errors, high, wide):
    rows, _, flat, ins = hidden.shape
    cells, outs = errors.shape
    found = pl.pallas_call(
        functools.partial(second_kernel, high, wide),
        out_shape=jax.ShapeDtypeStruct((27, outs, ins), jnp.float32),
        in_specs=[VMEM, VMEM],
        out_specs=VMEM,
        compiler_params=pltpu.CompilerParams(vmem_limit_bytes=ROOM),
        cost_estimate=pl.CostEstimate(
            flops=54 * outs * ins * cells, bytes_accessed=32 * cells * ins, transcendentals=0
        ),
    )(hidden, errors)
    return jnp.transpose(found.reshape(3, 3, 3, outs, ins), (3, 0, 1, 2, 4))


def shifted(shard, by):
    peers = lax.axis_size("sp")
    pairs = [(i, i + by) for i in range(peers) if 0 <= i + by < peers]
    return lax.ppermute(shard, "sp", pairs)


def conv_plain(field, kernel, strides, pads, dilate):
    return lax.conv_general_dilated(
        field[None],
        kernel,
        strides,
        pads,
        lhs_dilation=dilate,
        dimension_numbers=("NDHWC", "DHWIO", "NDHWC"),
        preferred_element_type=jnp.float32,
    )[0]


def silu_slope(value):
    sig = jax.nn.sigmoid(value)
    return sig * (1.0 + value * (1.0 - sig))


def forward_taps(kernel):
    return jnp.transpose(kernel, (1, 2, 3, 4, 0))


def turned(kernel):
    return jnp.transpose(kernel[:, ::-1, ::-1, ::-1], (1, 2, 3, 0, 4))


def window(whole, below, above, start, size):
    padded = jnp.pad(whole, ((below, above),) + ((0, 0),) * (whole.ndim - 1))
    return lax.dynamic_slice_in_dim(padded, start, size, 0)


def cut_last(array, count):
    parts = array.reshape(array.shape[:-1] + (count, array.shape[-1] // count))
    return jnp.moveaxis(parts, -2, 0)


def cut_rows(array, count):
    parts = array.reshape((array.shape[0], count, array.shape[1] // count) + array.shape[2:])
    return jnp.moveaxis(parts, 1, 0)


def join_rows(parts):
    moved = jnp.moveaxis(parts, 0, 1)
    return moved.reshape((moved.shape[0], moved.shape[1] * moved.shape[2]) + moved.shape[3:])


def join_last(parts):
    moved = jnp.moveaxis(parts, 0, -2)
    return moved.reshape(moved.shape[:-2] + (moved.shape[-2] * moved.shape[-1],))


def own_term(parts_f32, parts_sent, me):
    mine = lax.broadcasted_iota(jnp.int32, (parts_sent.shape[0],) + (1,) * (parts_sent.ndim - 1), 0) == me
    rest = jnp.sum(jnp.where(mine, 0.0, parts_sent.astype(jnp.float32)), 0)
    return rest + lax.dynamic_index_in_dim(parts_f32, me, 0, keepdims=False)


def per_device(activations, w_first, w_second, cotangent):
    planes = activations.shape[0]
    rows = cotangent.shape[0]
    place, me = lax.axis_index("sp"), lax.axis_index("flt")
    count = lax.axis_size("flt")
    line = lax.axis_size("sp")
    single = (1, 1, 1)
    double = (2, 2, 2)
    x_parts, cot_parts = swap(1, (activations, False), (cut_last(cotangent, count), True))
    x_wide, cot_part = join_rows(x_parts), join_rows(cot_parts)
    high, wide = x_wide.shape[1], x_wide.shape[2]
    ins = x_wide.shape[3]
    x_full = lax.all_gather(x_wide, "sp", axis=0, tiled=True)
    x_near = jnp.concatenate([shifted(x_wide, 1), x_wide, shifted(x_wide[:1], -1)], 0)
    first_pre = conv_plain(x_near, forward_taps(w_first), single, ((0, 0), (1, 1), (1, 1)), single)
    plane = lax.broadcasted_iota(jnp.int32, (planes + 1, 1, 1, 1), 0) + place * planes
    hidden = jnp.where(plane > 0, jax.nn.silu(first_pre), 0.0).astype(jnp.bfloat16)
    (h_parts,) = swap(2, (hidden, False))
    h_wide = join_last(h_parts)
    h_own = h_wide[1:].reshape(rows, 2, high // 2, 2, wide // 2, 2, ins)
    h_own = jnp.transpose(h_own, (0, 1, 3, 5, 2, 4, 6)).reshape(rows, 8, high * wide // 4, ins)
    h_full = lax.all_gather(h_own, "sp", axis=0, tiled=True)
    second_pre = conv_plain(
        h_wide, forward_taps(w_second), double, ((0, 0), (1, 0), (1, 0)), single
    )
    second_err = (cot_part.astype(jnp.float32) * silu_slope(second_pre)).astype(jnp.bfloat16)
    outs = second_err.shape[-1]
    e_full = gather_line(second_err.reshape(-1, outs), 3).reshape((line * rows,) + second_err.shape[1:])
    e_near = window(e_full, 0, 1, place * rows, rows + 1)
    back_hidden = conv_plain(e_near, turned(w_second), single, ((1, 0), (1, 2), (1, 2)), double)
    back_parts = cut_last(back_hidden, count)
    section_parts = cut_rows(jax.nn.silu(second_pre), count)
    got, section_got = swap(4, (back_parts.astype(jnp.bfloat16), True), (section_parts, True))
    section_out = join_last(section_got)
    hidden_err = own_term(back_parts, got, me)
    first_err = (hidden_err * silu_slope(first_pre[1:])).astype(jnp.bfloat16)
    f_full = gather_line(first_err.reshape(planes, high * wide, outs), 5)
    f_full = f_full.reshape(line * planes, high * wide, outs)
    f_near = window(f_full, 1, 1, place * planes, planes + 2).reshape(planes + 2, high, wide, outs)
    back_input = conv_plain(f_near, turned(w_first), single, ((0, 0), (1, 1), (1, 1)), single)
    in_parts = cut_rows(back_input, count)
    (in_got,) = swap(6, (in_parts.astype(jnp.bfloat16), True))
    grad_input = own_term(in_parts, in_got, me)
    grad_second = second_grad(h_full, e_full.reshape(-1, outs), high // 2, wide // 2)
    grad_first = first_grad(x_full.reshape(-1, ins), f_full, high, wide)
    return (section_out, grad_input, grad_first, grad_second)


def slope_of(value):
    sig = 1.0 / (1.0 + jnp.exp(-value))
    return sig * (1.0 + value * (1.0 - sig))


def silu_of(value):
    return value / (1.0 + jnp.exp(-value))


def dot_rows(left, right):
    return lax.dot_general(left, right, (((1,), (1,)), ((), ())), preferred_element_type=jnp.float32)


def dot_plain(left, right):
    return jnp.dot(left, right, preferred_element_type=jnp.float32)


class Line:
    def __init__(self, own, out, local, send, recv, deep, here, other):
        self.own, self.out, self.local, self.send, self.recv = own, out, local, send, recv
        self.deep, self.here, self.other = deep, here, other
        self.z, self.y, self.core = here // 4, (here // 2) % 2, here % 2
        self.to_y = (self.spot(self.z, 1 - self.y, self.core), other)
        self.to_c = (self.spot(self.z, self.y, 1 - self.core), other)
        self.sends = []

    def spot(self, zz, yy, cc):
        return (zz * 2 + yy) * 2 + cc

    def far(self):
        return [
            (self.spot(lax.rem(self.z + step, self.deep), self.y, self.core), self.other)
            for step in range(1, self.deep)
        ]

    def push(self, src, slot, place):
        copy = remote(src, self.out.at[slot], self.send.at[len(self.sends)], self.recv.at[slot], place)
        copy.start()
        self.sends.append(copy)

    def arrived(self, slot):
        remote(self.own, self.out.at[slot], self.send.at[0], self.recv.at[slot], self.to_y).wait_recv()

    def first(self):
        for place in self.far():
            self.push(self.own, self.here, place)
        self.push(self.own, self.here, self.to_y)
        self.push(self.own, self.here, self.to_c)
        self.keep = pltpu.make_async_copy(self.own, self.out.at[self.here], self.local)
        self.keep.start()

    def second(self):
        for n in range(1, self.deep):
            slot = self.spot(lax.rem(self.z + self.deep - n, self.deep), self.y, self.core)
            self.arrived(slot)
            self.push(self.out.at[slot], slot, self.to_y)
            self.push(self.out.at[slot], slot, self.to_c)

    def third(self):
        for n in range(self.deep):
            slot = self.spot(lax.rem(self.z + self.deep - n, self.deep), 1 - self.y, self.core)
            self.arrived(slot)
            self.push(self.out.at[slot], slot, self.to_c)

    def last(self):
        for n in range(self.deep):
            for yy in (self.y, 1 - self.y):
                self.arrived(self.spot(lax.rem(self.z + self.deep - n, self.deep), yy, 1 - self.core))
        self.keep.wait()
        for copy in self.sends:
            copy.wait_send()


def line_sends(deep):
    return (deep - 1) + 2 + 2 * (deep - 1) + deep


def chain_kernel(dims, *refs):
    count, high, wide, ins, outs = dims
    x_hbm, w1_hbm, w2_hbm, cot_hbm = refs[:4]
    sec_out, gin_out, x_full, h_full, e_full, f_full = refs[4:10]
    (
        w1, w2, x_near, cot_near, cot_wide, acc, plain, pre, slope, h_own, h_near, sec, e_own, e_next, back_f, back_b,
        back_got, f_near, f_turn, acc_in, in_b, in_got, own_sem, send_sem, recv_sem, line_local, line_send, line_recv,
    ) = refs[10:]
    flat = high * wide
    nh, nw = high // 2, wide // 2
    cells = nh * nw
    half = flat // 2
    deep = count // 4
    here, me = lax.axis_index("sp"), lax.axis_index("flt")
    mate = 1 - me
    has_up, has_down = here < count - 1, here > 0
    part, up, up_o = (here, mate), (here + 1, me), (here + 1, mate)
    down, down_o = (here - 1, me), (here - 1, mate)
    my_lanes = pl.ds(pl.multiple_of(me * outs, outs), outs)
    mate_lanes = pl.ds(pl.multiple_of(mate * outs, outs), outs)
    my_half = pl.ds(pl.multiple_of(me * half, half), half)
    mate_half = pl.ds(pl.multiple_of(mate * half, half), half)

    load_w1 = pltpu.make_async_copy(w1_hbm, w1, own_sem.at[0])
    load_w2 = pltpu.make_async_copy(w2_hbm, w2, own_sem.at[1])
    load_x = pltpu.make_async_copy(x_hbm, x_near.at[1:3, my_half, :], own_sem.at[2])
    load_cot = pltpu.make_async_copy(
        cot_hbm.at[:, :, my_lanes], cot_near.at[pl.ds(me * (nh // 2), nh // 2)], own_sem.at[3]
    )
    load_x.start()
    load_cot.start()
    load_w1.start()
    load_w2.start()

    def line(number, own, out):
        return Line(
            own, out, line_local.at[number], line_send.at[number], line_recv.at[number], deep, here, me
        )

    x_line = line(0, x_near.at[1:3], x_full)
    h_line = line(1, h_near.at[4:12], h_full)
    e_line = line(2, e_own, e_full)
    f_line = line(3, f_turn, f_full)

    barrier = pltpu.get_barrier_semaphore()

    def hello(place):
        pl.semaphore_signal(barrier, inc=1, device_id=place, device_id_type=MESH)

    always = [part, x_line.to_y, x_line.to_c] + x_line.far()
    for place in always:
        hello(place)

    @pl.when(has_up)
    def _():
        hello(up)
        hello(up_o)

    @pl.when(has_down)
    def _():
        hello(down)
        hello(down_o)

    pl.semaphore_wait(
        barrier, len(always) + 2 * has_up.astype(jnp.int32) + 2 * has_down.astype(jnp.int32)
    )

    started = []

    def send(src, dst, slot, place, cond=None):
        copy = remote(src, dst, send_sem.at[len(started)], recv_sem.at[slot], place)
        if cond is None:
            copy.start()
        else:
            pl.when(cond)(copy.start)
        started.append((copy, cond))

    def wait(src, dst, slot, cond=None):
        copy = remote(src, dst, send_sem.at[0], recv_sem.at[slot], part)
        if cond is None:
            copy.wait_recv()
        else:
            pl.when(cond)(copy.wait_recv)

    send(x_hbm, x_near.at[1:3, my_half, :], 0, part)
    send(x_hbm.at[1], x_near.at[0, my_half, :], 1, up, has_up)
    send(x_hbm.at[1], x_near.at[0, my_half, :], 2, up_o, has_up)
    send(x_hbm.at[0], x_near.at[3, my_half, :], 3, down, has_down)
    send(x_hbm.at[0], x_near.at[3, my_half, :], 4, down_o, has_down)
    cot_rows = pl.ds(me * (nh // 2), nh // 2)
    cot_rows_mate = pl.ds(mate * (nh // 2), nh // 2)
    send(cot_hbm.at[:, :, mate_lanes], cot_near.at[cot_rows], 5, part)

    @pl.when(jnp.logical_not(has_down))
    def _():
        x_near[0] = jnp.zeros((flat, ins), jnp.bfloat16)
        h_near[0:4] = jnp.zeros((4, cells, ins), jnp.bfloat16)
        f_near[0] = jnp.zeros((flat, outs), jnp.bfloat16)

    @pl.when(jnp.logical_not(has_up))
    def _():
        x_near[3] = jnp.zeros((flat, ins), jnp.bfloat16)
        e_next[...] = jnp.zeros((cells, outs), jnp.bfloat16)
        f_near[3] = jnp.zeros((flat, outs), jnp.bfloat16)

    load_x.wait()
    wait(x_hbm, x_near.at[1:3, mate_half, :], 0)
    x_line.first()
    wait(x_hbm.at[1], x_near.at[0, my_half, :], 1, has_down)
    wait(x_hbm.at[1], x_near.at[0, mate_half, :], 2, has_down)
    wait(x_hbm.at[0], x_near.at[3, my_half, :], 3, has_up)
    wait(x_hbm.at[0], x_near.at[3, mate_half, :], 4, has_up)
    load_w1.wait()

    for ky in (1, 0, 2):
        total = None
        for kx in range(3):
            left = x_near[kx : kx + 2].reshape(2 * flat, ins)
            at = kx * 9 + ky * 3
            right = w1[at : at + 3].reshape(3 * outs, ins)
            term = dot_rows(left, right)
            total = term if total is None else total + term
        total = total.reshape(2, flat, 3 * outs)
        if ky == 1:
            acc[...] = total
        elif ky == 0:
            acc[:, wide:, :] += total[:, : flat - wide, :]
        else:
            acc[:, : flat - wide, :] += total[:, wide:, :]
    col = lax.broadcasted_iota(jnp.int32, (2 * flat, outs), 0) % wide
    whole = acc[...].reshape(2 * flat, 3 * outs)
    value = whole[:, outs : 2 * outs]
    value = value + jnp.where(col > 0, pltpu.roll(whole[:, :outs], 1, 0), 0.0)
    value = value + jnp.where(col < wide - 1, pltpu.roll(whole[:, 2 * outs :], 2 * flat - 1, 0), 0.0)
    plain[...] = value

    def pick(px, py, pz, qz):
        return pl.ds(px * flat + py * wide + 2 * qz + pz, nh, 2 * wide)

    for px in (1, 0):
        for py in range(2):
            for pz in range(2):
                kind = (px * 2 + py) * 2 + pz
                found = jnp.concatenate([plain[pick(px, py, pz, qz), :] for qz in range(nw)], 0)
                pre[kind] = found
                h_own[kind] = silu_of(found).astype(jnp.bfloat16)
    send(h_own.at[4:8], h_near.at[0:4, :, my_lanes], 6, up, has_up)
    send(h_own.at[4:8], h_near.at[0:4, :, my_lanes], 7, up_o, has_up)
    send(h_own, h_near.at[4:12, :, my_lanes], 8, part)
    keep_h = pltpu.make_async_copy(h_own, h_near.at[4:12, :, my_lanes], own_sem.at[4])
    keep_h.start()
    load_w2.wait()
    load_cot.wait()
    wait(cot_hbm.at[:, :, my_lanes], cot_near.at[cot_rows_mate], 5)
    cot_wide[...] = cot_near[...].astype(jnp.float32)
    slope[...] = slope_of(pre[...])
    keep_h.wait()
    wait(h_own, h_near.at[4:12, :, mate_lanes], 8)
    h_line.first()
    wait(h_own.at[4:8], h_near.at[0:4, :, my_lanes], 6, has_down)
    wait(h_own.at[4:8], h_near.at[0:4, :, mate_lanes], 7, has_down)

    row = lax.broadcasted_iota(jnp.int32, (cells, outs), 0)
    qy, qz_of = row % nh, row // nh

    def later_y(v):
        return jnp.where(qy > 0, pltpu.roll(v, 1, 0), 0.0)

    def later_z(v):
        return jnp.where(qz_of > 0, pltpu.roll(v, nh, 0), 0.0)

    def earlier_y(v):
        return jnp.where(qy < nh - 1, pltpu.roll(v, cells - 1, 0), 0.0)

    def earlier_z(v):
        return jnp.where(qz_of < nw - 1, pltpu.roll(v, cells - nh, 0), 0.0)

    sums = {}
    for ky in range(3):
        for kz in range(3):
            for kx in range(3):
                kind = kx * 4 + (ky != 1) * 2 + (kz != 1)
                term = dot_rows(h_near[kind], w2[kx * 9 + ky * 3 + kz])
                key = (ky == 0, kz == 0)
                sums[key] = sums[key] + term if key in sums else term
    second = (
        sums[False, False]
        + later_y(sums[True, False] + later_z(sums[True, True]))
        + later_z(sums[False, True])
    )
    cot = jnp.concatenate([cot_wide[:, qz, :] for qz in range(nw)], 0)
    err = (cot * slope_of(second)).astype(jnp.bfloat16)
    e_own[...] = err
    send(e_own, e_next, 9, down, has_down)
    e_line.first()
    shown = silu_of(second)
    for qz in range(nw):
        sec[:, qz, :] = shown[qz * nh : (qz + 1) * nh]
    send(sec.at[cot_rows_mate], sec_out.at[:, :, my_lanes], 10, part)
    keep_sec = pltpu.make_async_copy(sec.at[cot_rows], sec_out.at[:, :, my_lanes], own_sem.at[5])
    keep_sec.start()
    x_line.second()

    wait(e_own, e_next, 9, has_up)

    def variants(block):
        block = block.astype(jnp.float32)
        moved_y = earlier_y(block)
        found = {
            (0, 0): block,
            (1, 0): moved_y,
            (0, 1): earlier_z(block),
            (1, 1): earlier_z(moved_y),
        }
        return {key: v.astype(jnp.bfloat16) for key, v in found.items()}

    e_here, e_after = variants(err), variants(e_next[...])
    for px in range(2):
        for py in range(2):
            for pz in range(2):
                kind = (px * 2 + py) * 2 + pz
                total = None
                for kx in (2, 0) if px else (1,):
                    for ky in (2, 0) if py else (1,):
                        for kz in (2, 0) if pz else (1,):
                            source = e_after if kx == 0 else e_here
                            left = source[int(ky == 0), int(kz == 0)]
                            term = dot_plain(left, w2[kx * 9 + ky * 3 + kz])
                            total = term if total is None else total + term
                for side in range(2):
                    piece = total[:, side * outs : (side + 1) * outs]
                    back_f[side, kind] = piece
                    back_b[side, kind] = piece.astype(jnp.bfloat16)
    send(back_b.at[mate], back_got, 11, part)
    e_line.second()
    x_line.third()
    wait(back_b.at[me], back_got, 11)
    for px in range(2):
        for py in range(2):
            for pz in range(2):
                kind = (px * 2 + py) * 2 + pz
                total = back_f[me, kind] + back_got[kind].astype(jnp.float32)
                found = (total * slope[kind]).astype(jnp.bfloat16).astype(jnp.float32)
                for qz in range(nw):
                    plain[pick(px, py, pz, qz), :] = found[qz * nh : (qz + 1) * nh]
    first = plain[...]
    f_near[1:3] = first.astype(jnp.bfloat16).reshape(2, flat, outs)
    send(f_near.at[1], f_near.at[3], 12, down, has_down)
    send(f_near.at[2], f_near.at[0], 13, up, has_up)
    f_turn[...] = jnp.transpose(first).astype(jnp.bfloat16)
    f_line.first()
    h_line.second()
    wait(f_near.at[1], f_near.at[3], 12, has_up)
    wait(f_near.at[2], f_near.at[0], 13, has_down)

    for kz in range(3):
        for ky in (1, 0, 2):
            total = None
            for kx in range(3):
                left = f_near[2 - kx : 4 - kx].reshape(2 * flat, outs)
                term = dot_plain(left, w1[kx * 9 + ky * 3 + kz])
                total = term if total is None else total + term
            total = total.reshape(2, flat, ins)
            if ky == 1:
                acc_in[kz] = total
            elif ky == 0:
                acc_in[kz, :, : flat - wide, :] += total[:, wide:, :]
            else:
                acc_in[kz, :, wide:, :] += total[:, : flat - wide, :]
    col = lax.broadcasted_iota(jnp.int32, (2 * flat, ins), 0) % wide
    value = acc_in[1].reshape(2 * flat, ins)
    value = value + jnp.where(
        col < wide - 1, pltpu.roll(acc_in[0].reshape(2 * flat, ins), 2 * flat - 1, 0), 0.0
    )
    value = value + jnp.where(col > 0, pltpu.roll(acc_in[2].reshape(2 * flat, ins), 1, 0), 0.0)
    value = value.reshape(2, flat, ins)
    acc_in[1] = value
    in_b[...] = value.astype(jnp.bfloat16)
    send(in_b.at[:, mate_half, :], in_got, 14, part)
    f_line.second()
    h_line.third()
    e_line.third()
    f_line.third()
    wait(in_b.at[:, my_half, :], in_got, 14)
    gin_out[...] = acc_in[1, :, my_half, :] + in_got[...].astype(jnp.float32)
    wait(sec.at[cot_rows], sec_out.at[:, :, mate_lanes], 10)
    keep_sec.wait()
    x_line.last()
    e_line.last()
    h_line.last()
    f_line.last()
    for copy, cond in started:
        if cond is None:
            copy.wait_send()
        else:
            pl.when(cond)(copy.wait_send)


def chain(x, w1, w2, cot):
    count = lax.axis_size("sp")
    planes, high, wide, ins = x.shape
    high = high * 2
    outs = w1.shape[1]
    flat = high * wide
    nh, nw = high // 2, wide // 2
    cells = nh * nw
    deep = count // 4
    dma = pltpu.SemaphoreType.DMA
    bf, f32 = jnp.bfloat16, jnp.float32
    anywhere = pl.BlockSpec(memory_space=pl.ANY)
    shape = jax.ShapeDtypeStruct
    return pl.pallas_call(
        functools.partial(chain_kernel, (count, high, wide, ins, outs)),
        out_shape=[
            shape(cot.shape, f32),
            shape((planes, flat // 2, ins), f32),
            shape((count, planes, flat, ins), bf),
            shape((count, 8, cells, ins), bf),
            shape((count, cells, outs), bf),
            shape((count, outs, planes * flat), bf),
        ],
        in_specs=[anywhere] * 4,
        out_specs=[anywhere, VMEM] + [anywhere] * 4,
        scratch_shapes=[
            pltpu.VMEM(w1.shape, bf),
            pltpu.VMEM(w2.shape, bf),
            pltpu.VMEM((4, flat, ins), bf),
            pltpu.VMEM((nh, nw, outs), bf),
            pltpu.VMEM((nh, nw, outs), f32),
            pltpu.VMEM((2, flat, 3 * outs), f32),
            pltpu.VMEM((2 * flat, outs), f32),
            pltpu.VMEM((8, cells, outs), f32),
            pltpu.VMEM((8, cells, outs), f32),
            pltpu.VMEM((8, cells, outs), bf),
            pltpu.VMEM((12, cells, ins), bf),
            pltpu.VMEM((nh, nw, outs), f32),
            pltpu.VMEM((cells, outs), bf),
            pltpu.VMEM((cells, outs), bf),
            pltpu.VMEM((2, 8, cells, outs), f32),
            pltpu.VMEM((2, 8, cells, outs), bf),
            pltpu.VMEM((8, cells, outs), bf),
            pltpu.VMEM((4, flat, outs), bf),
            pltpu.VMEM((outs, 2 * flat), bf),
            pltpu.VMEM((3, 2, flat, ins), f32),
            pltpu.VMEM((2, flat, ins), bf),
            pltpu.VMEM((2, flat // 2, ins), bf),
            dma((6,)),
            dma((15,)),
            dma((15,)),
            dma((4,)),
            dma((4, line_sends(deep))),
            dma((4, count)),
        ],
        compiler_params=pltpu.CompilerParams(
            collective_id=1, has_side_effects=True, vmem_limit_bytes=ROOM
        ),
    )(x.reshape(planes, flat // 2, ins), w1, w2, cot)


def filter_kernel(dims, *refs):
    high, wide, outs, ins = dims
    sec_in, gin_in, x_hbm, h_hbm, e_hbm, f_hbm = refs[:6]
    sec_out, gin_out, first_out, second_out = refs[6:10]
    x_v, h_v, e_v, f_v, moved, found1, found2, in_sem, out_sem = refs[10:]
    count = f_v.shape[0]
    flat = high * wide
    nh, nw = high // 2, wide // 2
    cells = nh * nw
    loads = [
        pltpu.make_async_copy(src, dst, in_sem.at[n])
        for n, (src, dst) in enumerate(((e_hbm, e_v), (h_hbm, h_v), (f_hbm, f_v), (x_hbm, x_v)))
    ]
    for load in loads:
        load.start()
    outs_going = [
        pltpu.make_async_copy(sec_in, sec_out, out_sem.at[0]),
        pltpu.make_async_copy(gin_in, gin_out, out_sem.at[1]),
    ]
    for copy in outs_going:
        copy.start()

    loads[0].wait()
    total = count * cells
    errors = jnp.transpose(e_v[...].reshape(total, outs).astype(jnp.float32))
    lane = lax.broadcasted_iota(jnp.int32, (outs, total), 1)
    line, col, place = lane % nh, (lane // nh) % nw, lane // cells
    turned_by = {}
    for a in range(2):
        for b in range(2):
            for c in range(2):
                by = a * cells + c * nh + b
                ok = (place + a < count) & (line + b < nh) & (col + c < nw)
                rolled = pltpu.roll(errors, total - by, 1) if by else errors
                turned_by[a, b, c] = jnp.where(ok, rolled, 0.0).astype(jnp.bfloat16)
    loads[1].wait()
    for kx in range(3):
        for ky in range(3):
            for kz in range(3):
                kind = ((kx + 1) % 2 * 2 + (ky + 1) % 2) * 2 + (kz + 1) % 2
                left = turned_by[int(kx == 0), int(ky == 0), int(kz == 0)]
                right = h_v[:, kind].reshape(total, ins)
                found2[(kx * 3 + ky) * 3 + kz] = dot_plain(left, right)
    copy = pltpu.make_async_copy(found2, second_out, out_sem.at[2])
    copy.start()
    outs_going.append(copy)

    loads[2].wait()
    lane = lax.broadcasted_iota(jnp.int32, (outs, flat), 1)
    row, col = lane // wide, lane % wide
    blank = jnp.zeros((9 * outs, flat), jnp.bfloat16)
    moved[:, 0:flat] = blank
    moved[:, (2 * count + 1) * flat : (2 * count + 2) * flat] = blank

    def fill(block, carry):
        for p in range(2):
            errors = f_v[block, :, p * flat : (p + 1) * flat].astype(jnp.float32)
            start = pl.multiple_of((2 * block + p + 1) * flat, flat)
            for ky in range(3):
                for kz in range(3):
                    by = (ky - 1) * wide + (kz - 1)
                    there_y, there_z = row - (ky - 1), col - (kz - 1)
                    inside = (there_y >= 0) & (there_y < high) & (there_z >= 0) & (there_z < wide)
                    rolled = pltpu.roll(errors, by % flat, 1) if by else errors
                    at = (ky * 3 + kz) * outs
                    moved[at : at + outs, pl.ds(start, flat)] = jnp.where(inside, rolled, 0.0).astype(
                        jnp.bfloat16
                    )
        return carry

    lax.fori_loop(0, count, fill, 0)
    loads[3].wait()

    def tap(step, carry):
        kx, ky = step // 3, step % 3
        left = moved[
            pl.ds(pl.multiple_of(ky * 3 * outs, 3 * outs), 3 * outs),
            pl.ds(pl.multiple_of((2 - kx) * flat, flat), 2 * count * flat),
        ]
        found1[step] = dot_plain(left, x_v[...].reshape(2 * count * flat, ins)).reshape(3, outs, ins)
        pltpu.make_async_copy(found1.at[step], first_out.at[step], out_sem.at[3 + step]).start()
        return carry

    lax.fori_loop(0, 9, tap, 0)
    for step in range(9):
        pltpu.make_async_copy(found1.at[step], first_out.at[step], out_sem.at[3 + step]).wait()
    for copy in outs_going:
        copy.wait()


def filters(sec, gin, x_full, h_full, e_full, f_full, high, wide):
    count, _, cells, ins = h_full.shape
    outs = e_full.shape[-1]
    flat = high * wide
    dma = pltpu.SemaphoreType.DMA
    bf, f32 = jnp.bfloat16, jnp.float32
    anywhere = pl.BlockSpec(memory_space=pl.ANY)
    shape = jax.ShapeDtypeStruct
    sec, gin, first, second = pl.pallas_call(
        functools.partial(filter_kernel, (high, wide, outs, ins)),
        out_shape=[
            shape(sec.shape, f32),
            shape(gin.shape, f32),
            shape((9, 3, outs, ins), f32),
            shape((27, outs, ins), f32),
        ],
        in_specs=[anywhere] * 6,
        out_specs=[anywhere] * 4,
        scratch_shapes=[
            pltpu.VMEM(x_full.shape, bf),
            pltpu.VMEM(h_full.shape, bf),
            pltpu.VMEM(e_full.shape, bf),
            pltpu.VMEM(f_full.shape, bf),
            pltpu.VMEM((9 * outs, (2 * count + 2) * flat), bf),
            pltpu.VMEM((9, 3, outs, ins), f32),
            pltpu.VMEM((27, outs, ins), f32),
            dma((4,)),
            dma((12,)),
        ],
        compiler_params=pltpu.CompilerParams(vmem_limit_bytes=ROOM),
    )(sec, gin, x_full, h_full, e_full, f_full)

    def home(found):
        return jnp.transpose(found.reshape(3, 3, 3, outs, ins), (3, 0, 1, 2, 4))

    return sec, gin, home(first), home(second)


def taps_first(kernel):
    moved = jnp.transpose(kernel, (1, 2, 3, 0, 4))
    return moved.reshape((27,) + moved.shape[3:])


def per_device_pair(activations, w_first, w_second, cotangent):
    planes, part, wide, ins = activations.shape
    sec, gin, x_full, h_full, e_full, f_full = chain(
        activations, taps_first(w_first), taps_first(w_second), cotangent[0]
    )
    sec, gin, grad_first, grad_second = filters(sec, gin, x_full, h_full, e_full, f_full, part * 2, wide)
    return sec[None], gin.reshape(activations.shape), grad_first, grad_second


def per_device_any(activations, w_first, w_second, cotangent):
    planes, part, wide, ins = activations.shape
    outs = w_first.shape[0]
    pair = (
        lax.axis_size("flt") == 2
        and planes == 2
        and wide == 8
        and part % 8 == 0
        and outs % 128 == 0
        and cotangent.shape[0] == 1
    )
    run = per_device_pair if pair else per_device
    return run(activations, w_first, w_second, cotangent)


def solution(mesh):
    placed = (
        P("sp", "flt", None, None),
        P("flt", None, None, None, None),
        P("flt", None, None, None, None),
        P("sp", "flt", None, None),
    )
    return jax.shard_map(
        per_device_any,
        mesh=mesh,
        in_specs=placed,
        out_specs=(
            P("sp", "flt", None, None),
            P("sp", "flt", None, None),
            P("flt", None, None, None, None),
            P("flt", None, None, None, None),
        ),
        check_vma=False,
    )
```

```python
import functools

import jax
import jax.numpy as jnp
from jax import lax
from jax.experimental import pallas as pl
from jax.experimental.pallas import tpu as pltpu
from jax.sharding import PartitionSpec as P

MESH = pl.DeviceIdType.MESH
VMEM = pl.BlockSpec(memory_space=pltpu.VMEM)
ROOM = 62 * 1024 * 1024


def remote(src, dst, send, recv, place):
    return pltpu.make_async_remote_copy(
        src_ref=src, dst_ref=dst, send_sem=send, recv_sem=recv, device_id=place, device_id_type=MESH
    )


def greet(places):
    barrier = pltpu.get_barrier_semaphore()
    for place in places:
        pl.semaphore_signal(barrier, inc=1, device_id=place, device_id_type=MESH)
    pl.semaphore_wait(barrier, len(places))


def line_kernel(count, own, out, local, recv, send_z, send_y, send_c):
    here, other = lax.axis_index("sp"), lax.axis_index("flt")
    deep = count // 4
    z, y, core = here // 4, (here // 2) % 2, here % 2

    def spot(zz, yy, cc):
        return (zz * 2 + yy) * 2 + cc

    far = [lax.rem(z + step, deep) for step in range(1, deep)]
    to_y = (spot(z, 1 - y, core), other)
    to_c = (spot(z, y, 1 - core), other)
    greet([(spot(zz, y, core), other) for zz in far] + [to_y, to_c])
    sends = []

    def push(src, slot, send, place):
        copy = remote(src, out.at[slot], send, recv.at[slot], place)
        copy.start()
        sends.append(copy)

    def arrived(slot):
        remote(own, out.at[slot], send_y.at[0], recv.at[slot], to_y).wait_recv()

    for n, zz in enumerate(far):
        push(own, here, send_z.at[n], (spot(zz, y, core), other))
    push(own, here, send_y.at[0], to_y)
    push(own, here, send_c.at[0], to_c)
    keep = pltpu.make_async_copy(own, out.at[here], local)
    keep.start()
    for n in range(1, deep):
        slot = spot(lax.rem(z + deep - n, deep), y, core)
        arrived(slot)
        push(out.at[slot], slot, send_y.at[n], to_y)
        push(out.at[slot], slot, send_c.at[n], to_c)
    for n in range(deep):
        slot = spot(lax.rem(z + deep - n, deep), 1 - y, core)
        arrived(slot)
        push(out.at[slot], slot, send_c.at[deep + n], to_c)
    for n in range(deep):
        for yy in (y, 1 - y):
            arrived(spot(lax.rem(z + deep - n, deep), yy, 1 - core))
    keep.wait()
    for copy in sends:
        copy.wait_send()


def gather_line(block, number):
    count = lax.axis_size("sp")
    deep = count // 4
    dma = pltpu.SemaphoreType.DMA
    return pl.pallas_call(
        functools.partial(line_kernel, count),
        out_shape=jax.ShapeDtypeStruct((count,) + block.shape, block.dtype),
        in_specs=[VMEM],
        out_specs=VMEM,
        scratch_shapes=[dma, dma((count,)), dma((max(deep - 1, 1),)), dma((deep,)), dma((2 * deep,))],
        compiler_params=pltpu.CompilerParams(
            collective_id=number, has_side_effects=True, vmem_limit_bytes=ROOM
        ),
    )(block)


def swap_kernel(count, split, *refs):
    kinds = len(split)
    ins, outs = refs[:kinds], refs[kinds : 2 * kinds]
    local, send, recv = refs[2 * kinds :]
    here, me = lax.axis_index("sp"), lax.axis_index("flt")
    peers = [lax.rem(me + step, count) for step in range(1, count)]
    greet([(here, peer) for peer in peers])
    sends, keeps = [], []
    for k in range(kinds):
        for n, peer in enumerate(peers):
            src = ins[k].at[peer] if split[k] else ins[k]
            copy = remote(src, outs[k].at[me], send.at[k, n], recv.at[k, me], (here, peer))
            copy.start()
            sends.append(copy)
        keep = pltpu.make_async_copy(ins[k].at[me] if split[k] else ins[k], outs[k].at[me], local.at[k])
        keep.start()
        keeps.append(keep)
    for k in range(kinds):
        for n, peer in enumerate(peers):
            src = ins[k].at[peer] if split[k] else ins[k]
            remote(src, outs[k].at[peer], send.at[k, n], recv.at[k, peer], (here, peer)).wait_recv()
    for copy in sends:
        copy.wait_send()
    for keep in keeps:
        keep.wait()


def swap(number, *pieces):
    count = lax.axis_size("flt")
    split = tuple(cut for _, cut in pieces)
    arrays = [array for array, _ in pieces]
    dma = pltpu.SemaphoreType.DMA
    shapes = [a.shape if cut else (count,) + a.shape for a, cut in pieces]
    return pl.pallas_call(
        functools.partial(swap_kernel, count, split),
        out_shape=[jax.ShapeDtypeStruct(s, a.dtype) for s, a in zip(shapes, arrays)],
        in_specs=[VMEM] * len(arrays),
        out_specs=[VMEM] * len(arrays),
        scratch_shapes=[
            dma((len(arrays),)),
            dma((len(arrays), max(count - 1, 1))),
            dma((len(arrays), count)),
        ],
        compiler_params=pltpu.CompilerParams(
            collective_id=number, has_side_effects=True, vmem_limit_bytes=ROOM
        ),
    )(*arrays)


def first_kernel(high, wide, x_ref, e_ref, out_ref, moved):
    planes, flat, outs = e_ref.shape
    lane = lax.broadcasted_iota(jnp.int32, (outs, flat), 1)
    row, col = lane // wide, lane % wide
    blank = jnp.zeros((9 * outs, flat), jnp.bfloat16)
    moved[:, 0:flat] = blank
    moved[:, (planes + 1) * flat : (planes + 2) * flat] = blank

    def fill(plane, carry):
        errors = jnp.transpose(e_ref[plane].astype(jnp.float32))
        start = pl.multiple_of((plane + 1) * flat, flat)
        for ky in range(3):
            for kz in range(3):
                by = (ky - 1) * wide + (kz - 1)
                there_y, there_z = row - (ky - 1), col - (kz - 1)
                inside = (there_y >= 0) & (there_y < high) & (there_z >= 0) & (there_z < wide)
                turned_by = pltpu.roll(errors, by % flat, 1) if by else errors
                at = (ky * 3 + kz) * outs
                moved[at : at + outs, pl.ds(start, flat)] = jnp.where(inside, turned_by, 0.0).astype(
                    jnp.bfloat16
                )
        return carry

    lax.fori_loop(0, planes, fill, 0)

    def tap(step, carry):
        kx, ky = step // 3, step % 3
        left = moved[
            pl.ds(pl.multiple_of(ky * 3 * outs, 3 * outs), 3 * outs),
            pl.ds(pl.multiple_of((2 - kx) * flat, flat), planes * flat),
        ]
        out_ref[step] = jnp.dot(left, x_ref[...], preferred_element_type=jnp.float32)
        return carry

    lax.fori_loop(0, 9, tap, 0)


def first_grad(x_cells, errors, high, wide):
    planes, flat, outs = errors.shape
    ins = x_cells.shape[1]
    found = pl.pallas_call(
        functools.partial(first_kernel, high, wide),
        out_shape=jax.ShapeDtypeStruct((9, 3 * outs, ins), jnp.float32),
        in_specs=[VMEM, VMEM],
        out_specs=VMEM,
        scratch_shapes=[pltpu.VMEM((9 * outs, (planes + 2) * flat), jnp.bfloat16)],
        compiler_params=pltpu.CompilerParams(vmem_limit_bytes=ROOM),
        cost_estimate=pl.CostEstimate(
            flops=54 * outs * ins * planes * flat, bytes_accessed=8 * planes * flat * ins, transcendentals=0
        ),
    )(x_cells, errors)
    return jnp.transpose(found.reshape(3, 3, 3, outs, ins), (3, 0, 1, 2, 4))


def second_kernel(high, wide, h_ref, e_ref, out_ref):
    rows, _, flat, ins = h_ref.shape
    cells, outs = e_ref.shape
    errors = jnp.transpose(e_ref[...].astype(jnp.float32))
    lane = lax.broadcasted_iota(jnp.int32, (outs, cells), 1)
    col, line, deep = lane % wide, (lane // wide) % high, lane // flat
    found = {}
    for a in range(2):
        for b in range(2):
            for c in range(2):
                by = a * flat + b * wide + c
                ok = (deep + a < rows) & (line + b < high) & (col + c < wide)
                rolled = pltpu.roll(errors, (cells - by) % cells, 1) if by else errors
                found[a, b, c] = jnp.where(ok, rolled, 0.0).astype(jnp.bfloat16)
    for kx in range(3):
        for ky in range(3):
            for kz in range(3):
                kind = ((kx + 1) % 2 * 2 + (ky + 1) % 2) * 2 + (kz + 1) % 2
                left = found[int(kx == 0), int(ky == 0), int(kz == 0)]
                right = h_ref[:, kind].reshape(cells, ins)
                out_ref[(kx * 3 + ky) * 3 + kz] = jnp.dot(
                    left, right, preferred_element_type=jnp.float32
                )


def second_grad(hidden, errors, high, wide):
    rows, _, flat, ins = hidden.shape
    cells, outs = errors.shape
    found = pl.pallas_call(
        functools.partial(second_kernel, high, wide),
        out_shape=jax.ShapeDtypeStruct((27, outs, ins), jnp.float32),
        in_specs=[VMEM, VMEM],
        out_specs=VMEM,
        compiler_params=pltpu.CompilerParams(vmem_limit_bytes=ROOM),
        cost_estimate=pl.CostEstimate(
            flops=54 * outs * ins * cells, bytes_accessed=32 * cells * ins, transcendentals=0
        ),
    )(hidden, errors)
    return jnp.transpose(found.reshape(3, 3, 3, outs, ins), (3, 0, 1, 2, 4))


def shifted(shard, by):
    peers = lax.axis_size("sp")
    pairs = [(i, i + by) for i in range(peers) if 0 <= i + by < peers]
    return lax.ppermute(shard, "sp", pairs)


def conv_plain(field, kernel, strides, pads, dilate):
    return lax.conv_general_dilated(
        field[None],
        kernel,
        strides,
        pads,
        lhs_dilation=dilate,
        dimension_numbers=("NDHWC", "DHWIO", "NDHWC"),
        preferred_element_type=jnp.float32,
    )[0]


def silu_slope(value):
    sig = jax.nn.sigmoid(value)
    return sig * (1.0 + value * (1.0 - sig))


def forward_taps(kernel):
    return jnp.transpose(kernel, (1, 2, 3, 4, 0))


def turned(kernel):
    return jnp.transpose(kernel[:, ::-1, ::-1, ::-1], (1, 2, 3, 0, 4))


def window(whole, below, above, start, size):
    padded = jnp.pad(whole, ((below, above),) + ((0, 0),) * (whole.ndim - 1))
    return lax.dynamic_slice_in_dim(padded, start, size, 0)


def cut_last(array, count):
    parts = array.reshape(array.shape[:-1] + (count, array.shape[-1] // count))
    return jnp.moveaxis(parts, -2, 0)


def cut_rows(array, count):
    parts = array.reshape((array.shape[0], count, array.shape[1] // count) + array.shape[2:])
    return jnp.moveaxis(parts, 1, 0)


def join_rows(parts):
    moved = jnp.moveaxis(parts, 0, 1)
    return moved.reshape((moved.shape[0], moved.shape[1] * moved.shape[2]) + moved.shape[3:])


def join_last(parts):
    moved = jnp.moveaxis(parts, 0, -2)
    return moved.reshape(moved.shape[:-2] + (moved.shape[-2] * moved.shape[-1],))


def own_term(parts_f32, parts_sent, me):
    mine = lax.broadcasted_iota(jnp.int32, (parts_sent.shape[0],) + (1,) * (parts_sent.ndim - 1), 0) == me
    rest = jnp.sum(jnp.where(mine, 0.0, parts_sent.astype(jnp.float32)), 0)
    return rest + lax.dynamic_index_in_dim(parts_f32, me, 0, keepdims=False)


def per_device(activations, w_first, w_second, cotangent):
    planes = activations.shape[0]
    rows = cotangent.shape[0]
    place, me = lax.axis_index("sp"), lax.axis_index("flt")
    count = lax.axis_size("flt")
    line = lax.axis_size("sp")
    single = (1, 1, 1)
    double = (2, 2, 2)
    x_parts, cot_parts = swap(1, (activations, False), (cut_last(cotangent, count), True))
    x_wide, cot_part = join_rows(x_parts), join_rows(cot_parts)
    high, wide = x_wide.shape[1], x_wide.shape[2]
    ins = x_wide.shape[3]
    x_full = lax.all_gather(x_wide, "sp", axis=0, tiled=True)
    x_near = jnp.concatenate([shifted(x_wide, 1), x_wide, shifted(x_wide[:1], -1)], 0)
    first_pre = conv_plain(x_near, forward_taps(w_first), single, ((0, 0), (1, 1), (1, 1)), single)
    plane = lax.broadcasted_iota(jnp.int32, (planes + 1, 1, 1, 1), 0) + place * planes
    hidden = jnp.where(plane > 0, jax.nn.silu(first_pre), 0.0).astype(jnp.bfloat16)
    (h_parts,) = swap(2, (hidden, False))
    h_wide = join_last(h_parts)
    h_own = h_wide[1:].reshape(rows, 2, high // 2, 2, wide // 2, 2, ins)
    h_own = jnp.transpose(h_own, (0, 1, 3, 5, 2, 4, 6)).reshape(rows, 8, high * wide // 4, ins)
    h_full = lax.all_gather(h_own, "sp", axis=0, tiled=True)
    second_pre = conv_plain(
        h_wide, forward_taps(w_second), double, ((0, 0), (1, 0), (1, 0)), single
    )
    second_err = (cot_part.astype(jnp.float32) * silu_slope(second_pre)).astype(jnp.bfloat16)
    outs = second_err.shape[-1]
    e_full = gather_line(second_err.reshape(-1, outs), 3).reshape((line * rows,) + second_err.shape[1:])
    e_near = window(e_full, 0, 1, place * rows, rows + 1)
    back_hidden = conv_plain(e_near, turned(w_second), single, ((1, 0), (1, 2), (1, 2)), double)
    back_parts = cut_last(back_hidden, count)
    section_parts = cut_rows(jax.nn.silu(second_pre), count)
    got, section_got = swap(4, (back_parts.astype(jnp.bfloat16), True), (section_parts, True))
    section_out = join_last(section_got)
    hidden_err = own_term(back_parts, got, me)
    first_err = (hidden_err * silu_slope(first_pre[1:])).astype(jnp.bfloat16)
    f_full = gather_line(first_err.reshape(planes, high * wide, outs), 5)
    f_full = f_full.reshape(line * planes, high * wide, outs)
    f_near = window(f_full, 1, 1, place * planes, planes + 2).reshape(planes + 2, high, wide, outs)
    back_input = conv_plain(f_near, turned(w_first), single, ((0, 0), (1, 1), (1, 1)), single)
    in_parts = cut_rows(back_input, count)
    (in_got,) = swap(6, (in_parts.astype(jnp.bfloat16), True))
    grad_input = own_term(in_parts, in_got, me)
    grad_second = second_grad(h_full, e_full.reshape(-1, outs), high // 2, wide // 2)
    grad_first = first_grad(x_full.reshape(-1, ins), f_full, high, wide)
    return (section_out, grad_input, grad_first, grad_second)


def slope_of(value):
    sig = 1.0 / (1.0 + jnp.exp(-value))
    return sig * (1.0 + value * (1.0 - sig))


def silu_of(value):
    return value / (1.0 + jnp.exp(-value))


def dot_rows(left, right):
    return lax.dot_general(left, right, (((1,), (1,)), ((), ())), preferred_element_type=jnp.float32)


def dot_plain(left, right):
    return jnp.dot(left, right, preferred_element_type=jnp.float32)


class Spread:
    def __init__(self, own, block, row, local, send, recv, deep, both, mixed=False):
        here, me = lax.axis_index("sp"), lax.axis_index("flt")
        self.own, self.block, self.row = own, block, row
        self.local, self.send, self.recv, self.deep, self.both = local, send, recv, deep, both
        self.z, self.y, self.core, self.me = here // 4, (here // 2) % 2, here % 2, me
        self.to_c = (here + 1 - 2 * self.core, me)
        self.sends = []
        self.is_mixed = mixed
        across = self.core if mixed else 0 * self.core
        self.near = (self.y + (1 - across) * (1 - 2 * self.y), me + across * (1 - 2 * me))
        self.next = (self.y + across * (1 - 2 * self.y), me + (1 - across) * (1 - 2 * me))
        self.both_off = (1 - self.y, 1 - me)

    def at(self, spot):
        y, part = spot
        return ((self.z * 2 + y) * 2 + self.core, part)

    def push(self, src, dst, slot, place):
        copy = remote(src, dst, self.send.at[len(self.sends)], self.recv.at[slot], place)
        copy.start()
        self.sends.append(copy)

    def took(self, dst, slot):
        remote(dst, dst, self.send.at[0], self.recv.at[slot], self.to_c).wait_recv()

    def push_row(self, spot, slot, place):
        view = self.row(spot[0], self.core, spot[1])
        self.push(view, view, slot, place)

    def took_row(self, spot, slot, core=None):
        self.took(self.row(spot[0], self.core if core is None else core, spot[1]), slot)

    def first(self):
        mine = self.block(self.z, self.y, self.core, self.me)
        for step in range(1, self.deep):
            zz = lax.rem(self.z + step, self.deep)
            self.push(self.own, mine, step - 1, ((zz * 2 + self.y) * 2 + self.core, self.me))
        self.keep = pltpu.make_async_copy(self.own, mine, self.local)
        self.keep.start()

    def second(self):
        for step in range(1, self.deep):
            zz = lax.rem(self.z + self.deep - step, self.deep)
            self.took(self.block(zz, self.y, self.core, self.me), step - 1)
        self.keep.wait()
        slot = self.deep - 1
        own = (self.y, self.me)
        self.push_row(own, slot, self.at(self.near))
        if self.both:
            self.push_row(own, slot + 1, self.at(self.next))
        self.push_row(own, slot + 3, self.to_c)

    def third(self):
        slot = self.deep - 1
        self.took_row(self.near, slot)
        if self.both:
            self.push_row(self.near, slot + 2, self.at(self.next))
        self.push_row(self.near, slot + 4, self.to_c)

    def fourth(self):
        slot = self.deep - 1
        if self.both:
            self.took_row(self.next, slot + 1)
            self.push_row(self.next, slot + 5, self.to_c)
            self.took_row(self.both_off, slot + 2)
            self.push_row(self.both_off, slot + 6, self.to_c)

    def last(self):
        slot = self.deep - 1
        near, far = (self.next, self.near) if self.is_mixed else (self.near, self.next)
        spots = [(self.y, self.me), near, far, self.both_off]
        for n, spot in enumerate(spots if self.both else spots[:2]):
            self.took_row(spot, slot + 3 + n, 1 - self.core)
        for copy in self.sends:
            copy.wait_send()


def spread_sends(deep):
    return (deep - 1) + 8


def spread_slots(deep):
    return (deep - 1) + 7


def chain_kernel(dims, *refs):
    count, high, wide, ins, outs = dims
    x_hbm, w1_hbm, w2_hbm, cot_hbm = refs[:4]
    sec_out, gin_out, x_full, h_full, e_full, f_full = refs[4:10]
    (
        w1, w2, x_near, cot_near, cot_wide, acc, plain, pre, slope, h_own, h_near, sec, e_own, e_next, back_f, back_b,
        back_got, f_near, f_turn, acc_in, in_b, in_got, own_sem, send_sem, recv_sem, line_local, line_send, line_recv,
    ) = refs[10:]
    flat = high * wide
    nh, nw = high // 2, wide // 2
    cells = nh * nw
    half = flat // 2
    deep = count // 4
    here, me = lax.axis_index("sp"), lax.axis_index("flt")
    mate = 1 - me
    has_up, has_down = here < count - 1, here > 0
    part, up, up_o = (here, mate), (here + 1, me), (here + 1, mate)
    down, down_o = (here - 1, me), (here - 1, mate)
    my_lanes = pl.ds(pl.multiple_of(me * outs, outs), outs)
    mate_lanes = pl.ds(pl.multiple_of(mate * outs, outs), outs)
    my_half = pl.ds(pl.multiple_of(me * half, half), half)
    mate_half = pl.ds(pl.multiple_of(mate * half, half), half)

    load_w1 = pltpu.make_async_copy(w1_hbm, w1, own_sem.at[0])
    load_w2 = pltpu.make_async_copy(w2_hbm, w2, own_sem.at[1])
    load_x = pltpu.make_async_copy(x_hbm, x_near.at[1:3, my_half, :], own_sem.at[2])
    load_cot = pltpu.make_async_copy(
        cot_hbm.at[:, :, my_lanes], cot_near.at[pl.ds(me * (nh // 2), nh // 2)], own_sem.at[3]
    )
    load_x.start()
    load_cot.start()
    load_w1.start()
    load_w2.start()

    def spread(number, own, block, row, both, mixed=False):
        return Spread(
            own, block, row, line_local.at[number], line_send.at[number], line_recv.at[number], deep, both, mixed
        )

    def half_of(part):
        return pl.ds(pl.multiple_of(part * half, half), half)

    def lanes_of(part):
        return pl.ds(pl.multiple_of(part * outs, outs), outs)

    x_line = spread(
        0,
        x_hbm,
        lambda zz, yy, cc, part: x_full.at[zz, yy, cc, :, half_of(part), :],
        lambda yy, cc, part: x_full.at[:, yy, cc, :, half_of(part), :],
        True,
        True,
    )
    h_line = spread(
        1,
        h_own,
        lambda zz, yy, cc, part: h_full.at[zz, yy, cc, :, :, lanes_of(part)],
        lambda yy, cc, part: h_full.at[:, yy, cc, :, :, lanes_of(part)],
        True,
    )
    e_line = spread(
        2, e_own, lambda zz, yy, cc, part: e_full.at[zz, yy, cc], lambda yy, cc, part: e_full.at[:, yy, cc], False
    )
    f_line = spread(
        3, f_turn, lambda zz, yy, cc, part: f_full.at[zz, yy, cc], lambda yy, cc, part: f_full.at[:, yy, cc], False
    )

    barrier = pltpu.get_barrier_semaphore()

    def hello(place):
        pl.semaphore_signal(barrier, inc=1, device_id=place, device_id_type=MESH)

    zz, yy, cc = here // 4, (here // 2) % 2, here % 2
    always = [part, x_line.to_c, ((zz * 2 + 1 - yy) * 2 + cc, me)]
    for step in range(1, deep):
        always.append(((lax.rem(zz + step, deep) * 2 + yy) * 2 + cc, me))
    for place in always:
        hello(place)

    @pl.when(has_up)
    def _():
        hello(up)
        hello(up_o)

    @pl.when(has_down)
    def _():
        hello(down)
        hello(down_o)

    pl.semaphore_wait(
        barrier, len(always) + 2 * has_up.astype(jnp.int32) + 2 * has_down.astype(jnp.int32)
    )

    started = []

    def send(src, dst, slot, place, cond=None):
        copy = remote(src, dst, send_sem.at[len(started)], recv_sem.at[slot], place)
        if cond is None:
            copy.start()
        else:
            pl.when(cond)(copy.start)
        started.append((copy, cond))

    def wait(src, dst, slot, cond=None):
        copy = remote(src, dst, send_sem.at[0], recv_sem.at[slot], part)
        if cond is None:
            copy.wait_recv()
        else:
            pl.when(cond)(copy.wait_recv)

    send(x_hbm, x_near.at[1:3, my_half, :], 0, part)
    send(x_hbm.at[1], x_near.at[0, my_half, :], 1, up, has_up)
    send(x_hbm.at[1], x_near.at[0, my_half, :], 2, up_o, has_up)
    send(x_hbm.at[0], x_near.at[3, my_half, :], 3, down, has_down)
    send(x_hbm.at[0], x_near.at[3, my_half, :], 4, down_o, has_down)
    cot_rows = pl.ds(me * (nh // 2), nh // 2)
    cot_rows_mate = pl.ds(mate * (nh // 2), nh // 2)
    send(cot_hbm.at[:, :, mate_lanes], cot_near.at[cot_rows], 5, part)
    x_line.first()

    @pl.when(jnp.logical_not(has_down))
    def _():
        x_near[0] = jnp.zeros((flat, ins), jnp.bfloat16)
        h_near[0:4] = jnp.zeros((4, cells, ins), jnp.bfloat16)
        f_near[0] = jnp.zeros((flat, outs), jnp.bfloat16)

    @pl.when(jnp.logical_not(has_up))
    def _():
        x_near[3] = jnp.zeros((flat, ins), jnp.bfloat16)
        e_next[...] = jnp.zeros((cells, outs), jnp.bfloat16)
        f_near[3] = jnp.zeros((flat, outs), jnp.bfloat16)

    load_x.wait()
    wait(x_hbm, x_near.at[1:3, mate_half, :], 0)
    wait(x_hbm.at[1], x_near.at[0, my_half, :], 1, has_down)
    wait(x_hbm.at[1], x_near.at[0, mate_half, :], 2, has_down)
    wait(x_hbm.at[0], x_near.at[3, my_half, :], 3, has_up)
    wait(x_hbm.at[0], x_near.at[3, mate_half, :], 4, has_up)
    load_w1.wait()

    for ky in (1, 0, 2):
        total = None
        for kx in range(3):
            left = x_near[kx : kx + 2].reshape(2 * flat, ins)
            at = kx * 9 + ky * 3
            right = w1[at : at + 3].reshape(3 * outs, ins)
            term = dot_rows(left, right)
            total = term if total is None else total + term
        total = total.reshape(2, flat, 3 * outs)
        if ky == 1:
            acc[...] = total
        elif ky == 0:
            acc[:, wide:, :] += total[:, : flat - wide, :]
        else:
            acc[:, : flat - wide, :] += total[:, wide:, :]
    col = lax.broadcasted_iota(jnp.int32, (2 * flat, outs), 0) % wide
    whole = acc[...].reshape(2 * flat, 3 * outs)
    value = whole[:, outs : 2 * outs]
    value = value + jnp.where(col > 0, pltpu.roll(whole[:, :outs], 1, 0), 0.0)
    value = value + jnp.where(col < wide - 1, pltpu.roll(whole[:, 2 * outs :], 2 * flat - 1, 0), 0.0)
    plain[...] = value

    def pick(px, py, pz, qz):
        return pl.ds(px * flat + py * wide + 2 * qz + pz, nh, 2 * wide)

    for px in (1, 0):
        for py in range(2):
            for pz in range(2):
                kind = (px * 2 + py) * 2 + pz
                found = jnp.concatenate([plain[pick(px, py, pz, qz), :] for qz in range(nw)], 0)
                pre[kind] = found
                h_own[kind] = silu_of(found).astype(jnp.bfloat16)
    send(h_own.at[4:8], h_near.at[0:4, :, my_lanes], 6, up, has_up)
    send(h_own.at[4:8], h_near.at[0:4, :, my_lanes], 7, up_o, has_up)
    send(h_own, h_near.at[4:12, :, my_lanes], 8, part)
    h_line.first()
    keep_h = pltpu.make_async_copy(h_own, h_near.at[4:12, :, my_lanes], own_sem.at[4])
    keep_h.start()
    load_w2.wait()
    load_cot.wait()
    wait(cot_hbm.at[:, :, my_lanes], cot_near.at[cot_rows_mate], 5)
    cot_wide[...] = cot_near[...].astype(jnp.float32)
    slope[...] = slope_of(pre[...])
    keep_h.wait()
    wait(h_own, h_near.at[4:12, :, mate_lanes], 8)
    wait(h_own.at[4:8], h_near.at[0:4, :, my_lanes], 6, has_down)
    wait(h_own.at[4:8], h_near.at[0:4, :, mate_lanes], 7, has_down)
    x_line.second()

    row = lax.broadcasted_iota(jnp.int32, (cells, outs), 0)
    qy, qz_of = row % nh, row // nh

    def later_y(v):
        return jnp.where(qy > 0, pltpu.roll(v, 1, 0), 0.0)

    def later_z(v):
        return jnp.where(qz_of > 0, pltpu.roll(v, nh, 0), 0.0)

    def earlier_y(v):
        return jnp.where(qy < nh - 1, pltpu.roll(v, cells - 1, 0), 0.0)

    def earlier_z(v):
        return jnp.where(qz_of < nw - 1, pltpu.roll(v, cells - nh, 0), 0.0)

    sums = {}
    for ky in range(3):
        for kz in range(3):
            for kx in range(3):
                kind = kx * 4 + (ky != 1) * 2 + (kz != 1)
                term = dot_rows(h_near[kind], w2[kx * 9 + ky * 3 + kz])
                key = (ky == 0, kz == 0)
                sums[key] = sums[key] + term if key in sums else term
    second = (
        sums[False, False]
        + later_y(sums[True, False] + later_z(sums[True, True]))
        + later_z(sums[False, True])
    )
    cot = jnp.concatenate([cot_wide[:, qz, :] for qz in range(nw)], 0)
    err = (cot * slope_of(second)).astype(jnp.bfloat16)
    e_own[...] = err
    send(e_own, e_next, 9, down, has_down)
    e_line.first()
    shown = silu_of(second)
    for qz in range(nw):
        sec[:, qz, :] = shown[qz * nh : (qz + 1) * nh]
    send(sec.at[cot_rows_mate], sec_out.at[:, :, my_lanes], 10, part)
    keep_sec = pltpu.make_async_copy(sec.at[cot_rows], sec_out.at[:, :, my_lanes], own_sem.at[5])
    keep_sec.start()

    wait(e_own, e_next, 9, has_up)

    def variants(block):
        block = block.astype(jnp.float32)
        moved_y = earlier_y(block)
        found = {
            (0, 0): block,
            (1, 0): moved_y,
            (0, 1): earlier_z(block),
            (1, 1): earlier_z(moved_y),
        }
        return {key: v.astype(jnp.bfloat16) for key, v in found.items()}

    e_here, e_after = variants(err), variants(e_next[...])
    for px in range(2):
        for py in range(2):
            for pz in range(2):
                kind = (px * 2 + py) * 2 + pz
                total = None
                for kx in (2, 0) if px else (1,):
                    for ky in (2, 0) if py else (1,):
                        for kz in (2, 0) if pz else (1,):
                            source = e_after if kx == 0 else e_here
                            left = source[int(ky == 0), int(kz == 0)]
                            term = dot_plain(left, w2[kx * 9 + ky * 3 + kz])
                            total = term if total is None else total + term
                for side in range(2):
                    piece = total[:, side * outs : (side + 1) * outs]
                    back_f[side, kind] = piece
                    back_b[side, kind] = piece.astype(jnp.bfloat16)
    send(back_b.at[mate], back_got, 11, part)
    h_line.second()
    e_line.second()
    wait(back_b.at[me], back_got, 11)
    for px in range(2):
        for py in range(2):
            for pz in range(2):
                kind = (px * 2 + py) * 2 + pz
                total = back_f[me, kind] + back_got[kind].astype(jnp.float32)
                found = (total * slope[kind]).astype(jnp.bfloat16).astype(jnp.float32)
                for qz in range(nw):
                    plain[pick(px, py, pz, qz), :] = found[qz * nh : (qz + 1) * nh]
    first = plain[...]
    f_near[1:3] = first.astype(jnp.bfloat16).reshape(2, flat, outs)
    send(f_near.at[1], f_near.at[3], 12, down, has_down)
    send(f_near.at[2], f_near.at[0], 13, up, has_up)
    f_turn[...] = jnp.transpose(first).astype(jnp.bfloat16)
    f_line.first()
    x_line.third()
    wait(f_near.at[1], f_near.at[3], 12, has_up)
    wait(f_near.at[2], f_near.at[0], 13, has_down)

    for kz in range(3):
        for ky in (1, 0, 2):
            total = None
            for kx in range(3):
                left = f_near[2 - kx : 4 - kx].reshape(2 * flat, outs)
                term = dot_plain(left, w1[kx * 9 + ky * 3 + kz])
                total = term if total is None else total + term
            total = total.reshape(2, flat, ins)
            if ky == 1:
                acc_in[kz] = total
            elif ky == 0:
                acc_in[kz, :, : flat - wide, :] += total[:, wide:, :]
            else:
                acc_in[kz, :, wide:, :] += total[:, : flat - wide, :]
    col = lax.broadcasted_iota(jnp.int32, (2 * flat, ins), 0) % wide
    value = acc_in[1].reshape(2 * flat, ins)
    value = value + jnp.where(
        col < wide - 1, pltpu.roll(acc_in[0].reshape(2 * flat, ins), 2 * flat - 1, 0), 0.0
    )
    value = value + jnp.where(col > 0, pltpu.roll(acc_in[2].reshape(2 * flat, ins), 1, 0), 0.0)
    value = value.reshape(2, flat, ins)
    acc_in[1] = value
    in_b[...] = value.astype(jnp.bfloat16)
    send(in_b.at[:, mate_half, :], in_got, 14, part)
    e_line.third()
    h_line.third()
    f_line.second()
    x_line.fourth()
    f_line.third()
    h_line.fourth()
    wait(in_b.at[:, my_half, :], in_got, 14)
    gin_out[...] = acc_in[1, :, my_half, :] + in_got[...].astype(jnp.float32)
    wait(sec.at[cot_rows], sec_out.at[:, :, mate_lanes], 10)
    keep_sec.wait()
    x_line.last()
    e_line.last()
    h_line.last()
    f_line.last()
    for copy, cond in started:
        if cond is None:
            copy.wait_send()
        else:
            pl.when(cond)(copy.wait_send)


def chain(x, w1, w2, cot):
    count = lax.axis_size("sp")
    planes, high, wide, ins = x.shape
    high = high * 2
    outs = w1.shape[1]
    flat = high * wide
    nh, nw = high // 2, wide // 2
    cells = nh * nw
    deep = count // 4
    dma = pltpu.SemaphoreType.DMA
    bf, f32 = jnp.bfloat16, jnp.float32
    anywhere = pl.BlockSpec(memory_space=pl.ANY)
    shape = jax.ShapeDtypeStruct
    return pl.pallas_call(
        functools.partial(chain_kernel, (count, high, wide, ins, outs)),
        out_shape=[
            shape(cot.shape, f32),
            shape((planes, flat // 2, ins), f32),
            shape((deep, 2, 2, planes, flat, ins), bf),
            shape((deep, 2, 2, 8, cells, ins), bf),
            shape((deep, 2, 2, cells, outs), bf),
            shape((deep, 2, 2, outs, planes * flat), bf),
        ],
        in_specs=[anywhere] * 4,
        out_specs=[anywhere, VMEM] + [anywhere] * 4,
        scratch_shapes=[
            pltpu.VMEM(w1.shape, bf),
            pltpu.VMEM(w2.shape, bf),
            pltpu.VMEM((4, flat, ins), bf),
            pltpu.VMEM((nh, nw, outs), bf),
            pltpu.VMEM((nh, nw, outs), f32),
            pltpu.VMEM((2, flat, 3 * outs), f32),
            pltpu.VMEM((2 * flat, outs), f32),
            pltpu.VMEM((8, cells, outs), f32),
            pltpu.VMEM((8, cells, outs), f32),
            pltpu.VMEM((8, cells, outs), bf),
            pltpu.VMEM((12, cells, ins), bf),
            pltpu.VMEM((nh, nw, outs), f32),
            pltpu.VMEM((cells, outs), bf),
            pltpu.VMEM((cells, outs), bf),
            pltpu.VMEM((2, 8, cells, outs), f32),
            pltpu.VMEM((2, 8, cells, outs), bf),
            pltpu.VMEM((8, cells, outs), bf),
            pltpu.VMEM((4, flat, outs), bf),
            pltpu.VMEM((outs, 2 * flat), bf),
            pltpu.VMEM((3, 2, flat, ins), f32),
            pltpu.VMEM((2, flat, ins), bf),
            pltpu.VMEM((2, flat // 2, ins), bf),
            dma((6,)),
            dma((15,)),
            dma((15,)),
            dma((4,)),
            dma((4, spread_sends(deep))),
            dma((4, spread_slots(deep))),
        ],
        compiler_params=pltpu.CompilerParams(
            collective_id=1, has_side_effects=True, vmem_limit_bytes=ROOM
        ),
    )(x.reshape(planes, flat // 2, ins), w1, w2, cot)


def filter_kernel(dims, *refs):
    high, wide, outs, ins = dims
    sec_in, gin_in, x_hbm, h_hbm, e_hbm, f_hbm = refs[:6]
    sec_out, gin_out, first_out, second_out = refs[6:10]
    x_v, h_v, e_v, f_v, moved, found1, found2, in_sem, out_sem = refs[10:]
    count = f_v.shape[0]
    flat = high * wide
    nh, nw = high // 2, wide // 2
    cells = nh * nw
    loads = [
        pltpu.make_async_copy(src, dst, in_sem.at[n])
        for n, (src, dst) in enumerate(((e_hbm, e_v), (h_hbm, h_v), (f_hbm, f_v), (x_hbm, x_v)))
    ]
    for load in loads:
        load.start()
    outs_going = [
        pltpu.make_async_copy(sec_in, sec_out, out_sem.at[0]),
        pltpu.make_async_copy(gin_in, gin_out, out_sem.at[1]),
    ]
    for copy in outs_going:
        copy.start()

    loads[0].wait()
    total = count * cells
    errors = jnp.transpose(e_v[...].reshape(total, outs).astype(jnp.float32))
    lane = lax.broadcasted_iota(jnp.int32, (outs, total), 1)
    line, col, place = lane % nh, (lane // nh) % nw, lane // cells
    turned_by = {}
    for a in range(2):
        for b in range(2):
            for c in range(2):
                by = a * cells + c * nh + b
                ok = (place + a < count) & (line + b < nh) & (col + c < nw)
                rolled = pltpu.roll(errors, total - by, 1) if by else errors
                turned_by[a, b, c] = jnp.where(ok, rolled, 0.0).astype(jnp.bfloat16)
    loads[1].wait()
    for kx in range(3):
        for ky in range(3):
            for kz in range(3):
                kind = ((kx + 1) % 2 * 2 + (ky + 1) % 2) * 2 + (kz + 1) % 2
                left = turned_by[int(kx == 0), int(ky == 0), int(kz == 0)]
                right = h_v[:, kind].reshape(total, ins)
                found2[(kx * 3 + ky) * 3 + kz] = dot_plain(left, right)
    copy = pltpu.make_async_copy(found2, second_out, out_sem.at[2])
    copy.start()
    outs_going.append(copy)

    loads[2].wait()
    lane = lax.broadcasted_iota(jnp.int32, (outs, flat), 1)
    row, col = lane // wide, lane % wide
    blank = jnp.zeros((9 * outs, flat), jnp.bfloat16)
    moved[:, 0:flat] = blank
    moved[:, (2 * count + 1) * flat : (2 * count + 2) * flat] = blank

    def fill(block, carry):
        for p in range(2):
            errors = f_v[block, :, p * flat : (p + 1) * flat].astype(jnp.float32)
            start = pl.multiple_of((2 * block + p + 1) * flat, flat)
            for ky in range(3):
                for kz in range(3):
                    by = (ky - 1) * wide + (kz - 1)
                    there_y, there_z = row - (ky - 1), col - (kz - 1)
                    inside = (there_y >= 0) & (there_y < high) & (there_z >= 0) & (there_z < wide)
                    rolled = pltpu.roll(errors, by % flat, 1) if by else errors
                    at = (ky * 3 + kz) * outs
                    moved[at : at + outs, pl.ds(start, flat)] = jnp.where(inside, rolled, 0.0).astype(
                        jnp.bfloat16
                    )
        return carry

    lax.fori_loop(0, count, fill, 0)
    loads[3].wait()

    def tap(step, carry):
        kx, ky = step // 3, step % 3
        left = moved[
            pl.ds(pl.multiple_of(ky * 3 * outs, 3 * outs), 3 * outs),
            pl.ds(pl.multiple_of((2 - kx) * flat, flat), 2 * count * flat),
        ]
        found1[step] = dot_plain(left, x_v[...].reshape(2 * count * flat, ins)).reshape(3, outs, ins)
        pltpu.make_async_copy(found1.at[step], first_out.at[step], out_sem.at[3 + step]).start()
        return carry

    lax.fori_loop(0, 9, tap, 0)
    for step in range(9):
        pltpu.make_async_copy(found1.at[step], first_out.at[step], out_sem.at[3 + step]).wait()
    for copy in outs_going:
        copy.wait()


def filters(sec, gin, x_full, h_full, e_full, f_full, high, wide):
    count, _, cells, ins = h_full.shape
    outs = e_full.shape[-1]
    flat = high * wide
    dma = pltpu.SemaphoreType.DMA
    bf, f32 = jnp.bfloat16, jnp.float32
    anywhere = pl.BlockSpec(memory_space=pl.ANY)
    shape = jax.ShapeDtypeStruct
    sec, gin, first, second = pl.pallas_call(
        functools.partial(filter_kernel, (high, wide, outs, ins)),
        out_shape=[
            shape(sec.shape, f32),
            shape(gin.shape, f32),
            shape((9, 3, outs, ins), f32),
            shape((27, outs, ins), f32),
        ],
        in_specs=[anywhere] * 6,
        out_specs=[anywhere] * 4,
        scratch_shapes=[
            pltpu.VMEM(x_full.shape, bf),
            pltpu.VMEM(h_full.shape, bf),
            pltpu.VMEM(e_full.shape, bf),
            pltpu.VMEM(f_full.shape, bf),
            pltpu.VMEM((9 * outs, (2 * count + 2) * flat), bf),
            pltpu.VMEM((9, 3, outs, ins), f32),
            pltpu.VMEM((27, outs, ins), f32),
            dma((4,)),
            dma((12,)),
        ],
        compiler_params=pltpu.CompilerParams(vmem_limit_bytes=ROOM),
    )(sec, gin, x_full, h_full, e_full, f_full)

    def home(found):
        return jnp.transpose(found.reshape(3, 3, 3, outs, ins), (3, 0, 1, 2, 4))

    return sec, gin, home(first), home(second)


def taps_first(kernel):
    moved = jnp.transpose(kernel, (1, 2, 3, 0, 4))
    return moved.reshape((27,) + moved.shape[3:])


def per_device_pair(activations, w_first, w_second, cotangent):
    planes, part, wide, ins = activations.shape
    sec, gin, *gathered = chain(activations, taps_first(w_first), taps_first(w_second), cotangent[0])
    x_full, h_full, e_full, f_full = (a.reshape((-1,) + a.shape[3:]) for a in gathered)
    sec, gin, grad_first, grad_second = filters(sec, gin, x_full, h_full, e_full, f_full, part * 2, wide)
    return sec[None], gin.reshape(activations.shape), grad_first, grad_second


def per_device_any(activations, w_first, w_second, cotangent):
    planes, part, wide, ins = activations.shape
    outs = w_first.shape[0]
    pair = (
        lax.axis_size("flt") == 2
        and planes == 2
        and wide == 8
        and part % 8 == 0
        and outs % 128 == 0
        and cotangent.shape[0] == 1
    )
    run = per_device_pair if pair else per_device
    return run(activations, w_first, w_second, cotangent)


def solution(mesh):
    placed = (
        P("sp", "flt", None, None),
        P("flt", None, None, None, None),
        P("flt", None, None, None, None),
        P("sp", "flt", None, None),
    )
    return jax.shard_map(
        per_device_any,
        mesh=mesh,
        in_specs=placed,
        out_specs=(
            P("sp", "flt", None, None),
            P("sp", "flt", None, None),
            P("flt", None, None, None, None),
            P("flt", None, None, None, None),
        ),
        check_vma=False,
    )
```

```python
import functools

import jax
import jax.numpy as jnp
from jax import lax
from jax.experimental import pallas as pl
from jax.experimental.pallas import tpu as pltpu
from jax.sharding import PartitionSpec as P

MESH = pl.DeviceIdType.MESH
VMEM = pl.BlockSpec(memory_space=pltpu.VMEM)
ROOM = 62 * 1024 * 1024
GRANT = 2 * 1024 * 1024


def remote(src, dst, send, recv, place):
    return pltpu.make_async_remote_copy(
        src_ref=src, dst_ref=dst, send_sem=send, recv_sem=recv, device_id=place, device_id_type=MESH
    )


def greet(places):
    barrier = pltpu.get_barrier_semaphore()
    for place in places:
        pl.semaphore_signal(barrier, inc=1, device_id=place, device_id_type=MESH)
    pl.semaphore_wait(barrier, len(places))


def line_kernel(count, own, out, local, recv, send_z, send_y, send_c):
    here, other = lax.axis_index("sp"), lax.axis_index("flt")
    deep = count // 4
    z, y, core = here // 4, (here // 2) % 2, here % 2

    def spot(zz, yy, cc):
        return (zz * 2 + yy) * 2 + cc

    far = [lax.rem(z + step, deep) for step in range(1, deep)]
    to_y = (spot(z, 1 - y, core), other)
    to_c = (spot(z, y, 1 - core), other)
    greet([(spot(zz, y, core), other) for zz in far] + [to_y, to_c])
    sends = []

    def push(src, slot, send, place):
        copy = remote(src, out.at[slot], send, recv.at[slot], place)
        copy.start()
        sends.append(copy)

    def arrived(slot):
        remote(own, out.at[slot], send_y.at[0], recv.at[slot], to_y).wait_recv()

    for n, zz in enumerate(far):
        push(own, here, send_z.at[n], (spot(zz, y, core), other))
    push(own, here, send_y.at[0], to_y)
    push(own, here, send_c.at[0], to_c)
    keep = pltpu.make_async_copy(own, out.at[here], local)
    keep.start()
    for n in range(1, deep):
        slot = spot(lax.rem(z + deep - n, deep), y, core)
        arrived(slot)
        push(out.at[slot], slot, send_y.at[n], to_y)
        push(out.at[slot], slot, send_c.at[n], to_c)
    for n in range(deep):
        slot = spot(lax.rem(z + deep - n, deep), 1 - y, core)
        arrived(slot)
        push(out.at[slot], slot, send_c.at[deep + n], to_c)
    for n in range(deep):
        for yy in (y, 1 - y):
            arrived(spot(lax.rem(z + deep - n, deep), yy, 1 - core))
    keep.wait()
    for copy in sends:
        copy.wait_send()


def gather_line(block, number):
    count = lax.axis_size("sp")
    deep = count // 4
    dma = pltpu.SemaphoreType.DMA
    return pl.pallas_call(
        functools.partial(line_kernel, count),
        out_shape=jax.ShapeDtypeStruct((count,) + block.shape, block.dtype),
        in_specs=[VMEM],
        out_specs=VMEM,
        scratch_shapes=[dma, dma((count,)), dma((max(deep - 1, 1),)), dma((deep,)), dma((2 * deep,))],
        compiler_params=pltpu.CompilerParams(
            collective_id=number, has_side_effects=True, vmem_limit_bytes=ROOM
        ),
    )(block)


def swap_kernel(count, split, *refs):
    kinds = len(split)
    ins, outs = refs[:kinds], refs[kinds : 2 * kinds]
    local, send, recv = refs[2 * kinds :]
    here, me = lax.axis_index("sp"), lax.axis_index("flt")
    peers = [lax.rem(me + step, count) for step in range(1, count)]
    greet([(here, peer) for peer in peers])
    sends, keeps = [], []
    for k in range(kinds):
        for n, peer in enumerate(peers):
            src = ins[k].at[peer] if split[k] else ins[k]
            copy = remote(src, outs[k].at[me], send.at[k, n], recv.at[k, me], (here, peer))
            copy.start()
            sends.append(copy)
        keep = pltpu.make_async_copy(ins[k].at[me] if split[k] else ins[k], outs[k].at[me], local.at[k])
        keep.start()
        keeps.append(keep)
    for k in range(kinds):
        for n, peer in enumerate(peers):
            src = ins[k].at[peer] if split[k] else ins[k]
            remote(src, outs[k].at[peer], send.at[k, n], recv.at[k, peer], (here, peer)).wait_recv()
    for copy in sends:
        copy.wait_send()
    for keep in keeps:
        keep.wait()


def swap(number, *pieces):
    count = lax.axis_size("flt")
    split = tuple(cut for _, cut in pieces)
    arrays = [array for array, _ in pieces]
    dma = pltpu.SemaphoreType.DMA
    shapes = [a.shape if cut else (count,) + a.shape for a, cut in pieces]
    return pl.pallas_call(
        functools.partial(swap_kernel, count, split),
        out_shape=[jax.ShapeDtypeStruct(s, a.dtype) for s, a in zip(shapes, arrays)],
        in_specs=[VMEM] * len(arrays),
        out_specs=[VMEM] * len(arrays),
        scratch_shapes=[
            dma((len(arrays),)),
            dma((len(arrays), max(count - 1, 1))),
            dma((len(arrays), count)),
        ],
        compiler_params=pltpu.CompilerParams(
            collective_id=number, has_side_effects=True, vmem_limit_bytes=ROOM
        ),
    )(*arrays)


def first_kernel(high, wide, x_ref, e_ref, out_ref, moved):
    planes, flat, outs = e_ref.shape
    lane = lax.broadcasted_iota(jnp.int32, (outs, flat), 1)
    row, col = lane // wide, lane % wide
    blank = jnp.zeros((9 * outs, flat), jnp.bfloat16)
    moved[:, 0:flat] = blank
    moved[:, (planes + 1) * flat : (planes + 2) * flat] = blank

    def fill(plane, carry):
        errors = jnp.transpose(e_ref[plane].astype(jnp.float32))
        start = pl.multiple_of((plane + 1) * flat, flat)
        for ky in range(3):
            for kz in range(3):
                by = (ky - 1) * wide + (kz - 1)
                there_y, there_z = row - (ky - 1), col - (kz - 1)
                inside = (there_y >= 0) & (there_y < high) & (there_z >= 0) & (there_z < wide)
                turned_by = pltpu.roll(errors, by % flat, 1) if by else errors
                at = (ky * 3 + kz) * outs
                moved[at : at + outs, pl.ds(start, flat)] = jnp.where(inside, turned_by, 0.0).astype(
                    jnp.bfloat16
                )
        return carry

    lax.fori_loop(0, planes, fill, 0)

    def tap(step, carry):
        kx, ky = step // 3, step % 3
        left = moved[
            pl.ds(pl.multiple_of(ky * 3 * outs, 3 * outs), 3 * outs),
            pl.ds(pl.multiple_of((2 - kx) * flat, flat), planes * flat),
        ]
        out_ref[step] = jnp.dot(left, x_ref[...], preferred_element_type=jnp.float32)
        return carry

    lax.fori_loop(0, 9, tap, 0)


def first_grad(x_cells, errors, high, wide):
    planes, flat, outs = errors.shape
    ins = x_cells.shape[1]
    found = pl.pallas_call(
        functools.partial(first_kernel, high, wide),
        out_shape=jax.ShapeDtypeStruct((9, 3 * outs, ins), jnp.float32),
        in_specs=[VMEM, VMEM],
        out_specs=VMEM,
        scratch_shapes=[pltpu.VMEM((9 * outs, (planes + 2) * flat), jnp.bfloat16)],
        compiler_params=pltpu.CompilerParams(vmem_limit_bytes=ROOM),
        cost_estimate=pl.CostEstimate(
            flops=54 * outs * ins * planes * flat, bytes_accessed=8 * planes * flat * ins, transcendentals=0
        ),
    )(x_cells, errors)
    return jnp.transpose(found.reshape(3, 3, 3, outs, ins), (3, 0, 1, 2, 4))


def second_kernel(high, wide, h_ref, e_ref, out_ref):
    rows, _, flat, ins = h_ref.shape
    cells, outs = e_ref.shape
    errors = jnp.transpose(e_ref[...].astype(jnp.float32))
    lane = lax.broadcasted_iota(jnp.int32, (outs, cells), 1)
    col, line, deep = lane % wide, (lane // wide) % high, lane // flat
    found = {}
    for a in range(2):
        for b in range(2):
            for c in range(2):
                by = a * flat + b * wide + c
                ok = (deep + a < rows) & (line + b < high) & (col + c < wide)
                rolled = pltpu.roll(errors, (cells - by) % cells, 1) if by else errors
                found[a, b, c] = jnp.where(ok, rolled, 0.0).astype(jnp.bfloat16)
    for kx in range(3):
        for ky in range(3):
            for kz in range(3):
                kind = ((kx + 1) % 2 * 2 + (ky + 1) % 2) * 2 + (kz + 1) % 2
                left = found[int(kx == 0), int(ky == 0), int(kz == 0)]
                right = h_ref[:, kind].reshape(cells, ins)
                out_ref[(kx * 3 + ky) * 3 + kz] = jnp.dot(
                    left, right, preferred_element_type=jnp.float32
                )


def second_grad(hidden, errors, high, wide):
    rows, _, flat, ins = hidden.shape
    cells, outs = errors.shape
    found = pl.pallas_call(
        functools.partial(second_kernel, high, wide),
        out_shape=jax.ShapeDtypeStruct((27, outs, ins), jnp.float32),
        in_specs=[VMEM, VMEM],
        out_specs=VMEM,
        compiler_params=pltpu.CompilerParams(vmem_limit_bytes=ROOM),
        cost_estimate=pl.CostEstimate(
            flops=54 * outs * ins * cells, bytes_accessed=32 * cells * ins, transcendentals=0
        ),
    )(hidden, errors)
    return jnp.transpose(found.reshape(3, 3, 3, outs, ins), (3, 0, 1, 2, 4))


def shifted(shard, by):
    peers = lax.axis_size("sp")
    pairs = [(i, i + by) for i in range(peers) if 0 <= i + by < peers]
    return lax.ppermute(shard, "sp", pairs)


def conv_plain(field, kernel, strides, pads, dilate):
    return lax.conv_general_dilated(
        field[None],
        kernel,
        strides,
        pads,
        lhs_dilation=dilate,
        dimension_numbers=("NDHWC", "DHWIO", "NDHWC"),
        preferred_element_type=jnp.float32,
    )[0]


def silu_slope(value):
    sig = jax.nn.sigmoid(value)
    return sig * (1.0 + value * (1.0 - sig))


def forward_taps(kernel):
    return jnp.transpose(kernel, (1, 2, 3, 4, 0))


def turned(kernel):
    return jnp.transpose(kernel[:, ::-1, ::-1, ::-1], (1, 2, 3, 0, 4))


def window(whole, below, above, start, size):
    padded = jnp.pad(whole, ((below, above),) + ((0, 0),) * (whole.ndim - 1))
    return lax.dynamic_slice_in_dim(padded, start, size, 0)


def cut_last(array, count):
    parts = array.reshape(array.shape[:-1] + (count, array.shape[-1] // count))
    return jnp.moveaxis(parts, -2, 0)


def cut_rows(array, count):
    parts = array.reshape((array.shape[0], count, array.shape[1] // count) + array.shape[2:])
    return jnp.moveaxis(parts, 1, 0)


def join_rows(parts):
    moved = jnp.moveaxis(parts, 0, 1)
    return moved.reshape((moved.shape[0], moved.shape[1] * moved.shape[2]) + moved.shape[3:])


def join_last(parts):
    moved = jnp.moveaxis(parts, 0, -2)
    return moved.reshape(moved.shape[:-2] + (moved.shape[-2] * moved.shape[-1],))


def own_term(parts_f32, parts_sent, me):
    mine = lax.broadcasted_iota(jnp.int32, (parts_sent.shape[0],) + (1,) * (parts_sent.ndim - 1), 0) == me
    rest = jnp.sum(jnp.where(mine, 0.0, parts_sent.astype(jnp.float32)), 0)
    return rest + lax.dynamic_index_in_dim(parts_f32, me, 0, keepdims=False)


def per_device(activations, w_first, w_second, cotangent):
    planes = activations.shape[0]
    rows = cotangent.shape[0]
    place, me = lax.axis_index("sp"), lax.axis_index("flt")
    count = lax.axis_size("flt")
    line = lax.axis_size("sp")
    single = (1, 1, 1)
    double = (2, 2, 2)
    x_parts, cot_parts = swap(1, (activations, False), (cut_last(cotangent, count), True))
    x_wide, cot_part = join_rows(x_parts), join_rows(cot_parts)
    high, wide = x_wide.shape[1], x_wide.shape[2]
    ins = x_wide.shape[3]
    x_full = lax.all_gather(x_wide, "sp", axis=0, tiled=True)
    x_near = jnp.concatenate([shifted(x_wide, 1), x_wide, shifted(x_wide[:1], -1)], 0)
    first_pre = conv_plain(x_near, forward_taps(w_first), single, ((0, 0), (1, 1), (1, 1)), single)
    plane = lax.broadcasted_iota(jnp.int32, (planes + 1, 1, 1, 1), 0) + place * planes
    hidden = jnp.where(plane > 0, jax.nn.silu(first_pre), 0.0).astype(jnp.bfloat16)
    (h_parts,) = swap(2, (hidden, False))
    h_wide = join_last(h_parts)
    h_own = h_wide[1:].reshape(rows, 2, high // 2, 2, wide // 2, 2, ins)
    h_own = jnp.transpose(h_own, (0, 1, 3, 5, 2, 4, 6)).reshape(rows, 8, high * wide // 4, ins)
    h_full = lax.all_gather(h_own, "sp", axis=0, tiled=True)
    second_pre = conv_plain(
        h_wide, forward_taps(w_second), double, ((0, 0), (1, 0), (1, 0)), single
    )
    second_err = (cot_part.astype(jnp.float32) * silu_slope(second_pre)).astype(jnp.bfloat16)
    outs = second_err.shape[-1]
    e_full = gather_line(second_err.reshape(-1, outs), 3).reshape((line * rows,) + second_err.shape[1:])
    e_near = window(e_full, 0, 1, place * rows, rows + 1)
    back_hidden = conv_plain(e_near, turned(w_second), single, ((1, 0), (1, 2), (1, 2)), double)
    back_parts = cut_last(back_hidden, count)
    section_parts = cut_rows(jax.nn.silu(second_pre), count)
    got, section_got = swap(4, (back_parts.astype(jnp.bfloat16), True), (section_parts, True))
    section_out = join_last(section_got)
    hidden_err = own_term(back_parts, got, me)
    first_err = (hidden_err * silu_slope(first_pre[1:])).astype(jnp.bfloat16)
    f_full = gather_line(first_err.reshape(planes, high * wide, outs), 5)
    f_full = f_full.reshape(line * planes, high * wide, outs)
    f_near = window(f_full, 1, 1, place * planes, planes + 2).reshape(planes + 2, high, wide, outs)
    back_input = conv_plain(f_near, turned(w_first), single, ((0, 0), (1, 1), (1, 1)), single)
    in_parts = cut_rows(back_input, count)
    (in_got,) = swap(6, (in_parts.astype(jnp.bfloat16), True))
    grad_input = own_term(in_parts, in_got, me)
    grad_second = second_grad(h_full, e_full.reshape(-1, outs), high // 2, wide // 2)
    grad_first = first_grad(x_full.reshape(-1, ins), f_full, high, wide)
    return (section_out, grad_input, grad_first, grad_second)


def slope_of(value):
    sig = 1.0 / (1.0 + jnp.exp(-value))
    return sig * (1.0 + value * (1.0 - sig))


def silu_of(value):
    return value / (1.0 + jnp.exp(-value))


def dot_rows(left, right):
    return lax.dot_general(left, right, (((1,), (1,)), ((), ())), preferred_element_type=jnp.float32)


def dot_plain(left, right):
    return jnp.dot(left, right, preferred_element_type=jnp.float32)


class Spread:
    def __init__(self, own, block, local, send, recv, deep, both, mixed=False, cores=True):
        here, me = lax.axis_index("sp"), lax.axis_index("flt")
        self.own, self.block = own, block
        self.local, self.send, self.recv, self.deep, self.both = local, send, recv, deep, both
        self.z, self.y, self.core, self.me = here // 4, (here // 2) % 2, here % 2, me
        self.to_c = (here + 1 - 2 * self.core, me)
        self.sends = []
        self.is_mixed, self.cores = mixed, cores
        across = self.core if mixed else 0 * self.core
        self.near = (self.y + (1 - across) * (1 - 2 * self.y), me + across * (1 - 2 * me))
        self.next = (self.y + across * (1 - 2 * self.y), me + (1 - across) * (1 - 2 * me))
        self.both_off = (1 - self.y, 1 - me)

    def at(self, spot):
        y, part = spot
        return ((self.z * 2 + y) * 2 + self.core, part)

    def push(self, src, dst, slot, place):
        copy = remote(src, dst, self.send.at[len(self.sends)], self.recv.at[slot], place)
        copy.start()
        self.sends.append(copy)

    def took(self, dst, slot):
        remote(dst, dst, self.send.at[0], self.recv.at[slot], self.to_c).wait_recv()

    def view(self, n, spot, core=None):
        zz = lax.rem(self.z + self.deep - n, self.deep) if n else self.z
        return self.block(zz, spot[0], self.core if core is None else core, spot[1])

    def slot(self, kind, n):
        return kind * self.deep + n

    def hand(self, n, spot, kind, place, src=None):
        view = self.view(n, spot)
        self.push(view if src is None else src, view, self.slot(kind, n), place)

    def first(self):
        mine = self.block(self.z, self.y, self.core, self.me)
        for step in range(1, self.deep):
            zz = lax.rem(self.z + step, self.deep)
            self.push(self.own, mine, self.slot(0, step), ((zz * 2 + self.y) * 2 + self.core, self.me))
        self.share(0, self.own)
        self.keep = pltpu.make_async_copy(self.own, mine, self.local)
        self.keep.start()

    def share(self, n, src=None):
        own = (self.y, self.me)
        self.hand(n, own, 1, self.at(self.near), src)
        if self.both:
            self.hand(n, own, 2, self.at(self.next), src)
        if self.cores:
            self.hand(n, own, 4, self.to_c, src)

    def line(self, *steps):
        for n in steps:
            self.took(self.view(n, (self.y, self.me)), self.slot(0, n))
            self.share(n)

    def side(self, *steps):
        for n in steps:
            self.took(self.view(n, self.near), self.slot(1, n))
            if self.both:
                self.hand(n, self.near, 3, self.at(self.next))
            if self.cores:
                self.hand(n, self.near, 5, self.to_c)

    def rest(self, *steps):
        for n in steps:
            self.took(self.view(n, self.next), self.slot(2, n))
            self.hand(n, self.next, 6, self.to_c)
            self.took(self.view(n, self.both_off), self.slot(3, n))
            self.hand(n, self.both_off, 7, self.to_c)

    def ended(self, *steps):
        near, far = (self.next, self.near) if self.is_mixed else (self.near, self.next)
        spots = [(self.y, self.me), near, far, self.both_off]
        for n in steps:
            if n == 0:
                self.keep.wait()
            if not self.cores:
                continue
            for kind, spot in enumerate(spots if self.both else spots[:2]):
                self.took(self.view(n, spot, 1 - self.core), self.slot(4 + kind, n))

    def sent(self):
        for copy in self.sends:
            copy.wait_send()


def spread_sends(deep):
    return (deep - 1) + 7 * deep


def spread_slots(deep):
    return 8 * deep


def chain_kernel(dims, *refs):
    count, high, wide, ins, outs = dims
    x_hbm, w1_hbm, w2_hbm, cot_hbm = refs[:4]
    sec_out, gin_out, found1, found2 = refs[4:8]
    (
        w1, w2, x_near, cot_near, cot_wide, acc, plain, pre, slope, h_own, h_near, sec, e_own, e_next, back_f, back_b,
        back_got, f_near, f_turn, acc_in, in_b, in_got, x_full, h_full, e_full, f_full, f_pair, moved,
        own_sem, send_sem, recv_sem, line_local, line_send, line_recv,
    ) = refs[8:]
    flat = high * wide
    nh, nw = high // 2, wide // 2
    cells = nh * nw
    half = flat // 2
    deep = count // 4
    here, me = lax.axis_index("sp"), lax.axis_index("flt")
    mate = 1 - me
    core = here % 2
    share = outs // 2
    has_up, has_down = here < count - 1, here > 0
    part, up, up_o = (here, mate), (here + 1, me), (here + 1, mate)
    down, down_o = (here - 1, me), (here - 1, mate)
    my_lanes = pl.ds(pl.multiple_of(me * outs, outs), outs)
    mate_lanes = pl.ds(pl.multiple_of(mate * outs, outs), outs)
    my_half = pl.ds(pl.multiple_of(me * half, half), half)
    mate_half = pl.ds(pl.multiple_of(mate * half, half), half)

    load_w1 = pltpu.make_async_copy(w1_hbm, w1, own_sem.at[0])
    load_w2 = pltpu.make_async_copy(w2_hbm, w2, own_sem.at[1])
    load_x = pltpu.make_async_copy(x_hbm, x_near.at[1:3, my_half, :], own_sem.at[2])
    load_cot = pltpu.make_async_copy(
        cot_hbm.at[:, :, my_lanes], cot_near.at[pl.ds(me * (nh // 2), nh // 2)], own_sem.at[3]
    )
    load_x.start()
    load_cot.start()
    load_w1.start()
    load_w2.start()

    def spread(number, own, block, both, mixed=False, cores=True):
        return Spread(
            own, block, line_local.at[number], line_send.at[number], line_recv.at[number], deep, both, mixed, cores
        )

    def half_of(part):
        return pl.ds(pl.multiple_of(part * half, half), half)

    def lanes_of(part):
        return pl.ds(pl.multiple_of(part * outs, outs), outs)

    x_line = spread(
        0,
        x_hbm,
        lambda zz, yy, cc, part: x_full.at[pl.ds(((zz * 2 + yy) * 2 + cc) * 2 + 1, 2), half_of(part), :],
        True,
    )
    h_line = spread(
        1,
        h_own,
        lambda zz, yy, cc, part: h_full.at[zz, yy, cc, :, :, lanes_of(part)],
        True,
        True,
    )
    e_line = spread(
        2, e_own, lambda zz, yy, cc, part: e_full.at[zz, yy, cc], False
    )
    f_line = spread(3, f_pair, lambda zz, yy, cc, part: f_full.at[zz, yy], False, False, False)

    barrier = pltpu.get_barrier_semaphore()

    def hello(place):
        pl.semaphore_signal(barrier, inc=1, device_id=place, device_id_type=MESH)

    zz, yy, cc = here // 4, (here // 2) % 2, here % 2
    always = [part, x_line.to_c, ((zz * 2 + 1 - yy) * 2 + cc, me)]
    for step in range(1, deep):
        always.append(((lax.rem(zz + step, deep) * 2 + yy) * 2 + cc, me))
    for place in always:
        hello(place)

    @pl.when(has_up)
    def _():
        hello(up)
        hello(up_o)

    @pl.when(has_down)
    def _():
        hello(down)
        hello(down_o)

    pl.semaphore_wait(
        barrier, len(always) + 2 * has_up.astype(jnp.int32) + 2 * has_down.astype(jnp.int32)
    )

    started = []

    def send(src, dst, slot, place, cond=None):
        copy = remote(src, dst, send_sem.at[len(started)], recv_sem.at[slot], place)
        if cond is None:
            copy.start()
        else:
            pl.when(cond)(copy.start)
        started.append((copy, cond))

    def wait(src, dst, slot, cond=None):
        copy = remote(src, dst, send_sem.at[0], recv_sem.at[slot], part)
        if cond is None:
            copy.wait_recv()
        else:
            pl.when(cond)(copy.wait_recv)

    send(x_hbm, x_near.at[1:3, my_half, :], 0, part)
    send(x_hbm.at[1], x_near.at[0, my_half, :], 1, up, has_up)
    send(x_hbm.at[1], x_near.at[0, my_half, :], 2, up_o, has_up)
    send(x_hbm.at[0], x_near.at[3, my_half, :], 3, down, has_down)
    send(x_hbm.at[0], x_near.at[3, my_half, :], 4, down_o, has_down)
    cot_rows = pl.ds(me * (nh // 2), nh // 2)
    cot_rows_mate = pl.ds(mate * (nh // 2), nh // 2)
    send(cot_hbm.at[:, :, mate_lanes], cot_near.at[cot_rows], 5, part)
    x_line.first()

    x_full[0] = jnp.zeros((flat, ins), jnp.bfloat16)
    x_full[2 * count + 1] = jnp.zeros((flat, ins), jnp.bfloat16)

    @pl.when(jnp.logical_not(has_down))
    def _():
        x_near[0] = jnp.zeros((flat, ins), jnp.bfloat16)
        h_near[0:4] = jnp.zeros((4, cells, ins), jnp.bfloat16)
        f_near[0] = jnp.zeros((flat, outs), jnp.bfloat16)

    @pl.when(jnp.logical_not(has_up))
    def _():
        x_near[3] = jnp.zeros((flat, ins), jnp.bfloat16)
        e_next[...] = jnp.zeros((cells, outs), jnp.bfloat16)
        f_near[3] = jnp.zeros((flat, outs), jnp.bfloat16)

    load_x.wait()
    wait(x_hbm, x_near.at[1:3, mate_half, :], 0)
    wait(x_hbm.at[1], x_near.at[0, my_half, :], 1, has_down)
    wait(x_hbm.at[1], x_near.at[0, mate_half, :], 2, has_down)
    wait(x_hbm.at[0], x_near.at[3, my_half, :], 3, has_up)
    wait(x_hbm.at[0], x_near.at[3, mate_half, :], 4, has_up)
    load_w1.wait()

    for ky in (1, 0, 2):
        total = None
        for kx in range(3):
            left = x_near[kx : kx + 2].reshape(2 * flat, ins)
            at = kx * 9 + ky * 3
            right = w1[at : at + 3].reshape(3 * outs, ins)
            term = dot_rows(left, right)
            total = term if total is None else total + term
        total = total.reshape(2, flat, 3 * outs)
        if ky == 1:
            acc[...] = total
        elif ky == 0:
            acc[:, wide:, :] += total[:, : flat - wide, :]
        else:
            acc[:, : flat - wide, :] += total[:, wide:, :]
    col = lax.broadcasted_iota(jnp.int32, (2 * flat, outs), 0) % wide
    whole = acc[...].reshape(2 * flat, 3 * outs)
    value = whole[:, outs : 2 * outs]
    value = value + jnp.where(col > 0, pltpu.roll(whole[:, :outs], 1, 0), 0.0)
    value = value + jnp.where(col < wide - 1, pltpu.roll(whole[:, 2 * outs :], 2 * flat - 1, 0), 0.0)
    plain[...] = value

    def pick(px, py, pz, qz):
        return pl.ds(px * flat + py * wide + 2 * qz + pz, nh, 2 * wide)

    for px in (1, 0):
        for py in range(2):
            for pz in range(2):
                kind = (px * 2 + py) * 2 + pz
                found = jnp.concatenate([plain[pick(px, py, pz, qz), :] for qz in range(nw)], 0)
                pre[kind] = found
                h_own[kind] = silu_of(found).astype(jnp.bfloat16)
    send(h_own.at[4:8], h_near.at[0:4, :, my_lanes], 6, up, has_up)
    send(h_own.at[4:8], h_near.at[0:4, :, my_lanes], 7, up_o, has_up)
    send(h_own, h_near.at[4:12, :, my_lanes], 8, part)
    h_line.first()
    keep_h = pltpu.make_async_copy(h_own, h_near.at[4:12, :, my_lanes], own_sem.at[4])
    keep_h.start()
    load_w2.wait()
    load_cot.wait()
    wait(cot_hbm.at[:, :, my_lanes], cot_near.at[cot_rows_mate], 5)
    cot_wide[...] = cot_near[...].astype(jnp.float32)
    slope[...] = slope_of(pre[...])
    keep_h.wait()
    wait(h_own, h_near.at[4:12, :, mate_lanes], 8)
    wait(h_own.at[4:8], h_near.at[0:4, :, my_lanes], 6, has_down)
    wait(h_own.at[4:8], h_near.at[0:4, :, mate_lanes], 7, has_down)
    x_line.line(1)

    row = lax.broadcasted_iota(jnp.int32, (cells, outs), 0)
    qy, qz_of = row % nh, row // nh

    def later_y(v):
        return jnp.where(qy > 0, pltpu.roll(v, 1, 0), 0.0)

    def later_z(v):
        return jnp.where(qz_of > 0, pltpu.roll(v, nh, 0), 0.0)

    def earlier_y(v):
        return jnp.where(qy < nh - 1, pltpu.roll(v, cells - 1, 0), 0.0)

    def earlier_z(v):
        return jnp.where(qz_of < nw - 1, pltpu.roll(v, cells - nh, 0), 0.0)

    sums = {}
    for ky in range(3):
        for kz in range(3):
            for kx in range(3):
                kind = kx * 4 + (ky != 1) * 2 + (kz != 1)
                term = dot_rows(h_near[kind], w2[kx * 9 + ky * 3 + kz])
                key = (ky == 0, kz == 0)
                sums[key] = sums[key] + term if key in sums else term
    second = (
        sums[False, False]
        + later_y(sums[True, False] + later_z(sums[True, True]))
        + later_z(sums[False, True])
    )
    cot = jnp.concatenate([cot_wide[:, qz, :] for qz in range(nw)], 0)
    err = (cot * slope_of(second)).astype(jnp.bfloat16)
    e_own[...] = err
    send(e_own, e_next, 9, down, has_down)
    e_line.first()
    x_line.line(2, 3)
    x_line.side(0)
    shown = silu_of(second)
    for qz in range(nw):
        sec[:, qz, :] = shown[qz * nh : (qz + 1) * nh]
    send(sec.at[cot_rows_mate], sec_out.at[:, :, my_lanes], 10, part)
    keep_sec = pltpu.make_async_copy(sec.at[cot_rows], sec_out.at[:, :, my_lanes], own_sem.at[5])
    keep_sec.start()

    wait(e_own, e_next, 9, has_up)

    def variants(block):
        block = block.astype(jnp.float32)
        moved_y = earlier_y(block)
        found = {
            (0, 0): block,
            (1, 0): moved_y,
            (0, 1): earlier_z(block),
            (1, 1): earlier_z(moved_y),
        }
        return {key: v.astype(jnp.bfloat16) for key, v in found.items()}

    e_here, e_after = variants(err), variants(e_next[...])
    for px in range(2):
        for py in range(2):
            for pz in range(2):
                kind = (px * 2 + py) * 2 + pz
                total = None
                for kx in (2, 0) if px else (1,):
                    for ky in (2, 0) if py else (1,):
                        for kz in (2, 0) if pz else (1,):
                            source = e_after if kx == 0 else e_here
                            left = source[int(ky == 0), int(kz == 0)]
                            term = dot_plain(left, w2[kx * 9 + ky * 3 + kz])
                            total = term if total is None else total + term
                for side in range(2):
                    piece = total[:, side * outs : (side + 1) * outs]
                    back_f[side, kind] = piece
                    back_b[side, kind] = piece.astype(jnp.bfloat16)
    send(back_b.at[mate], back_got, 11, part)
    x_line.side(1, 2, 3)
    h_line.line(1, 2, 3)
    h_line.side(0)
    e_line.line(1, 2, 3)
    wait(back_b.at[me], back_got, 11)
    for px in range(2):
        for py in range(2):
            for pz in range(2):
                kind = (px * 2 + py) * 2 + pz
                total = back_f[me, kind] + back_got[kind].astype(jnp.float32)
                found = (total * slope[kind]).astype(jnp.bfloat16).astype(jnp.float32)
                for qz in range(nw):
                    plain[pick(px, py, pz, qz), :] = found[qz * nh : (qz + 1) * nh]
    first = plain[...]
    f_near[1:3] = first.astype(jnp.bfloat16).reshape(2, flat, outs)
    send(f_near.at[1], f_near.at[3], 12, down, has_down)
    send(f_near.at[2], f_near.at[0], 13, up, has_up)
    f_turn[...] = jnp.transpose(first).astype(jnp.bfloat16).reshape(2, share, 2 * flat)
    send(f_turn.at[1 - core], f_pair.at[core], 15, x_line.to_c)
    f_pair[core] = f_turn[core]
    wait(f_turn.at[core], f_pair.at[1 - core], 15)
    f_line.first()
    wait(f_near.at[1], f_near.at[3], 12, has_up)
    wait(f_near.at[2], f_near.at[0], 13, has_down)

    for kz in range(3):
        for ky in (1, 0, 2):
            total = None
            for kx in range(3):
                left = f_near[2 - kx : 4 - kx].reshape(2 * flat, outs)
                term = dot_plain(left, w1[kx * 9 + ky * 3 + kz])
                total = term if total is None else total + term
            total = total.reshape(2, flat, ins)
            if ky == 1:
                acc_in[kz] = total
            elif ky == 0:
                acc_in[kz, :, : flat - wide, :] += total[:, wide:, :]
            else:
                acc_in[kz, :, wide:, :] += total[:, : flat - wide, :]
    col = lax.broadcasted_iota(jnp.int32, (2 * flat, ins), 0) % wide
    value = acc_in[1].reshape(2 * flat, ins)
    value = value + jnp.where(
        col < wide - 1, pltpu.roll(acc_in[0].reshape(2 * flat, ins), 2 * flat - 1, 0), 0.0
    )
    value = value + jnp.where(col > 0, pltpu.roll(acc_in[2].reshape(2 * flat, ins), 1, 0), 0.0)
    value = value.reshape(2, flat, ins)
    acc_in[1] = value
    in_b[...] = value.astype(jnp.bfloat16)
    send(in_b.at[:, mate_half, :], in_got, 14, part)
    f_line.line(1, 2, 3)
    x_line.rest(0, 1, 2, 3)
    e_line.side(0, 1, 2, 3)
    h_line.side(1, 2, 3)
    lane = lax.broadcasted_iota(jnp.int32, (share, flat), 1)
    row, col = lane // wide, lane % wide

    def fill(zz):
        def one(block, carry):
            for p in range(2):
                errors = f_full[zz, block // 2, block % 2, :, p * flat : (p + 1) * flat].astype(jnp.float32)
                start = pl.multiple_of((2 * block + p) * flat, flat)
                for ky in range(3):
                    for kz in range(3):
                        by = (ky - 1) * wide + (kz - 1)
                        there_y, there_z = row - (ky - 1), col - (kz - 1)
                        inside = (there_y >= 0) & (there_y < high) & (there_z >= 0) & (there_z < wide)
                        rolled = pltpu.roll(errors, by % flat, 1) if by else errors
                        at = (ky * 3 + kz) * share
                        moved[at : at + share, pl.ds(start, flat)] = jnp.where(inside, rolled, 0.0).astype(
                            jnp.bfloat16
                        )
            return carry

        lax.fori_loop(0, 4, one, 0)

    def gather_taps(zz, fresh):
        def tap(kx, carry):
            right = x_full[pl.ds(zz * 8 + kx, 8)].reshape(8 * flat, ins)
            term = dot_plain(moved[...], right).reshape(9, share, ins)
            found1[kx, :, core] = term if fresh else found1[kx, :, core] + term
            return carry

        lax.fori_loop(0, 3, tap, 0)

    def group(n):
        return lax.rem(here // 4 + deep - n, deep) if n else here // 4

    f_line.side(0)
    f_line.ended(0)
    fill(group(0))
    x_line.ended(0, 1, 2, 3)
    gather_taps(group(0), True)
    wait(in_b.at[:, my_half, :], in_got, 14)
    gin_out[...] = acc_in[1, :, my_half, :] + in_got[...].astype(jnp.float32)
    wait(sec.at[cot_rows], sec_out.at[:, :, mate_lanes], 10)
    keep_sec.wait()
    f_line.side(1)
    fill(group(1))
    gather_taps(group(1), False)
    h_line.rest(0, 1, 2, 3)
    f_line.side(2)
    fill(group(2))
    gather_taps(group(2), False)
    f_line.side(3)
    fill(group(3))
    for kx in range(3):
        right = x_full[pl.ds(group(deep - 1) * 8 + kx, 8)].reshape(8 * flat, ins)
        term = dot_plain(moved[...], right)
        found1[kx, :, core] = found1[kx, :, core] + term.reshape(9, share, ins)
        send(found1.at[kx, :, core], found1.at[kx, :, core], 16 + kx, x_line.to_c)
    e_line.ended(0, 1, 2, 3)
    h_line.ended(0, 1, 2, 3)
    total = count * cells
    errors = jnp.transpose(e_full[...].reshape(total, outs).astype(jnp.float32))
    lane = lax.broadcasted_iota(jnp.int32, (outs, total), 1)
    spot_y, spot_z, spot_x = lane % nh, (lane // nh) % nw, lane // cells
    turned_by = {}
    for a in range(2):
        for b in range(2):
            for c in range(2):
                by = a * cells + c * nh + b
                ok = (spot_x + a < count) & (spot_y + b < nh) & (spot_z + c < nw)
                rolled = pltpu.roll(errors, total - by, 1) if by else errors
                turned_by[a, b, c] = jnp.where(ok, rolled, 0.0).astype(jnp.bfloat16)
    for kind in range(8):
        px, py, pz = kind // 4, (kind // 2) % 2, kind % 2
        taps = [
            (kx, ky, kz)
            for kx in ((0, 2) if px else (1,))
            for ky in ((0, 2) if py else (1,))
            for kz in ((0, 2) if pz else (1,))
        ]
        left = jnp.concatenate([turned_by[int(kx == 0), int(ky == 0), int(kz == 0)] for kx, ky, kz in taps], 0)
        term = dot_plain(left, h_full[:, :, :, kind].reshape(total, ins))
        for n, (kx, ky, kz) in enumerate(taps):
            found2[(kx * 3 + ky) * 3 + kz] = term[n * outs : (n + 1) * outs]
    for kx in range(3):
        wait(found1.at[kx, :, core], found1.at[kx, :, 1 - core], 16 + kx)
    x_line.sent()
    e_line.sent()
    h_line.sent()
    f_line.sent()
    for copy, cond in started:
        if cond is None:
            copy.wait_send()
        else:
            pl.when(cond)(copy.wait_send)


def chain(x, w1, w2, cot):
    count = lax.axis_size("sp")
    planes, high, wide, ins = x.shape
    high = high * 2
    outs = w1.shape[1]
    flat = high * wide
    nh, nw = high // 2, wide // 2
    cells = nh * nw
    deep = count // 4
    dma = pltpu.SemaphoreType.DMA
    bf, f32 = jnp.bfloat16, jnp.float32
    anywhere = pl.BlockSpec(memory_space=pl.ANY)
    shape = jax.ShapeDtypeStruct
    return pl.pallas_call(
        functools.partial(chain_kernel, (count, high, wide, ins, outs)),
        out_shape=[
            shape(cot.shape, f32),
            shape((planes, flat // 2, ins), f32),
            pltpu.VMEM((3, 9, 2, outs // 2, ins), f32),
            pltpu.VMEM((27, outs, ins), f32),
        ],
        in_specs=[anywhere] * 4,
        out_specs=[anywhere, VMEM, VMEM, VMEM],
        scratch_shapes=[
            pltpu.VMEM(w1.shape, bf),
            pltpu.VMEM(w2.shape, bf),
            pltpu.VMEM((4, flat, ins), bf),
            pltpu.VMEM((nh, nw, outs), bf),
            pltpu.VMEM((nh, nw, outs), f32),
            pltpu.VMEM((2, flat, 3 * outs), f32),
            pltpu.VMEM((2 * flat, outs), f32),
            pltpu.VMEM((8, cells, outs), f32),
            pltpu.VMEM((8, cells, outs), f32),
            pltpu.VMEM((8, cells, outs), bf),
            pltpu.VMEM((12, cells, ins), bf),
            pltpu.VMEM((nh, nw, outs), f32),
            pltpu.VMEM((cells, outs), bf),
            pltpu.VMEM((cells, outs), bf),
            pltpu.VMEM((2, 8, cells, outs), f32),
            pltpu.VMEM((2, 8, cells, outs), bf),
            pltpu.VMEM((8, cells, outs), bf),
            pltpu.VMEM((4, flat, outs), bf),
            pltpu.VMEM((2, outs // 2, 2 * flat), bf),
            pltpu.VMEM((3, 2, flat, ins), f32),
            pltpu.VMEM((2, flat, ins), bf),
            pltpu.VMEM((2, flat // 2, ins), bf),
            pltpu.VMEM((planes * count + 2, flat, ins), bf),
            pltpu.VMEM((deep, 2, 2, 8, cells, ins), bf),
            pltpu.VMEM((deep, 2, 2, cells, outs), bf),
            pltpu.VMEM((deep, 2, 2, outs // 2, planes * flat), bf),
            pltpu.VMEM((2, outs // 2, planes * flat), bf),
            pltpu.VMEM((9 * outs // 2, 8 * flat), bf),
            dma((6,)),
            dma((19,)),
            dma((19,)),
            dma((4,)),
            dma((4, spread_sends(deep))),
            dma((4, spread_slots(deep))),
        ],
        compiler_params=pltpu.CompilerParams(
            collective_id=1, has_side_effects=True, vmem_limit_bytes=40 * 1024 * 1024
        ),
    )(*(pltpu.with_memory_space_constraint(a, pltpu.HBM) for a in (x.reshape(planes, flat // 2, ins), w1, w2, cot)))


def write_kernel(*refs):
    sources, places, sem = refs[:4], refs[4:8], refs[8]
    copies = [pltpu.make_async_copy(src, dst, sem.at[n]) for n, (src, dst) in enumerate(zip(sources, places))]
    for copy in copies:
        copy.start()
    for copy in copies:
        copy.wait()


def write(*arrays):
    anywhere = pl.BlockSpec(memory_space=pl.ANY)
    return pl.pallas_call(
        write_kernel,
        out_shape=[jax.ShapeDtypeStruct(a.shape, a.dtype) for a in arrays],
        in_specs=[anywhere] * 4,
        out_specs=[anywhere] * 4,
        scratch_shapes=[pltpu.SemaphoreType.DMA((4,))],
        compiler_params=pltpu.CompilerParams(vmem_limit_bytes=GRANT),
    )(*arrays)


def taps_first(kernel):
    moved = jnp.transpose(kernel, (1, 2, 3, 0, 4))
    return moved.reshape((27,) + moved.shape[3:])


def per_device_pair(activations, w_first, w_second, cotangent):
    planes, part, wide, ins = activations.shape
    outs = w_first.shape[0]

    def home(found):
        return jnp.transpose(found.reshape(3, 3, 3, outs, ins), (3, 0, 1, 2, 4))

    found = chain(activations, taps_first(w_first), taps_first(w_second), cotangent[0])
    sec, gin, grad_first, grad_second = write(*found)
    grad_first, grad_second = home(grad_first), home(grad_second)
    return sec[None], gin.reshape(activations.shape), grad_first, grad_second


def per_device_any(activations, w_first, w_second, cotangent):
    planes, part, wide, ins = activations.shape
    outs = w_first.shape[0]
    pair = (
        lax.axis_size("flt") == 2
        and planes == 2
        and wide == 8
        and part % 8 == 0
        and outs % 128 == 0
        and cotangent.shape[0] == 1
    )
    run = per_device_pair if pair else per_device
    return run(activations, w_first, w_second, cotangent)


def solution(mesh):
    placed = (
        P("sp", "flt", None, None),
        P("flt", None, None, None, None),
        P("flt", None, None, None, None),
        P("sp", "flt", None, None),
    )
    return jax.shard_map(
        per_device_any,
        mesh=mesh,
        in_specs=placed,
        out_specs=(
            P("sp", "flt", None, None),
            P("sp", "flt", None, None),
            P("flt", None, None, None, None),
            P("flt", None, None, None, None),
        ),
        check_vma=False,
    )
```

```python
import functools

import jax
import jax.numpy as jnp
from jax import lax
from jax.experimental import pallas as pl
from jax.experimental.pallas import tpu as pltpu
from jax.sharding import PartitionSpec as P

MESH = pl.DeviceIdType.MESH
VMEM = pl.BlockSpec(memory_space=pltpu.VMEM)
ROOM = 62 * 1024 * 1024
GRANT = 2 * 1024 * 1024


def remote(src, dst, send, recv, place):
    return pltpu.make_async_remote_copy(
        src_ref=src, dst_ref=dst, send_sem=send, recv_sem=recv, device_id=place, device_id_type=MESH
    )


def greet(places):
    barrier = pltpu.get_barrier_semaphore()
    for place in places:
        pl.semaphore_signal(barrier, inc=1, device_id=place, device_id_type=MESH)
    pl.semaphore_wait(barrier, len(places))


def line_kernel(count, own, out, local, recv, send_z, send_y, send_c):
    here, other = lax.axis_index("sp"), lax.axis_index("flt")
    deep = count // 4
    z, y, core = here // 4, (here // 2) % 2, here % 2

    def spot(zz, yy, cc):
        return (zz * 2 + yy) * 2 + cc

    far = [lax.rem(z + step, deep) for step in range(1, deep)]
    to_y = (spot(z, 1 - y, core), other)
    to_c = (spot(z, y, 1 - core), other)
    greet([(spot(zz, y, core), other) for zz in far] + [to_y, to_c])
    sends = []

    def push(src, slot, send, place):
        copy = remote(src, out.at[slot], send, recv.at[slot], place)
        copy.start()
        sends.append(copy)

    def arrived(slot):
        remote(own, out.at[slot], send_y.at[0], recv.at[slot], to_y).wait_recv()

    for n, zz in enumerate(far):
        push(own, here, send_z.at[n], (spot(zz, y, core), other))
    push(own, here, send_y.at[0], to_y)
    push(own, here, send_c.at[0], to_c)
    keep = pltpu.make_async_copy(own, out.at[here], local)
    keep.start()
    for n in range(1, deep):
        slot = spot(lax.rem(z + deep - n, deep), y, core)
        arrived(slot)
        push(out.at[slot], slot, send_y.at[n], to_y)
        push(out.at[slot], slot, send_c.at[n], to_c)
    for n in range(deep):
        slot = spot(lax.rem(z + deep - n, deep), 1 - y, core)
        arrived(slot)
        push(out.at[slot], slot, send_c.at[deep + n], to_c)
    for n in range(deep):
        for yy in (y, 1 - y):
            arrived(spot(lax.rem(z + deep - n, deep), yy, 1 - core))
    keep.wait()
    for copy in sends:
        copy.wait_send()


def gather_line(block, number):
    count = lax.axis_size("sp")
    deep = count // 4
    dma = pltpu.SemaphoreType.DMA
    return pl.pallas_call(
        functools.partial(line_kernel, count),
        out_shape=jax.ShapeDtypeStruct((count,) + block.shape, block.dtype),
        in_specs=[VMEM],
        out_specs=VMEM,
        scratch_shapes=[dma, dma((count,)), dma((max(deep - 1, 1),)), dma((deep,)), dma((2 * deep,))],
        compiler_params=pltpu.CompilerParams(
            collective_id=number, has_side_effects=True, vmem_limit_bytes=ROOM
        ),
    )(block)


def swap_kernel(count, split, *refs):
    kinds = len(split)
    ins, outs = refs[:kinds], refs[kinds : 2 * kinds]
    local, send, recv = refs[2 * kinds :]
    here, me = lax.axis_index("sp"), lax.axis_index("flt")
    peers = [lax.rem(me + step, count) for step in range(1, count)]
    greet([(here, peer) for peer in peers])
    sends, keeps = [], []
    for k in range(kinds):
        for n, peer in enumerate(peers):
            src = ins[k].at[peer] if split[k] else ins[k]
            copy = remote(src, outs[k].at[me], send.at[k, n], recv.at[k, me], (here, peer))
            copy.start()
            sends.append(copy)
        keep = pltpu.make_async_copy(ins[k].at[me] if split[k] else ins[k], outs[k].at[me], local.at[k])
        keep.start()
        keeps.append(keep)
    for k in range(kinds):
        for n, peer in enumerate(peers):
            src = ins[k].at[peer] if split[k] else ins[k]
            remote(src, outs[k].at[peer], send.at[k, n], recv.at[k, peer], (here, peer)).wait_recv()
    for copy in sends:
        copy.wait_send()
    for keep in keeps:
        keep.wait()


def swap(number, *pieces):
    count = lax.axis_size("flt")
    split = tuple(cut for _, cut in pieces)
    arrays = [array for array, _ in pieces]
    dma = pltpu.SemaphoreType.DMA
    shapes = [a.shape if cut else (count,) + a.shape for a, cut in pieces]
    return pl.pallas_call(
        functools.partial(swap_kernel, count, split),
        out_shape=[jax.ShapeDtypeStruct(s, a.dtype) for s, a in zip(shapes, arrays)],
        in_specs=[VMEM] * len(arrays),
        out_specs=[VMEM] * len(arrays),
        scratch_shapes=[
            dma((len(arrays),)),
            dma((len(arrays), max(count - 1, 1))),
            dma((len(arrays), count)),
        ],
        compiler_params=pltpu.CompilerParams(
            collective_id=number, has_side_effects=True, vmem_limit_bytes=ROOM
        ),
    )(*arrays)


def first_kernel(high, wide, x_ref, e_ref, out_ref, moved):
    planes, flat, outs = e_ref.shape
    lane = lax.broadcasted_iota(jnp.int32, (outs, flat), 1)
    row, col = lane // wide, lane % wide
    blank = jnp.zeros((9 * outs, flat), jnp.bfloat16)
    moved[:, 0:flat] = blank
    moved[:, (planes + 1) * flat : (planes + 2) * flat] = blank

    def fill(plane, carry):
        errors = jnp.transpose(e_ref[plane].astype(jnp.float32))
        start = pl.multiple_of((plane + 1) * flat, flat)
        for ky in range(3):
            for kz in range(3):
                by = (ky - 1) * wide + (kz - 1)
                there_y, there_z = row - (ky - 1), col - (kz - 1)
                inside = (there_y >= 0) & (there_y < high) & (there_z >= 0) & (there_z < wide)
                turned_by = pltpu.roll(errors, by % flat, 1) if by else errors
                at = (ky * 3 + kz) * outs
                moved[at : at + outs, pl.ds(start, flat)] = jnp.where(inside, turned_by, 0.0).astype(
                    jnp.bfloat16
                )
        return carry

    lax.fori_loop(0, planes, fill, 0)

    def tap(step, carry):
        kx, ky = step // 3, step % 3
        left = moved[
            pl.ds(pl.multiple_of(ky * 3 * outs, 3 * outs), 3 * outs),
            pl.ds(pl.multiple_of((2 - kx) * flat, flat), planes * flat),
        ]
        out_ref[step] = jnp.dot(left, x_ref[...], preferred_element_type=jnp.float32)
        return carry

    lax.fori_loop(0, 9, tap, 0)


def first_grad(x_cells, errors, high, wide):
    planes, flat, outs = errors.shape
    ins = x_cells.shape[1]
    found = pl.pallas_call(
        functools.partial(first_kernel, high, wide),
        out_shape=jax.ShapeDtypeStruct((9, 3 * outs, ins), jnp.float32),
        in_specs=[VMEM, VMEM],
        out_specs=VMEM,
        scratch_shapes=[pltpu.VMEM((9 * outs, (planes + 2) * flat), jnp.bfloat16)],
        compiler_params=pltpu.CompilerParams(vmem_limit_bytes=ROOM),
        cost_estimate=pl.CostEstimate(
            flops=54 * outs * ins * planes * flat, bytes_accessed=8 * planes * flat * ins, transcendentals=0
        ),
    )(x_cells, errors)
    return jnp.transpose(found.reshape(3, 3, 3, outs, ins), (3, 0, 1, 2, 4))


def second_kernel(high, wide, h_ref, e_ref, out_ref):
    rows, _, flat, ins = h_ref.shape
    cells, outs = e_ref.shape
    errors = jnp.transpose(e_ref[...].astype(jnp.float32))
    lane = lax.broadcasted_iota(jnp.int32, (outs, cells), 1)
    col, line, deep = lane % wide, (lane // wide) % high, lane // flat
    found = {}
    for a in range(2):
        for b in range(2):
            for c in range(2):
                by = a * flat + b * wide + c
                ok = (deep + a < rows) & (line + b < high) & (col + c < wide)
                rolled = pltpu.roll(errors, (cells - by) % cells, 1) if by else errors
                found[a, b, c] = jnp.where(ok, rolled, 0.0).astype(jnp.bfloat16)
    for kx in range(3):
        for ky in range(3):
            for kz in range(3):
                kind = ((kx + 1) % 2 * 2 + (ky + 1) % 2) * 2 + (kz + 1) % 2
                left = found[int(kx == 0), int(ky == 0), int(kz == 0)]
                right = h_ref[:, kind].reshape(cells, ins)
                out_ref[(kx * 3 + ky) * 3 + kz] = jnp.dot(
                    left, right, preferred_element_type=jnp.float32
                )


def second_grad(hidden, errors, high, wide):
    rows, _, flat, ins = hidden.shape
    cells, outs = errors.shape
    found = pl.pallas_call(
        functools.partial(second_kernel, high, wide),
        out_shape=jax.ShapeDtypeStruct((27, outs, ins), jnp.float32),
        in_specs=[VMEM, VMEM],
        out_specs=VMEM,
        compiler_params=pltpu.CompilerParams(vmem_limit_bytes=ROOM),
        cost_estimate=pl.CostEstimate(
            flops=54 * outs * ins * cells, bytes_accessed=32 * cells * ins, transcendentals=0
        ),
    )(hidden, errors)
    return jnp.transpose(found.reshape(3, 3, 3, outs, ins), (3, 0, 1, 2, 4))


def shifted(shard, by):
    peers = lax.axis_size("sp")
    pairs = [(i, i + by) for i in range(peers) if 0 <= i + by < peers]
    return lax.ppermute(shard, "sp", pairs)


def conv_plain(field, kernel, strides, pads, dilate):
    return lax.conv_general_dilated(
        field[None],
        kernel,
        strides,
        pads,
        lhs_dilation=dilate,
        dimension_numbers=("NDHWC", "DHWIO", "NDHWC"),
        preferred_element_type=jnp.float32,
    )[0]


def silu_slope(value):
    sig = jax.nn.sigmoid(value)
    return sig * (1.0 + value * (1.0 - sig))


def forward_taps(kernel):
    return jnp.transpose(kernel, (1, 2, 3, 4, 0))


def turned(kernel):
    return jnp.transpose(kernel[:, ::-1, ::-1, ::-1], (1, 2, 3, 0, 4))


def window(whole, below, above, start, size):
    padded = jnp.pad(whole, ((below, above),) + ((0, 0),) * (whole.ndim - 1))
    return lax.dynamic_slice_in_dim(padded, start, size, 0)


def cut_last(array, count):
    parts = array.reshape(array.shape[:-1] + (count, array.shape[-1] // count))
    return jnp.moveaxis(parts, -2, 0)


def cut_rows(array, count):
    parts = array.reshape((array.shape[0], count, array.shape[1] // count) + array.shape[2:])
    return jnp.moveaxis(parts, 1, 0)


def join_rows(parts):
    moved = jnp.moveaxis(parts, 0, 1)
    return moved.reshape((moved.shape[0], moved.shape[1] * moved.shape[2]) + moved.shape[3:])


def join_last(parts):
    moved = jnp.moveaxis(parts, 0, -2)
    return moved.reshape(moved.shape[:-2] + (moved.shape[-2] * moved.shape[-1],))


def own_term(parts_f32, parts_sent, me):
    mine = lax.broadcasted_iota(jnp.int32, (parts_sent.shape[0],) + (1,) * (parts_sent.ndim - 1), 0) == me
    rest = jnp.sum(jnp.where(mine, 0.0, parts_sent.astype(jnp.float32)), 0)
    return rest + lax.dynamic_index_in_dim(parts_f32, me, 0, keepdims=False)


def per_device(activations, w_first, w_second, cotangent):
    planes = activations.shape[0]
    rows = cotangent.shape[0]
    place, me = lax.axis_index("sp"), lax.axis_index("flt")
    count = lax.axis_size("flt")
    line = lax.axis_size("sp")
    single = (1, 1, 1)
    double = (2, 2, 2)
    x_parts, cot_parts = swap(1, (activations, False), (cut_last(cotangent, count), True))
    x_wide, cot_part = join_rows(x_parts), join_rows(cot_parts)
    high, wide = x_wide.shape[1], x_wide.shape[2]
    ins = x_wide.shape[3]
    x_full = lax.all_gather(x_wide, "sp", axis=0, tiled=True)
    x_near = jnp.concatenate([shifted(x_wide, 1), x_wide, shifted(x_wide[:1], -1)], 0)
    first_pre = conv_plain(x_near, forward_taps(w_first), single, ((0, 0), (1, 1), (1, 1)), single)
    plane = lax.broadcasted_iota(jnp.int32, (planes + 1, 1, 1, 1), 0) + place * planes
    hidden = jnp.where(plane > 0, jax.nn.silu(first_pre), 0.0).astype(jnp.bfloat16)
    (h_parts,) = swap(2, (hidden, False))
    h_wide = join_last(h_parts)
    h_own = h_wide[1:].reshape(rows, 2, high // 2, 2, wide // 2, 2, ins)
    h_own = jnp.transpose(h_own, (0, 1, 3, 5, 2, 4, 6)).reshape(rows, 8, high * wide // 4, ins)
    h_full = lax.all_gather(h_own, "sp", axis=0, tiled=True)
    second_pre = conv_plain(
        h_wide, forward_taps(w_second), double, ((0, 0), (1, 0), (1, 0)), single
    )
    second_err = (cot_part.astype(jnp.float32) * silu_slope(second_pre)).astype(jnp.bfloat16)
    outs = second_err.shape[-1]
    e_full = gather_line(second_err.reshape(-1, outs), 3).reshape((line * rows,) + second_err.shape[1:])
    e_near = window(e_full, 0, 1, place * rows, rows + 1)
    back_hidden = conv_plain(e_near, turned(w_second), single, ((1, 0), (1, 2), (1, 2)), double)
    back_parts = cut_last(back_hidden, count)
    section_parts = cut_rows(jax.nn.silu(second_pre), count)
    got, section_got = swap(4, (back_parts.astype(jnp.bfloat16), True), (section_parts, True))
    section_out = join_last(section_got)
    hidden_err = own_term(back_parts, got, me)
    first_err = (hidden_err * silu_slope(first_pre[1:])).astype(jnp.bfloat16)
    f_full = gather_line(first_err.reshape(planes, high * wide, outs), 5)
    f_full = f_full.reshape(line * planes, high * wide, outs)
    f_near = window(f_full, 1, 1, place * planes, planes + 2).reshape(planes + 2, high, wide, outs)
    back_input = conv_plain(f_near, turned(w_first), single, ((0, 0), (1, 1), (1, 1)), single)
    in_parts = cut_rows(back_input, count)
    (in_got,) = swap(6, (in_parts.astype(jnp.bfloat16), True))
    grad_input = own_term(in_parts, in_got, me)
    grad_second = second_grad(h_full, e_full.reshape(-1, outs), high // 2, wide // 2)
    grad_first = first_grad(x_full.reshape(-1, ins), f_full, high, wide)
    return (section_out, grad_input, grad_first, grad_second)


def slope_of(value):
    sig = 1.0 / (1.0 + jnp.exp(-value))
    return sig * (1.0 + value * (1.0 - sig))


def silu_of(value):
    return value / (1.0 + jnp.exp(-value))


def dot_rows(left, right):
    return lax.dot_general(left, right, (((1,), (1,)), ((), ())), preferred_element_type=jnp.float32)


def dot_plain(left, right):
    return jnp.dot(left, right, preferred_element_type=jnp.float32)


class Spread:
    def __init__(self, own, block, local, send, recv, deep, both, mixed=False, cores=True):
        here, me = lax.axis_index("sp"), lax.axis_index("flt")
        self.own, self.block = own, block
        self.local, self.send, self.recv, self.deep, self.both = local, send, recv, deep, both
        self.z, self.y, self.core, self.me = here // 4, (here // 2) % 2, here % 2, me
        self.to_c = (here + 1 - 2 * self.core, me)
        self.sends = []
        self.is_mixed, self.cores = mixed, cores
        across = self.core if mixed else 0 * self.core
        self.near = (self.y + (1 - across) * (1 - 2 * self.y), me + across * (1 - 2 * me))
        self.next = (self.y + across * (1 - 2 * self.y), me + (1 - across) * (1 - 2 * me))
        self.both_off = (1 - self.y, 1 - me)

    def at(self, spot):
        y, part = spot
        return ((self.z * 2 + y) * 2 + self.core, part)

    def push(self, src, dst, slot, place):
        copy = remote(src, dst, self.send.at[len(self.sends)], self.recv.at[slot], place)
        copy.start()
        self.sends.append(copy)

    def took(self, dst, slot):
        remote(dst, dst, self.send.at[0], self.recv.at[slot], self.to_c).wait_recv()

    def view(self, n, spot, core=None):
        zz = lax.rem(self.z + self.deep - n, self.deep) if n else self.z
        return self.block(zz, spot[0], self.core if core is None else core, spot[1])

    def slot(self, kind, n):
        return kind * self.deep + n

    def hand(self, n, spot, kind, place, src=None):
        view = self.view(n, spot)
        self.push(view if src is None else src, view, self.slot(kind, n), place)

    def first(self):
        mine = self.block(self.z, self.y, self.core, self.me)
        for step in range(1, self.deep):
            zz = lax.rem(self.z + step, self.deep)
            self.push(self.own, mine, self.slot(0, step), ((zz * 2 + self.y) * 2 + self.core, self.me))
        self.share(0, self.own)
        self.keep = pltpu.make_async_copy(self.own, mine, self.local)
        self.keep.start()

    def share(self, n, src=None):
        own = (self.y, self.me)
        self.hand(n, own, 1, self.at(self.near), src)
        if self.both:
            self.hand(n, own, 2, self.at(self.next), src)
        if self.cores:
            self.hand(n, own, 4, self.to_c, src)

    def line(self, *steps):
        for n in steps:
            self.took(self.view(n, (self.y, self.me)), self.slot(0, n))
            self.share(n)

    def side(self, *steps):
        for n in steps:
            self.took(self.view(n, self.near), self.slot(1, n))
            if self.both:
                self.hand(n, self.near, 3, self.at(self.next))
            if self.cores:
                self.hand(n, self.near, 5, self.to_c)

    def rest(self, *steps):
        for n in steps:
            self.took(self.view(n, self.next), self.slot(2, n))
            self.hand(n, self.next, 6, self.to_c)
            self.took(self.view(n, self.both_off), self.slot(3, n))
            self.hand(n, self.both_off, 7, self.to_c)

    def ended(self, *steps):
        near, far = (self.next, self.near) if self.is_mixed else (self.near, self.next)
        spots = [(self.y, self.me), near, far, self.both_off]
        for n in steps:
            if n == 0:
                self.keep.wait()
            if not self.cores:
                continue
            for kind, spot in enumerate(spots if self.both else spots[:2]):
                self.took(self.view(n, spot, 1 - self.core), self.slot(4 + kind, n))

    def sent(self):
        for copy in self.sends:
            copy.wait_send()


def spread_sends(deep):
    return (deep - 1) + 7 * deep


def spread_slots(deep):
    return 8 * deep


def chain_kernel(dims, *refs):
    count, high, wide, ins, outs = dims
    x_hbm, w1_hbm, w2_hbm, cot_hbm = refs[:4]
    sec_out, gin_out, found1, found2 = refs[4:8]
    (
        w1, w2, x_near, cot_near, cot_wide, acc, plain, pre, slope, h_own, h_near, sec, e_own, e_next, back_f, back_b,
        back_got, f_near, f_turn, acc_in, in_b, in_got, x_full, h_full, e_full, f_full, f_pair, moved,
        own_sem, send_sem, recv_sem, line_local, line_send, line_recv,
    ) = refs[8:]
    flat = high * wide
    nh, nw = high // 2, wide // 2
    cells = nh * nw
    half = flat // 2
    deep = count // 4
    here, me = lax.axis_index("sp"), lax.axis_index("flt")
    mate = 1 - me
    core = here % 2
    share = outs // 2
    has_up, has_down = here < count - 1, here > 0
    part, up, up_o = (here, mate), (here + 1, me), (here + 1, mate)
    down, down_o = (here - 1, me), (here - 1, mate)
    my_lanes = pl.ds(pl.multiple_of(me * outs, outs), outs)
    mate_lanes = pl.ds(pl.multiple_of(mate * outs, outs), outs)
    my_half = pl.ds(pl.multiple_of(me * half, half), half)
    mate_half = pl.ds(pl.multiple_of(mate * half, half), half)

    load_w1 = pltpu.make_async_copy(w1_hbm, w1, own_sem.at[0])
    load_w2 = pltpu.make_async_copy(w2_hbm, w2, own_sem.at[1])
    load_x = pltpu.make_async_copy(x_hbm, x_near.at[1:3, my_half, :], own_sem.at[2])
    load_cot = pltpu.make_async_copy(
        cot_hbm.at[:, :, my_lanes], cot_near.at[pl.ds(me * (nh // 2), nh // 2)], own_sem.at[3]
    )
    load_x.start()
    load_cot.start()
    load_w1.start()
    load_w2.start()

    def spread(number, own, block, both, mixed=False, cores=True):
        return Spread(
            own, block, line_local.at[number], line_send.at[number], line_recv.at[number], deep, both, mixed, cores
        )

    def half_of(part):
        return pl.ds(pl.multiple_of(part * half, half), half)

    def lanes_of(part):
        return pl.ds(pl.multiple_of(part * outs, outs), outs)

    x_line = spread(
        0,
        x_hbm,
        lambda zz, yy, cc, part: x_full.at[pl.ds(((zz * 2 + yy) * 2 + cc) * 2 + 1, 2), half_of(part), :],
        True,
        True,
    )
    h_line = spread(
        1,
        h_own,
        lambda zz, yy, cc, part: h_full.at[zz, yy, cc, :, :, lanes_of(part)],
        True,
    )
    e_line = spread(
        2, e_own, lambda zz, yy, cc, part: e_full.at[zz, yy, cc], False
    )
    f_line = spread(3, f_pair, lambda zz, yy, cc, part: f_full.at[zz, yy], False, False, False)

    barrier = pltpu.get_barrier_semaphore()

    def hello(place):
        pl.semaphore_signal(barrier, inc=1, device_id=place, device_id_type=MESH)

    zz, yy, cc = here // 4, (here // 2) % 2, here % 2
    always = [part, x_line.to_c, ((zz * 2 + 1 - yy) * 2 + cc, me)]
    for step in range(1, deep):
        always.append(((lax.rem(zz + step, deep) * 2 + yy) * 2 + cc, me))
    for place in always:
        hello(place)

    @pl.when(has_up)
    def _():
        hello(up)
        hello(up_o)

    @pl.when(has_down)
    def _():
        hello(down)
        hello(down_o)

    pl.semaphore_wait(
        barrier, len(always) + 2 * has_up.astype(jnp.int32) + 2 * has_down.astype(jnp.int32)
    )

    started = []

    def send(src, dst, slot, place, cond=None):
        copy = remote(src, dst, send_sem.at[len(started)], recv_sem.at[slot], place)
        if cond is None:
            copy.start()
        else:
            pl.when(cond)(copy.start)
        started.append((copy, cond))

    def wait(src, dst, slot, cond=None):
        copy = remote(src, dst, send_sem.at[0], recv_sem.at[slot], part)
        if cond is None:
            copy.wait_recv()
        else:
            pl.when(cond)(copy.wait_recv)

    send(x_hbm, x_near.at[1:3, my_half, :], 0, part)
    send(x_hbm.at[1], x_near.at[0, my_half, :], 1, up, has_up)
    send(x_hbm.at[1], x_near.at[0, my_half, :], 2, up_o, has_up)
    send(x_hbm.at[0], x_near.at[3, my_half, :], 3, down, has_down)
    send(x_hbm.at[0], x_near.at[3, my_half, :], 4, down_o, has_down)
    cot_rows = pl.ds(me * (nh // 2), nh // 2)
    cot_rows_mate = pl.ds(mate * (nh // 2), nh // 2)
    send(cot_hbm.at[:, :, mate_lanes], cot_near.at[cot_rows], 5, part)
    x_line.first()

    x_full[0] = jnp.zeros((flat, ins), jnp.bfloat16)
    x_full[2 * count + 1] = jnp.zeros((flat, ins), jnp.bfloat16)

    @pl.when(jnp.logical_not(has_down))
    def _():
        x_near[0] = jnp.zeros((flat, ins), jnp.bfloat16)
        h_near[0:4] = jnp.zeros((4, cells, ins), jnp.bfloat16)
        f_near[0] = jnp.zeros((flat, outs), jnp.bfloat16)

    @pl.when(jnp.logical_not(has_up))
    def _():
        x_near[3] = jnp.zeros((flat, ins), jnp.bfloat16)
        e_next[...] = jnp.zeros((cells, outs), jnp.bfloat16)
        f_near[3] = jnp.zeros((flat, outs), jnp.bfloat16)

    load_x.wait()
    wait(x_hbm, x_near.at[1:3, mate_half, :], 0)
    wait(x_hbm.at[1], x_near.at[0, my_half, :], 1, has_down)
    wait(x_hbm.at[1], x_near.at[0, mate_half, :], 2, has_down)
    wait(x_hbm.at[0], x_near.at[3, my_half, :], 3, has_up)
    wait(x_hbm.at[0], x_near.at[3, mate_half, :], 4, has_up)
    load_w1.wait()

    for ky in (1, 0, 2):
        lefts = [x_near[kx : kx + 2].reshape(2 * flat, ins) for kx in range(3)]
        rights = [w1[kx * 9 + ky * 3 : kx * 9 + ky * 3 + 3].reshape(3 * outs, ins) for kx in range(3)]
        total = dot_rows(jnp.concatenate(lefts, 1), jnp.concatenate(rights, 1))
        total = total.reshape(2, flat, 3 * outs)
        if ky == 1:
            acc[...] = total
        elif ky == 0:
            acc[:, wide:, :] += total[:, : flat - wide, :]
        else:
            acc[:, : flat - wide, :] += total[:, wide:, :]
    col = lax.broadcasted_iota(jnp.int32, (2 * flat, outs), 0) % wide
    whole = acc[...].reshape(2 * flat, 3 * outs)
    value = whole[:, outs : 2 * outs]
    value = value + jnp.where(col > 0, pltpu.roll(whole[:, :outs], 1, 0), 0.0)
    value = value + jnp.where(col < wide - 1, pltpu.roll(whole[:, 2 * outs :], 2 * flat - 1, 0), 0.0)
    plain[...] = value

    def pick(px, py, pz, qz):
        return pl.ds(px * flat + py * wide + 2 * qz + pz, nh, 2 * wide)

    for px in (1, 0):
        for py in range(2):
            for pz in range(2):
                kind = (px * 2 + py) * 2 + pz
                found = jnp.concatenate([plain[pick(px, py, pz, qz), :] for qz in range(nw)], 0)
                pre[kind] = found
                h_own[kind] = silu_of(found).astype(jnp.bfloat16)
    send(h_own.at[4:8], h_near.at[0:4, :, my_lanes], 6, up, has_up)
    send(h_own.at[4:8], h_near.at[0:4, :, my_lanes], 7, up_o, has_up)
    send(h_own, h_near.at[4:12, :, my_lanes], 8, part)
    h_line.first()
    keep_h = pltpu.make_async_copy(h_own, h_near.at[4:12, :, my_lanes], own_sem.at[4])
    keep_h.start()
    load_w2.wait()
    load_cot.wait()
    wait(cot_hbm.at[:, :, my_lanes], cot_near.at[cot_rows_mate], 5)
    cot_wide[...] = cot_near[...].astype(jnp.float32)
    slope[...] = slope_of(pre[...])
    keep_h.wait()
    wait(h_own, h_near.at[4:12, :, mate_lanes], 8)
    wait(h_own.at[4:8], h_near.at[0:4, :, my_lanes], 6, has_down)
    wait(h_own.at[4:8], h_near.at[0:4, :, mate_lanes], 7, has_down)
    x_line.line(1, 2)

    row = lax.broadcasted_iota(jnp.int32, (cells, outs), 0)
    qy, qz_of = row % nh, row // nh

    def later_y(v):
        return jnp.where(qy > 0, pltpu.roll(v, 1, 0), 0.0)

    def later_z(v):
        return jnp.where(qz_of > 0, pltpu.roll(v, nh, 0), 0.0)

    def earlier_y(v):
        return jnp.where(qy < nh - 1, pltpu.roll(v, cells - 1, 0), 0.0)

    def earlier_z(v):
        return jnp.where(qz_of < nw - 1, pltpu.roll(v, cells - nh, 0), 0.0)

    groups = {}
    for ky in range(3):
        for kz in range(3):
            for kx in range(3):
                kind = kx * 4 + (ky != 1) * 2 + (kz != 1)
                groups.setdefault((ky == 0, kz == 0), []).append((h_near[kind], w2[kx * 9 + ky * 3 + kz]))
    sums = {
        key: dot_rows(jnp.concatenate([p[0] for p in pairs], 1), jnp.concatenate([p[1] for p in pairs], 1))
        for key, pairs in groups.items()
    }
    second = (
        sums[False, False]
        + later_y(sums[True, False] + later_z(sums[True, True]))
        + later_z(sums[False, True])
    )
    cot = jnp.concatenate([cot_wide[:, qz, :] for qz in range(nw)], 0)
    err = (cot * slope_of(second)).astype(jnp.bfloat16)
    e_own[...] = err
    send(e_own, e_next, 9, down, has_down)
    e_line.first()
    x_line.line(3)
    x_line.side(0)
    shown = silu_of(second)
    for qz in range(nw):
        sec[:, qz, :] = shown[qz * nh : (qz + 1) * nh]
    send(sec.at[cot_rows_mate], sec_out.at[:, :, my_lanes], 10, part)
    keep_sec = pltpu.make_async_copy(sec.at[cot_rows], sec_out.at[:, :, my_lanes], own_sem.at[5])
    keep_sec.start()

    wait(e_own, e_next, 9, has_up)

    def variants(block):
        block = block.astype(jnp.float32)
        moved_y = earlier_y(block)
        found = {
            (0, 0): block,
            (1, 0): moved_y,
            (0, 1): earlier_z(block),
            (1, 1): earlier_z(moved_y),
        }
        return {key: v.astype(jnp.bfloat16) for key, v in found.items()}

    e_here, e_after = variants(err), variants(e_next[...])
    for px in range(2):
        for py in range(2):
            for pz in range(2):
                kind = (px * 2 + py) * 2 + pz
                lefts, rights = [], []
                for kx in (2, 0) if px else (1,):
                    for ky in (2, 0) if py else (1,):
                        for kz in (2, 0) if pz else (1,):
                            source = e_after if kx == 0 else e_here
                            lefts.append(source[int(ky == 0), int(kz == 0)])
                            rights.append(w2[kx * 9 + ky * 3 + kz])
                total = dot_plain(jnp.concatenate(lefts, 1), jnp.concatenate(rights, 0))
                for side in range(2):
                    piece = total[:, side * outs : (side + 1) * outs]
                    back_f[side, kind] = piece
                    back_b[side, kind] = piece.astype(jnp.bfloat16)
    send(back_b.at[mate], back_got, 11, part)
    x_line.side(1, 2, 3)
    h_line.line(1, 2, 3)
    h_line.side(0)
    e_line.line(1, 2, 3)
    wait(back_b.at[me], back_got, 11)
    for px in range(2):
        for py in range(2):
            for pz in range(2):
                kind = (px * 2 + py) * 2 + pz
                total = back_f[me, kind] + back_got[kind].astype(jnp.float32)
                found = (total * slope[kind]).astype(jnp.bfloat16).astype(jnp.float32)
                for qz in range(nw):
                    plain[pick(px, py, pz, qz), :] = found[qz * nh : (qz + 1) * nh]
    first = plain[...]
    f_near[1:3] = first.astype(jnp.bfloat16).reshape(2, flat, outs)
    send(f_near.at[1], f_near.at[3], 12, down, has_down)
    send(f_near.at[2], f_near.at[0], 13, up, has_up)
    f_turn[...] = jnp.transpose(first).astype(jnp.bfloat16).reshape(2, share, 2 * flat)
    send(f_turn.at[1 - core], f_pair.at[core], 15, x_line.to_c)
    f_pair[core] = f_turn[core]
    wait(f_turn.at[core], f_pair.at[1 - core], 15)
    f_line.first()
    wait(f_near.at[1], f_near.at[3], 12, has_up)
    wait(f_near.at[2], f_near.at[0], 13, has_down)

    for kz in range(3):
        for ky in (1, 0, 2):
            lefts = [f_near[2 - kx : 4 - kx].reshape(2 * flat, outs) for kx in range(3)]
            rights = [w1[kx * 9 + ky * 3 + kz] for kx in range(3)]
            total = dot_plain(jnp.concatenate(lefts, 1), jnp.concatenate(rights, 0))
            total = total.reshape(2, flat, ins)
            if ky == 1:
                acc_in[kz] = total
            elif ky == 0:
                acc_in[kz, :, : flat - wide, :] += total[:, wide:, :]
            else:
                acc_in[kz, :, wide:, :] += total[:, : flat - wide, :]
    col = lax.broadcasted_iota(jnp.int32, (2 * flat, ins), 0) % wide
    value = acc_in[1].reshape(2 * flat, ins)
    value = value + jnp.where(
        col < wide - 1, pltpu.roll(acc_in[0].reshape(2 * flat, ins), 2 * flat - 1, 0), 0.0
    )
    value = value + jnp.where(col > 0, pltpu.roll(acc_in[2].reshape(2 * flat, ins), 1, 0), 0.0)
    value = value.reshape(2, flat, ins)
    acc_in[1] = value
    in_b[...] = value.astype(jnp.bfloat16)
    send(in_b.at[:, mate_half, :], in_got, 14, part)
    f_line.line(1, 2, 3)
    x_line.rest(0, 1, 2, 3)
    e_line.side(0, 1, 2, 3)
    h_line.side(1, 2, 3)
    lane = lax.broadcasted_iota(jnp.int32, (share, flat), 1)
    row, col = lane // wide, lane % wide

    def fill(zz):
        def one(block, carry):
            for p in range(2):
                errors = f_full[zz, block // 2, block % 2, :, p * flat : (p + 1) * flat].astype(jnp.float32)
                start = pl.multiple_of((2 * block + p) * flat, flat)
                for ky in range(3):
                    for kz in range(3):
                        by = (ky - 1) * wide + (kz - 1)
                        there_y, there_z = row - (ky - 1), col - (kz - 1)
                        inside = (there_y >= 0) & (there_y < high) & (there_z >= 0) & (there_z < wide)
                        rolled = pltpu.roll(errors, by % flat, 1) if by else errors
                        at = (ky * 3 + kz) * share
                        moved[at : at + share, pl.ds(start, flat)] = jnp.where(inside, rolled, 0.0).astype(
                            jnp.bfloat16
                        )
            return carry

        lax.fori_loop(0, 4, one, 0)

    def gather_taps(zz, fresh):
        def tap(kx, carry):
            right = x_full[pl.ds(zz * 8 + kx, 8)].reshape(8 * flat, ins)
            term = dot_plain(moved[...], right).reshape(9, share, ins)
            found1[kx, :, core] = term if fresh else found1[kx, :, core] + term
            return carry

        lax.fori_loop(0, 3, tap, 0)

    def group(n):
        return lax.rem(here // 4 + deep - n, deep) if n else here // 4

    f_line.side(0)
    f_line.ended(0)
    fill(group(0))
    x_line.ended(0, 1, 2, 3)
    gather_taps(group(0), True)
    wait(in_b.at[:, my_half, :], in_got, 14)
    gin_out[...] = acc_in[1, :, my_half, :] + in_got[...].astype(jnp.float32)
    wait(sec.at[cot_rows], sec_out.at[:, :, mate_lanes], 10)
    keep_sec.wait()
    f_line.side(1)
    fill(group(1))
    gather_taps(group(1), False)
    h_line.rest(0, 1, 2, 3)
    f_line.side(2)
    fill(group(2))
    gather_taps(group(2), False)
    f_line.side(3)
    fill(group(3))
    for kx in range(3):
        right = x_full[pl.ds(group(deep - 1) * 8 + kx, 8)].reshape(8 * flat, ins)
        term = dot_plain(moved[...], right)
        found1[kx, :, core] = found1[kx, :, core] + term.reshape(9, share, ins)
        send(found1.at[kx, :, core], found1.at[kx, :, core], 16 + kx, x_line.to_c)
    e_line.ended(0, 1, 2, 3)
    h_line.ended(0, 1, 2, 3)
    total = count * cells
    errors = jnp.transpose(e_full[...].reshape(total, outs).astype(jnp.float32))
    lane = lax.broadcasted_iota(jnp.int32, (outs, total), 1)
    spot_y, spot_z, spot_x = lane % nh, (lane // nh) % nw, lane // cells
    turned_by = {}
    for a in range(2):
        for b in range(2):
            for c in range(2):
                by = a * cells + c * nh + b
                ok = (spot_x + a < count) & (spot_y + b < nh) & (spot_z + c < nw)
                rolled = pltpu.roll(errors, total - by, 1) if by else errors
                turned_by[a, b, c] = jnp.where(ok, rolled, 0.0).astype(jnp.bfloat16)
    for kind in range(8):
        px, py, pz = kind // 4, (kind // 2) % 2, kind % 2
        taps = [
            (kx, ky, kz)
            for kx in ((0, 2) if px else (1,))
            for ky in ((0, 2) if py else (1,))
            for kz in ((0, 2) if pz else (1,))
        ]
        left = jnp.concatenate([turned_by[int(kx == 0), int(ky == 0), int(kz == 0)] for kx, ky, kz in taps], 0)
        term = dot_plain(left, h_full[:, :, :, kind].reshape(total, ins))
        for n, (kx, ky, kz) in enumerate(taps):
            found2[(kx * 3 + ky) * 3 + kz] = term[n * outs : (n + 1) * outs]
    for kx in range(3):
        wait(found1.at[kx, :, core], found1.at[kx, :, 1 - core], 16 + kx)
    x_line.sent()
    e_line.sent()
    h_line.sent()
    f_line.sent()
    for copy, cond in started:
        if cond is None:
            copy.wait_send()
        else:
            pl.when(cond)(copy.wait_send)


def chain(x, w1, w2, cot):
    count = lax.axis_size("sp")
    planes, high, wide, ins = x.shape
    high = high * 2
    outs = w1.shape[1]
    flat = high * wide
    nh, nw = high // 2, wide // 2
    cells = nh * nw
    deep = count // 4
    dma = pltpu.SemaphoreType.DMA
    bf, f32 = jnp.bfloat16, jnp.float32
    anywhere = pl.BlockSpec(memory_space=pl.ANY)
    shape = jax.ShapeDtypeStruct
    return pl.pallas_call(
        functools.partial(chain_kernel, (count, high, wide, ins, outs)),
        out_shape=[
            shape(cot.shape, f32),
            shape((planes, flat // 2, ins), f32),
            pltpu.VMEM((3, 9, 2, outs // 2, ins), f32),
            pltpu.VMEM((27, outs, ins), f32),
        ],
        in_specs=[anywhere] * 4,
        out_specs=[anywhere, VMEM, VMEM, VMEM],
        scratch_shapes=[
            pltpu.VMEM(w1.shape, bf),
            pltpu.VMEM(w2.shape, bf),
            pltpu.VMEM((4, flat, ins), bf),
            pltpu.VMEM((nh, nw, outs), bf),
            pltpu.VMEM((nh, nw, outs), f32),
            pltpu.VMEM((2, flat, 3 * outs), f32),
            pltpu.VMEM((2 * flat, outs), f32),
            pltpu.VMEM((8, cells, outs), f32),
            pltpu.VMEM((8, cells, outs), f32),
            pltpu.VMEM((8, cells, outs), bf),
            pltpu.VMEM((12, cells, ins), bf),
            pltpu.VMEM((nh, nw, outs), f32),
            pltpu.VMEM((cells, outs), bf),
            pltpu.VMEM((cells, outs), bf),
            pltpu.VMEM((2, 8, cells, outs), f32),
            pltpu.VMEM((2, 8, cells, outs), bf),
            pltpu.VMEM((8, cells, outs), bf),
            pltpu.VMEM((4, flat, outs), bf),
            pltpu.VMEM((2, outs // 2, 2 * flat), bf),
            pltpu.VMEM((3, 2, flat, ins), f32),
            pltpu.VMEM((2, flat, ins), bf),
            pltpu.VMEM((2, flat // 2, ins), bf),
            pltpu.VMEM((planes * count + 2, flat, ins), bf),
            pltpu.VMEM((deep, 2, 2, 8, cells, ins), bf),
            pltpu.VMEM((deep, 2, 2, cells, outs), bf),
            pltpu.VMEM((deep, 2, 2, outs // 2, planes * flat), bf),
            pltpu.VMEM((2, outs // 2, planes * flat), bf),
            pltpu.VMEM((9 * outs // 2, 8 * flat), bf),
            dma((6,)),
            dma((19,)),
            dma((19,)),
            dma((4,)),
            dma((4, spread_sends(deep))),
            dma((4, spread_slots(deep))),
        ],
        compiler_params=pltpu.CompilerParams(
            collective_id=1, has_side_effects=True, vmem_limit_bytes=40 * 1024 * 1024
        ),
    )(*(pltpu.with_memory_space_constraint(a, pltpu.HBM) for a in (x.reshape(planes, flat // 2, ins), w1, w2, cot)))


def write_kernel(*refs):
    sources, places, sem = refs[:4], refs[4:8], refs[8]
    copies = [pltpu.make_async_copy(src, dst, sem.at[n]) for n, (src, dst) in enumerate(zip(sources, places))]
    for copy in copies:
        copy.start()
    for copy in copies:
        copy.wait()


def write(*arrays):
    anywhere = pl.BlockSpec(memory_space=pl.ANY)
    return pl.pallas_call(
        write_kernel,
        out_shape=[jax.ShapeDtypeStruct(a.shape, a.dtype) for a in arrays],
        in_specs=[anywhere] * 4,
        out_specs=[anywhere] * 4,
        scratch_shapes=[pltpu.SemaphoreType.DMA((4,))],
        compiler_params=pltpu.CompilerParams(vmem_limit_bytes=GRANT),
    )(*arrays)


def taps_first(kernel):
    moved = jnp.transpose(kernel, (1, 2, 3, 0, 4))
    return moved.reshape((27,) + moved.shape[3:])


def per_device_pair(activations, w_first, w_second, cotangent):
    planes, part, wide, ins = activations.shape
    outs = w_first.shape[0]

    def home(found):
        return jnp.transpose(found.reshape(3, 3, 3, outs, ins), (3, 0, 1, 2, 4))

    found = chain(activations, taps_first(w_first), taps_first(w_second), cotangent[0])
    sec, gin, grad_first, grad_second = write(*found)
    grad_first, grad_second = home(grad_first), home(grad_second)
    return sec[None], gin.reshape(activations.shape), grad_first, grad_second


def per_device_any(activations, w_first, w_second, cotangent):
    planes, part, wide, ins = activations.shape
    outs = w_first.shape[0]
    pair = (
        lax.axis_size("flt") == 2
        and planes == 2
        and wide == 8
        and part % 8 == 0
        and outs % 128 == 0
        and cotangent.shape[0] == 1
    )
    run = per_device_pair if pair else per_device
    return run(activations, w_first, w_second, cotangent)


def solution(mesh):
    placed = (
        P("sp", "flt", None, None),
        P("flt", None, None, None, None),
        P("flt", None, None, None, None),
        P("sp", "flt", None, None),
    )
    return jax.shard_map(
        per_device_any,
        mesh=mesh,
        in_specs=placed,
        out_specs=(
            P("sp", "flt", None, None),
            P("sp", "flt", None, None),
            P("flt", None, None, None, None),
            P("flt", None, None, None, None),
        ),
        check_vma=False,
    )
```

```python
import functools

import jax
import jax.numpy as jnp
from jax import lax
from jax.experimental import pallas as pl
from jax.experimental.pallas import tpu as pltpu
from jax.sharding import PartitionSpec as P

MESH = pl.DeviceIdType.MESH
VMEM = pl.BlockSpec(memory_space=pltpu.VMEM)
ROOM = 62 * 1024 * 1024
GRANT = 2 * 1024 * 1024


def remote(src, dst, send, recv, place):
    return pltpu.make_async_remote_copy(
        src_ref=src, dst_ref=dst, send_sem=send, recv_sem=recv, device_id=place, device_id_type=MESH
    )


def greet(places):
    barrier = pltpu.get_barrier_semaphore()
    for place in places:
        pl.semaphore_signal(barrier, inc=1, device_id=place, device_id_type=MESH)
    pl.semaphore_wait(barrier, len(places))


def line_kernel(count, own, out, local, recv, send_z, send_y, send_c):
    here, other = lax.axis_index("sp"), lax.axis_index("flt")
    deep = count // 4
    z, y, core = here // 4, (here // 2) % 2, here % 2

    def spot(zz, yy, cc):
        return (zz * 2 + yy) * 2 + cc

    far = [lax.rem(z + step, deep) for step in range(1, deep)]
    to_y = (spot(z, 1 - y, core), other)
    to_c = (spot(z, y, 1 - core), other)
    greet([(spot(zz, y, core), other) for zz in far] + [to_y, to_c])
    sends = []

    def push(src, slot, send, place):
        copy = remote(src, out.at[slot], send, recv.at[slot], place)
        copy.start()
        sends.append(copy)

    def arrived(slot):
        remote(own, out.at[slot], send_y.at[0], recv.at[slot], to_y).wait_recv()

    for n, zz in enumerate(far):
        push(own, here, send_z.at[n], (spot(zz, y, core), other))
    push(own, here, send_y.at[0], to_y)
    push(own, here, send_c.at[0], to_c)
    keep = pltpu.make_async_copy(own, out.at[here], local)
    keep.start()
    for n in range(1, deep):
        slot = spot(lax.rem(z + deep - n, deep), y, core)
        arrived(slot)
        push(out.at[slot], slot, send_y.at[n], to_y)
        push(out.at[slot], slot, send_c.at[n], to_c)
    for n in range(deep):
        slot = spot(lax.rem(z + deep - n, deep), 1 - y, core)
        arrived(slot)
        push(out.at[slot], slot, send_c.at[deep + n], to_c)
    for n in range(deep):
        for yy in (y, 1 - y):
            arrived(spot(lax.rem(z + deep - n, deep), yy, 1 - core))
    keep.wait()
    for copy in sends:
        copy.wait_send()


def gather_line(block, number):
    count = lax.axis_size("sp")
    deep = count // 4
    dma = pltpu.SemaphoreType.DMA
    return pl.pallas_call(
        functools.partial(line_kernel, count),
        out_shape=jax.ShapeDtypeStruct((count,) + block.shape, block.dtype),
        in_specs=[VMEM],
        out_specs=VMEM,
        scratch_shapes=[dma, dma((count,)), dma((max(deep - 1, 1),)), dma((deep,)), dma((2 * deep,))],
        compiler_params=pltpu.CompilerParams(
            collective_id=number, has_side_effects=True, vmem_limit_bytes=ROOM
        ),
    )(block)


def swap_kernel(count, split, *refs):
    kinds = len(split)
    ins, outs = refs[:kinds], refs[kinds : 2 * kinds]
    local, send, recv = refs[2 * kinds :]
    here, me = lax.axis_index("sp"), lax.axis_index("flt")
    peers = [lax.rem(me + step, count) for step in range(1, count)]
    greet([(here, peer) for peer in peers])
    sends, keeps = [], []
    for k in range(kinds):
        for n, peer in enumerate(peers):
            src = ins[k].at[peer] if split[k] else ins[k]
            copy = remote(src, outs[k].at[me], send.at[k, n], recv.at[k, me], (here, peer))
            copy.start()
            sends.append(copy)
        keep = pltpu.make_async_copy(ins[k].at[me] if split[k] else ins[k], outs[k].at[me], local.at[k])
        keep.start()
        keeps.append(keep)
    for k in range(kinds):
        for n, peer in enumerate(peers):
            src = ins[k].at[peer] if split[k] else ins[k]
            remote(src, outs[k].at[peer], send.at[k, n], recv.at[k, peer], (here, peer)).wait_recv()
    for copy in sends:
        copy.wait_send()
    for keep in keeps:
        keep.wait()


def swap(number, *pieces):
    count = lax.axis_size("flt")
    split = tuple(cut for _, cut in pieces)
    arrays = [array for array, _ in pieces]
    dma = pltpu.SemaphoreType.DMA
    shapes = [a.shape if cut else (count,) + a.shape for a, cut in pieces]
    return pl.pallas_call(
        functools.partial(swap_kernel, count, split),
        out_shape=[jax.ShapeDtypeStruct(s, a.dtype) for s, a in zip(shapes, arrays)],
        in_specs=[VMEM] * len(arrays),
        out_specs=[VMEM] * len(arrays),
        scratch_shapes=[
            dma((len(arrays),)),
            dma((len(arrays), max(count - 1, 1))),
            dma((len(arrays), count)),
        ],
        compiler_params=pltpu.CompilerParams(
            collective_id=number, has_side_effects=True, vmem_limit_bytes=ROOM
        ),
    )(*arrays)


def first_kernel(high, wide, x_ref, e_ref, out_ref, moved):
    planes, flat, outs = e_ref.shape
    lane = lax.broadcasted_iota(jnp.int32, (outs, flat), 1)
    row, col = lane // wide, lane % wide
    blank = jnp.zeros((9 * outs, flat), jnp.bfloat16)
    moved[:, 0:flat] = blank
    moved[:, (planes + 1) * flat : (planes + 2) * flat] = blank

    def fill(plane, carry):
        errors = jnp.transpose(e_ref[plane].astype(jnp.float32))
        start = pl.multiple_of((plane + 1) * flat, flat)
        for ky in range(3):
            for kz in range(3):
                by = (ky - 1) * wide + (kz - 1)
                there_y, there_z = row - (ky - 1), col - (kz - 1)
                inside = (there_y >= 0) & (there_y < high) & (there_z >= 0) & (there_z < wide)
                turned_by = pltpu.roll(errors, by % flat, 1) if by else errors
                at = (ky * 3 + kz) * outs
                moved[at : at + outs, pl.ds(start, flat)] = jnp.where(inside, turned_by, 0.0).astype(
                    jnp.bfloat16
                )
        return carry

    lax.fori_loop(0, planes, fill, 0)

    def tap(step, carry):
        kx, ky = step // 3, step % 3
        left = moved[
            pl.ds(pl.multiple_of(ky * 3 * outs, 3 * outs), 3 * outs),
            pl.ds(pl.multiple_of((2 - kx) * flat, flat), planes * flat),
        ]
        out_ref[step] = jnp.dot(left, x_ref[...], preferred_element_type=jnp.float32)
        return carry

    lax.fori_loop(0, 9, tap, 0)


def first_grad(x_cells, errors, high, wide):
    planes, flat, outs = errors.shape
    ins = x_cells.shape[1]
    found = pl.pallas_call(
        functools.partial(first_kernel, high, wide),
        out_shape=jax.ShapeDtypeStruct((9, 3 * outs, ins), jnp.float32),
        in_specs=[VMEM, VMEM],
        out_specs=VMEM,
        scratch_shapes=[pltpu.VMEM((9 * outs, (planes + 2) * flat), jnp.bfloat16)],
        compiler_params=pltpu.CompilerParams(vmem_limit_bytes=ROOM),
        cost_estimate=pl.CostEstimate(
            flops=54 * outs * ins * planes * flat, bytes_accessed=8 * planes * flat * ins, transcendentals=0
        ),
    )(x_cells, errors)
    return jnp.transpose(found.reshape(3, 3, 3, outs, ins), (3, 0, 1, 2, 4))


def second_kernel(high, wide, h_ref, e_ref, out_ref):
    rows, _, flat, ins = h_ref.shape
    cells, outs = e_ref.shape
    errors = jnp.transpose(e_ref[...].astype(jnp.float32))
    lane = lax.broadcasted_iota(jnp.int32, (outs, cells), 1)
    col, line, deep = lane % wide, (lane // wide) % high, lane // flat
    found = {}
    for a in range(2):
        for b in range(2):
            for c in range(2):
                by = a * flat + b * wide + c
                ok = (deep + a < rows) & (line + b < high) & (col + c < wide)
                rolled = pltpu.roll(errors, (cells - by) % cells, 1) if by else errors
                found[a, b, c] = jnp.where(ok, rolled, 0.0).astype(jnp.bfloat16)
    for kx in range(3):
        for ky in range(3):
            for kz in range(3):
                kind = ((kx + 1) % 2 * 2 + (ky + 1) % 2) * 2 + (kz + 1) % 2
                left = found[int(kx == 0), int(ky == 0), int(kz == 0)]
                right = h_ref[:, kind].reshape(cells, ins)
                out_ref[(kx * 3 + ky) * 3 + kz] = jnp.dot(
                    left, right, preferred_element_type=jnp.float32
                )


def second_grad(hidden, errors, high, wide):
    rows, _, flat, ins = hidden.shape
    cells, outs = errors.shape
    found = pl.pallas_call(
        functools.partial(second_kernel, high, wide),
        out_shape=jax.ShapeDtypeStruct((27, outs, ins), jnp.float32),
        in_specs=[VMEM, VMEM],
        out_specs=VMEM,
        compiler_params=pltpu.CompilerParams(vmem_limit_bytes=ROOM),
        cost_estimate=pl.CostEstimate(
            flops=54 * outs * ins * cells, bytes_accessed=32 * cells * ins, transcendentals=0
        ),
    )(hidden, errors)
    return jnp.transpose(found.reshape(3, 3, 3, outs, ins), (3, 0, 1, 2, 4))


def shifted(shard, by):
    peers = lax.axis_size("sp")
    pairs = [(i, i + by) for i in range(peers) if 0 <= i + by < peers]
    return lax.ppermute(shard, "sp", pairs)


def conv_plain(field, kernel, strides, pads, dilate):
    return lax.conv_general_dilated(
        field[None],
        kernel,
        strides,
        pads,
        lhs_dilation=dilate,
        dimension_numbers=("NDHWC", "DHWIO", "NDHWC"),
        preferred_element_type=jnp.float32,
    )[0]


def silu_slope(value):
    sig = jax.nn.sigmoid(value)
    return sig * (1.0 + value * (1.0 - sig))


def forward_taps(kernel):
    return jnp.transpose(kernel, (1, 2, 3, 4, 0))


def turned(kernel):
    return jnp.transpose(kernel[:, ::-1, ::-1, ::-1], (1, 2, 3, 0, 4))


def window(whole, below, above, start, size):
    padded = jnp.pad(whole, ((below, above),) + ((0, 0),) * (whole.ndim - 1))
    return lax.dynamic_slice_in_dim(padded, start, size, 0)


def cut_last(array, count):
    parts = array.reshape(array.shape[:-1] + (count, array.shape[-1] // count))
    return jnp.moveaxis(parts, -2, 0)


def cut_rows(array, count):
    parts = array.reshape((array.shape[0], count, array.shape[1] // count) + array.shape[2:])
    return jnp.moveaxis(parts, 1, 0)


def join_rows(parts):
    moved = jnp.moveaxis(parts, 0, 1)
    return moved.reshape((moved.shape[0], moved.shape[1] * moved.shape[2]) + moved.shape[3:])


def join_last(parts):
    moved = jnp.moveaxis(parts, 0, -2)
    return moved.reshape(moved.shape[:-2] + (moved.shape[-2] * moved.shape[-1],))


def own_term(parts_f32, parts_sent, me):
    mine = lax.broadcasted_iota(jnp.int32, (parts_sent.shape[0],) + (1,) * (parts_sent.ndim - 1), 0) == me
    rest = jnp.sum(jnp.where(mine, 0.0, parts_sent.astype(jnp.float32)), 0)
    return rest + lax.dynamic_index_in_dim(parts_f32, me, 0, keepdims=False)


def per_device(activations, w_first, w_second, cotangent):
    planes = activations.shape[0]
    rows = cotangent.shape[0]
    place, me = lax.axis_index("sp"), lax.axis_index("flt")
    count = lax.axis_size("flt")
    line = lax.axis_size("sp")
    single = (1, 1, 1)
    double = (2, 2, 2)
    x_parts, cot_parts = swap(1, (activations, False), (cut_last(cotangent, count), True))
    x_wide, cot_part = join_rows(x_parts), join_rows(cot_parts)
    high, wide = x_wide.shape[1], x_wide.shape[2]
    ins = x_wide.shape[3]
    x_full = lax.all_gather(x_wide, "sp", axis=0, tiled=True)
    x_near = jnp.concatenate([shifted(x_wide, 1), x_wide, shifted(x_wide[:1], -1)], 0)
    first_pre = conv_plain(x_near, forward_taps(w_first), single, ((0, 0), (1, 1), (1, 1)), single)
    plane = lax.broadcasted_iota(jnp.int32, (planes + 1, 1, 1, 1), 0) + place * planes
    hidden = jnp.where(plane > 0, jax.nn.silu(first_pre), 0.0).astype(jnp.bfloat16)
    (h_parts,) = swap(2, (hidden, False))
    h_wide = join_last(h_parts)
    h_own = h_wide[1:].reshape(rows, 2, high // 2, 2, wide // 2, 2, ins)
    h_own = jnp.transpose(h_own, (0, 1, 3, 5, 2, 4, 6)).reshape(rows, 8, high * wide // 4, ins)
    h_full = lax.all_gather(h_own, "sp", axis=0, tiled=True)
    second_pre = conv_plain(
        h_wide, forward_taps(w_second), double, ((0, 0), (1, 0), (1, 0)), single
    )
    second_err = (cot_part.astype(jnp.float32) * silu_slope(second_pre)).astype(jnp.bfloat16)
    outs = second_err.shape[-1]
    e_full = gather_line(second_err.reshape(-1, outs), 3).reshape((line * rows,) + second_err.shape[1:])
    e_near = window(e_full, 0, 1, place * rows, rows + 1)
    back_hidden = conv_plain(e_near, turned(w_second), single, ((1, 0), (1, 2), (1, 2)), double)
    back_parts = cut_last(back_hidden, count)
    section_parts = cut_rows(jax.nn.silu(second_pre), count)
    got, section_got = swap(4, (back_parts.astype(jnp.bfloat16), True), (section_parts, True))
    section_out = join_last(section_got)
    hidden_err = own_term(back_parts, got, me)
    first_err = (hidden_err * silu_slope(first_pre[1:])).astype(jnp.bfloat16)
    f_full = gather_line(first_err.reshape(planes, high * wide, outs), 5)
    f_full = f_full.reshape(line * planes, high * wide, outs)
    f_near = window(f_full, 1, 1, place * planes, planes + 2).reshape(planes + 2, high, wide, outs)
    back_input = conv_plain(f_near, turned(w_first), single, ((0, 0), (1, 1), (1, 1)), single)
    in_parts = cut_rows(back_input, count)
    (in_got,) = swap(6, (in_parts.astype(jnp.bfloat16), True))
    grad_input = own_term(in_parts, in_got, me)
    grad_second = second_grad(h_full, e_full.reshape(-1, outs), high // 2, wide // 2)
    grad_first = first_grad(x_full.reshape(-1, ins), f_full, high, wide)
    return (section_out, grad_input, grad_first, grad_second)


def slope_of(value):
    sig = 1.0 / (1.0 + jnp.exp(-value))
    return sig * (1.0 + value * (1.0 - sig))


def silu_of(value):
    return value / (1.0 + jnp.exp(-value))


def dot_rows(left, right):
    return lax.dot_general(left, right, (((1,), (1,)), ((), ())), preferred_element_type=jnp.float32)


def dot_plain(left, right):
    return jnp.dot(left, right, preferred_element_type=jnp.float32)


class Spread:
    def __init__(self, own, block, local, send, recv, deep, both, mixed=False, cores=True):
        here, me = lax.axis_index("sp"), lax.axis_index("flt")
        self.own, self.block = own, block
        self.local, self.send, self.recv, self.deep, self.both = local, send, recv, deep, both
        self.z, self.y, self.core, self.me = here // 4, (here // 2) % 2, here % 2, me
        self.to_c = (here + 1 - 2 * self.core, me)
        self.sends = []
        self.twin = None
        self.is_mixed, self.cores = mixed, cores
        across = self.core if mixed else 0 * self.core
        self.near = (self.y + (1 - across) * (1 - 2 * self.y), me + across * (1 - 2 * me))
        self.next = (self.y + across * (1 - 2 * self.y), me + (1 - across) * (1 - 2 * me))
        self.both_off = (1 - self.y, 1 - me)

    def at(self, spot):
        y, part = spot
        return ((self.z * 2 + y) * 2 + self.core, part)

    def push(self, src, dst, slot, place):
        copy = remote(src, dst, self.send.at[len(self.sends)], self.recv.at[slot], place)
        copy.start()
        self.sends.append(copy)

    def took(self, dst, slot):
        remote(dst, dst, self.send.at[0], self.recv.at[slot], self.to_c).wait_recv()

    def view(self, n, spot, core=None):
        zz = lax.rem(self.z + self.deep - n, self.deep) if n else self.z
        return self.block(zz, spot[0], self.core if core is None else core, spot[1])

    def slot(self, kind, n):
        return kind * self.deep + n

    def hand(self, n, spot, kind, place, src=None):
        view = self.view(n, spot)
        self.push(view if src is None else src, view, self.slot(kind, n), place)

    def first(self):
        mine = self.block(self.z, self.y, self.core, self.me)
        for step in range(1, self.deep):
            zz = lax.rem(self.z + step, self.deep)
            self.push(self.own, mine, self.slot(0, step), ((zz * 2 + self.y) * 2 + self.core, self.me))
        self.share(0, self.own)
        self.keep = pltpu.make_async_copy(self.own, mine, self.local)
        self.keep.start()

    def share(self, n, src=None):
        own = (self.y, self.me)
        self.hand(n, own, 1, self.at(self.near), src)
        if self.both and (n or self.twin is None):
            self.hand(n, own, 2, self.at(self.next), src)
        if self.cores:
            self.hand(n, own, 4, self.to_c, src)

    def line(self, *steps):
        for n in steps:
            self.took(self.view(n, (self.y, self.me)), self.slot(0, n))
            self.share(n)

    def side(self, *steps):
        for n in steps:
            self.took(self.view(n, self.near), self.slot(1, n))
            if self.both:
                self.hand(n, self.near, 3, self.at(self.next))
            if self.cores:
                self.hand(n, self.near, 5, self.to_c)

    def rest(self, *steps):
        for n in steps:
            if n or self.twin is None:
                self.took(self.view(n, self.next), self.slot(2, n))
            else:
                self.twin.wait()
            self.hand(n, self.next, 6, self.to_c)
            self.took(self.view(n, self.both_off), self.slot(3, n))
            self.hand(n, self.both_off, 7, self.to_c)

    def ended(self, *steps):
        near, far = (self.next, self.near) if self.is_mixed else (self.near, self.next)
        spots = [(self.y, self.me), near, far, self.both_off]
        for n in steps:
            if n == 0:
                self.keep.wait()
            if not self.cores:
                continue
            for kind, spot in enumerate(spots if self.both else spots[:2]):
                self.took(self.view(n, spot, 1 - self.core), self.slot(4 + kind, n))

    def sent(self):
        for copy in self.sends:
            copy.wait_send()


def spread_sends(deep):
    return (deep - 1) + 7 * deep


def spread_slots(deep):
    return 8 * deep


def chain_kernel(dims, *refs):
    count, high, wide, ins, outs = dims
    x_hbm, w1_hbm, w2_hbm, cot_hbm = refs[:4]
    sec_out, gin_out, found1, found2 = refs[4:8]
    (
        w1, w2, x_near, cot_near, cot_wide, acc, plain, pre, slope, h_own, h_near, sec, e_own, e_next, back_f, back_b,
        back_got, f_near, f_turn, acc_in, in_b, in_got, x_full, h_full, e_full, f_full, f_pair, moved,
        own_sem, send_sem, recv_sem, line_local, line_send, line_recv,
    ) = refs[8:]
    flat = high * wide
    nh, nw = high // 2, wide // 2
    cells = nh * nw
    half = flat // 2
    deep = count // 4
    here, me = lax.axis_index("sp"), lax.axis_index("flt")
    mate = 1 - me
    core = here % 2
    share = outs // 2
    has_up, has_down = here < count - 1, here > 0
    part, up, up_o = (here, mate), (here + 1, me), (here + 1, mate)
    down, down_o = (here - 1, me), (here - 1, mate)
    my_lanes = pl.ds(pl.multiple_of(me * outs, outs), outs)
    mate_lanes = pl.ds(pl.multiple_of(mate * outs, outs), outs)
    my_half = pl.ds(pl.multiple_of(me * half, half), half)
    mate_half = pl.ds(pl.multiple_of(mate * half, half), half)

    load_w1 = pltpu.make_async_copy(w1_hbm, w1, own_sem.at[0])
    load_w2 = pltpu.make_async_copy(w2_hbm, w2, own_sem.at[1])
    load_x = pltpu.make_async_copy(x_hbm, x_near.at[1:3, my_half, :], own_sem.at[2])
    load_cot = pltpu.make_async_copy(
        cot_hbm.at[:, :, my_lanes], cot_near.at[pl.ds(me * (nh // 2), nh // 2)], own_sem.at[3]
    )
    load_x.start()
    load_cot.start()
    load_w1.start()
    load_w2.start()

    def spread(number, own, block, both, mixed=False, cores=True):
        return Spread(
            own, block, line_local.at[number], line_send.at[number], line_recv.at[number], deep, both, mixed, cores
        )

    def half_of(part):
        return pl.ds(pl.multiple_of(part * half, half), half)

    def lanes_of(part):
        return pl.ds(pl.multiple_of(part * outs, outs), outs)

    x_line = spread(
        0,
        x_hbm,
        lambda zz, yy, cc, part: x_full.at[pl.ds(((zz * 2 + yy) * 2 + cc) * 2 + 1, 2), half_of(part), :],
        True,
        True,
    )
    h_line = spread(
        1,
        h_own,
        lambda zz, yy, cc, part: h_full.at[zz, yy, cc, :, :, lanes_of(part)],
        True,
    )
    e_line = spread(
        2, e_own, lambda zz, yy, cc, part: e_full.at[zz, yy, cc], False
    )
    f_line = spread(3, f_pair, lambda zz, yy, cc, part: f_full.at[zz, yy], False, False, False)

    h_line.twin = pltpu.make_async_copy(
        h_near.at[4:12, :, mate_lanes], h_line.view(0, h_line.next), own_sem.at[6]
    )

    barrier = pltpu.get_barrier_semaphore()

    def hello(place):
        pl.semaphore_signal(barrier, inc=1, device_id=place, device_id_type=MESH)

    zz, yy, cc = here // 4, (here // 2) % 2, here % 2
    always = [part, x_line.to_c, ((zz * 2 + 1 - yy) * 2 + cc, me)]
    for step in range(1, deep):
        always.append(((lax.rem(zz + step, deep) * 2 + yy) * 2 + cc, me))
    for place in always:
        hello(place)

    @pl.when(has_up)
    def _():
        hello(up)
        hello(up_o)

    @pl.when(has_down)
    def _():
        hello(down)
        hello(down_o)

    pl.semaphore_wait(
        barrier, len(always) + 2 * has_up.astype(jnp.int32) + 2 * has_down.astype(jnp.int32)
    )

    started = []

    def send(src, dst, slot, place, cond=None):
        copy = remote(src, dst, send_sem.at[len(started)], recv_sem.at[slot], place)
        if cond is None:
            copy.start()
        else:
            pl.when(cond)(copy.start)
        started.append((copy, cond))

    def wait(src, dst, slot, cond=None):
        copy = remote(src, dst, send_sem.at[0], recv_sem.at[slot], part)
        if cond is None:
            copy.wait_recv()
        else:
            pl.when(cond)(copy.wait_recv)

    send(x_hbm, x_near.at[1:3, my_half, :], 0, part)
    send(x_hbm.at[1], x_near.at[0, my_half, :], 1, up, has_up)
    send(x_hbm.at[1], x_near.at[0, my_half, :], 2, up_o, has_up)
    send(x_hbm.at[0], x_near.at[3, my_half, :], 3, down, has_down)
    send(x_hbm.at[0], x_near.at[3, my_half, :], 4, down_o, has_down)
    cot_rows = pl.ds(me * (nh // 2), nh // 2)
    cot_rows_mate = pl.ds(mate * (nh // 2), nh // 2)
    send(cot_hbm.at[:, :, mate_lanes], cot_near.at[cot_rows], 5, part)
    x_line.first()

    x_full[0] = jnp.zeros((flat, ins), jnp.bfloat16)
    x_full[2 * count + 1] = jnp.zeros((flat, ins), jnp.bfloat16)

    @pl.when(jnp.logical_not(has_down))
    def _():
        x_near[0] = jnp.zeros((flat, ins), jnp.bfloat16)
        h_near[0:4] = jnp.zeros((4, cells, ins), jnp.bfloat16)
        f_near[0] = jnp.zeros((flat, outs), jnp.bfloat16)

    @pl.when(jnp.logical_not(has_up))
    def _():
        x_near[3] = jnp.zeros((flat, ins), jnp.bfloat16)
        e_next[...] = jnp.zeros((cells, outs), jnp.bfloat16)
        f_near[3] = jnp.zeros((flat, outs), jnp.bfloat16)

    load_x.wait()
    wait(x_hbm, x_near.at[1:3, mate_half, :], 0)
    wait(x_hbm.at[1], x_near.at[0, my_half, :], 1, has_down)
    wait(x_hbm.at[1], x_near.at[0, mate_half, :], 2, has_down)
    wait(x_hbm.at[0], x_near.at[3, my_half, :], 3, has_up)
    wait(x_hbm.at[0], x_near.at[3, mate_half, :], 4, has_up)
    load_w1.wait()

    for ky in (1, 0, 2):
        lefts = [x_near[kx : kx + 2].reshape(2 * flat, ins) for kx in range(3)]
        rights = [w1[kx * 9 + ky * 3 : kx * 9 + ky * 3 + 3].reshape(3 * outs, ins) for kx in range(3)]
        total = dot_rows(jnp.concatenate(lefts, 1), jnp.concatenate(rights, 1))
        total = total.reshape(2, flat, 3 * outs)
        if ky == 1:
            acc[...] = total
        elif ky == 0:
            acc[:, wide:, :] += total[:, : flat - wide, :]
        else:
            acc[:, : flat - wide, :] += total[:, wide:, :]
    col = lax.broadcasted_iota(jnp.int32, (2 * flat, outs), 0) % wide
    whole = acc[...].reshape(2 * flat, 3 * outs)
    value = whole[:, outs : 2 * outs]
    value = value + jnp.where(col > 0, pltpu.roll(whole[:, :outs], 1, 0), 0.0)
    value = value + jnp.where(col < wide - 1, pltpu.roll(whole[:, 2 * outs :], 2 * flat - 1, 0), 0.0)
    plain[...] = value

    def pick(px, py, pz, qz):
        return pl.ds(px * flat + py * wide + 2 * qz + pz, nh, 2 * wide)

    for px in (1, 0):
        for py in range(2):
            for pz in range(2):
                kind = (px * 2 + py) * 2 + pz
                found = jnp.concatenate([plain[pick(px, py, pz, qz), :] for qz in range(nw)], 0)
                pre[kind] = found
                h_own[kind] = silu_of(found).astype(jnp.bfloat16)
        if px == 1:
            send(h_own.at[4:8], h_near.at[0:4, :, my_lanes], 6, up, has_up)
            send(h_own.at[4:8], h_near.at[0:4, :, my_lanes], 7, up_o, has_up)
    send(h_own, h_near.at[4:12, :, my_lanes], 8, part)
    h_line.first()
    keep_h = pltpu.make_async_copy(h_own, h_near.at[4:12, :, my_lanes], own_sem.at[4])
    keep_h.start()
    load_w2.wait()
    load_cot.wait()
    wait(cot_hbm.at[:, :, my_lanes], cot_near.at[cot_rows_mate], 5)
    cot_wide[...] = cot_near[...].astype(jnp.float32)
    slope[...] = slope_of(pre[...])
    keep_h.wait()
    wait(h_own, h_near.at[4:12, :, mate_lanes], 8)
    h_line.twin.start()
    wait(h_own.at[4:8], h_near.at[0:4, :, my_lanes], 6, has_down)
    wait(h_own.at[4:8], h_near.at[0:4, :, mate_lanes], 7, has_down)
    x_line.line(1, 2)

    row = lax.broadcasted_iota(jnp.int32, (cells, outs), 0)
    qy, qz_of = row % nh, row // nh

    def later_y(v):
        return jnp.where(qy > 0, pltpu.roll(v, 1, 0), 0.0)

    def later_z(v):
        return jnp.where(qz_of > 0, pltpu.roll(v, nh, 0), 0.0)

    def earlier_y(v):
        return jnp.where(qy < nh - 1, pltpu.roll(v, cells - 1, 0), 0.0)

    def earlier_z(v):
        return jnp.where(qz_of < nw - 1, pltpu.roll(v, cells - nh, 0), 0.0)

    groups = {}
    for ky in range(3):
        for kz in range(3):
            for kx in range(3):
                kind = kx * 4 + (ky != 1) * 2 + (kz != 1)
                groups.setdefault((ky == 0, kz == 0), []).append((h_near[kind], w2[kx * 9 + ky * 3 + kz]))
    sums = {
        key: dot_rows(jnp.concatenate([p[0] for p in pairs], 1), jnp.concatenate([p[1] for p in pairs], 1))
        for key, pairs in groups.items()
    }
    second = (
        sums[False, False]
        + later_y(sums[True, False] + later_z(sums[True, True]))
        + later_z(sums[False, True])
    )
    cot = jnp.concatenate([cot_wide[:, qz, :] for qz in range(nw)], 0)
    err = (cot * slope_of(second)).astype(jnp.bfloat16)
    e_own[...] = err
    send(e_own, e_next, 9, down, has_down)
    e_line.first()
    x_line.line(3)
    x_line.side(0)
    shown = silu_of(second)
    for qz in range(nw):
        sec[:, qz, :] = shown[qz * nh : (qz + 1) * nh]
    send(sec.at[cot_rows_mate], sec_out.at[:, :, my_lanes], 10, part)
    keep_sec = pltpu.make_async_copy(sec.at[cot_rows], sec_out.at[:, :, my_lanes], own_sem.at[5])
    keep_sec.start()

    wait(e_own, e_next, 9, has_up)

    def variants(block):
        block = block.astype(jnp.float32)
        moved_y = earlier_y(block)
        found = {
            (0, 0): block,
            (1, 0): moved_y,
            (0, 1): earlier_z(block),
            (1, 1): earlier_z(moved_y),
        }
        return {key: v.astype(jnp.bfloat16) for key, v in found.items()}

    e_here, e_after = variants(err), variants(e_next[...])
    for px in range(2):
        for py in range(2):
            for pz in range(2):
                kind = (px * 2 + py) * 2 + pz
                lefts, rights = [], []
                for kx in (2, 0) if px else (1,):
                    for ky in (2, 0) if py else (1,):
                        for kz in (2, 0) if pz else (1,):
                            source = e_after if kx == 0 else e_here
                            lefts.append(source[int(ky == 0), int(kz == 0)])
                            rights.append(w2[kx * 9 + ky * 3 + kz])
                total = dot_plain(jnp.concatenate(lefts, 1), jnp.concatenate(rights, 0))
                for side in range(2):
                    piece = total[:, side * outs : (side + 1) * outs]
                    back_f[side, kind] = piece
                    back_b[side, kind] = piece.astype(jnp.bfloat16)
    send(back_b.at[mate], back_got, 11, part)
    x_line.side(1, 2, 3)
    h_line.line(1, 2, 3)
    h_line.side(0)
    e_line.line(1, 2, 3)
    wait(back_b.at[me], back_got, 11)
    for px in range(2):
        for py in range(2):
            for pz in range(2):
                kind = (px * 2 + py) * 2 + pz
                total = back_f[me, kind] + back_got[kind].astype(jnp.float32)
                found = (total * slope[kind]).astype(jnp.bfloat16).astype(jnp.float32)
                for qz in range(nw):
                    plain[pick(px, py, pz, qz), :] = found[qz * nh : (qz + 1) * nh]
    first = plain[...]
    f_near[1:3] = first.astype(jnp.bfloat16).reshape(2, flat, outs)
    send(f_near.at[1], f_near.at[3], 12, down, has_down)
    send(f_near.at[2], f_near.at[0], 13, up, has_up)
    f_turn[...] = jnp.transpose(first).astype(jnp.bfloat16).reshape(2, share, 2 * flat)
    send(f_turn.at[1 - core], f_pair.at[core], 15, x_line.to_c)
    f_pair[core] = f_turn[core]
    wait(f_turn.at[core], f_pair.at[1 - core], 15)
    f_line.first()
    wait(f_near.at[1], f_near.at[3], 12, has_up)
    wait(f_near.at[2], f_near.at[0], 13, has_down)

    for kz in range(3):
        for ky in (1, 0, 2):
            lefts = [f_near[2 - kx : 4 - kx].reshape(2 * flat, outs) for kx in range(3)]
            rights = [w1[kx * 9 + ky * 3 + kz] for kx in range(3)]
            total = dot_plain(jnp.concatenate(lefts, 1), jnp.concatenate(rights, 0))
            total = total.reshape(2, flat, ins)
            if ky == 1:
                acc_in[kz] = total
            elif ky == 0:
                acc_in[kz, :, : flat - wide, :] += total[:, wide:, :]
            else:
                acc_in[kz, :, wide:, :] += total[:, : flat - wide, :]
    col = lax.broadcasted_iota(jnp.int32, (2 * flat, ins), 0) % wide
    value = acc_in[1].reshape(2 * flat, ins)
    value = value + jnp.where(
        col < wide - 1, pltpu.roll(acc_in[0].reshape(2 * flat, ins), 2 * flat - 1, 0), 0.0
    )
    value = value + jnp.where(col > 0, pltpu.roll(acc_in[2].reshape(2 * flat, ins), 1, 0), 0.0)
    value = value.reshape(2, flat, ins)
    acc_in[1] = value
    in_b[...] = value.astype(jnp.bfloat16)
    send(in_b.at[:, mate_half, :], in_got, 14, part)
    f_line.line(1, 2, 3)
    x_line.rest(0, 1, 2, 3)
    e_line.side(0, 1, 2, 3)
    h_line.side(1, 2, 3)
    lane = lax.broadcasted_iota(jnp.int32, (share, flat), 1)
    row, col = lane // wide, lane % wide

    def fill(zz):
        def one(block, carry):
            for p in range(2):
                errors = f_full[zz, block // 2, block % 2, :, p * flat : (p + 1) * flat].astype(jnp.float32)
                start = pl.multiple_of((2 * block + p) * flat, flat)
                for ky in range(3):
                    for kz in range(3):
                        by = (ky - 1) * wide + (kz - 1)
                        there_y, there_z = row - (ky - 1), col - (kz - 1)
                        inside = (there_y >= 0) & (there_y < high) & (there_z >= 0) & (there_z < wide)
                        rolled = pltpu.roll(errors, by % flat, 1) if by else errors
                        at = (ky * 3 + kz) * share
                        moved[at : at + share, pl.ds(start, flat)] = jnp.where(inside, rolled, 0.0).astype(
                            jnp.bfloat16
                        )
            return carry

        lax.fori_loop(0, 4, one, 0)

    def gather_taps(zz, fresh):
        def tap(kx, carry):
            right = x_full[pl.ds(zz * 8 + kx, 8)].reshape(8 * flat, ins)
            term = dot_plain(moved[...], right).reshape(9, share, ins)
            found1[kx, :, core] = term if fresh else found1[kx, :, core] + term
            return carry

        lax.fori_loop(0, 3, tap, 0)

    def group(n):
        return lax.rem(here // 4 + deep - n, deep) if n else here // 4

    f_line.side(0)
    f_line.ended(0)
    fill(group(0))
    x_line.ended(0, 1, 2, 3)
    gather_taps(group(0), True)
    wait(in_b.at[:, my_half, :], in_got, 14)
    gin_out[...] = acc_in[1, :, my_half, :] + in_got[...].astype(jnp.float32)
    wait(sec.at[cot_rows], sec_out.at[:, :, mate_lanes], 10)
    keep_sec.wait()
    f_line.side(1)
    fill(group(1))
    gather_taps(group(1), False)
    h_line.rest(0, 1, 2, 3)
    f_line.side(2)
    fill(group(2))
    gather_taps(group(2), False)
    f_line.side(3)
    fill(group(3))
    for kx in range(3):
        right = x_full[pl.ds(group(deep - 1) * 8 + kx, 8)].reshape(8 * flat, ins)
        term = dot_plain(moved[...], right)
        found1[kx, :, core] = found1[kx, :, core] + term.reshape(9, share, ins)
        send(found1.at[kx, :, core], found1.at[kx, :, core], 16 + kx, x_line.to_c)
    e_line.ended(0, 1, 2, 3)
    h_line.ended(0, 1, 2, 3)
    total = count * cells
    errors = jnp.transpose(e_full[...].reshape(total, outs).astype(jnp.float32))
    lane = lax.broadcasted_iota(jnp.int32, (outs, total), 1)
    spot_y, spot_z, spot_x = lane % nh, (lane // nh) % nw, lane // cells
    turned_by = {}
    for a in range(2):
        for b in range(2):
            for c in range(2):
                by = a * cells + c * nh + b
                ok = (spot_x + a < count) & (spot_y + b < nh) & (spot_z + c < nw)
                rolled = pltpu.roll(errors, total - by, 1) if by else errors
                turned_by[a, b, c] = jnp.where(ok, rolled, 0.0).astype(jnp.bfloat16)
    for kind in range(8):
        px, py, pz = kind // 4, (kind // 2) % 2, kind % 2
        taps = [
            (kx, ky, kz)
            for kx in ((0, 2) if px else (1,))
            for ky in ((0, 2) if py else (1,))
            for kz in ((0, 2) if pz else (1,))
        ]
        left = jnp.concatenate([turned_by[int(kx == 0), int(ky == 0), int(kz == 0)] for kx, ky, kz in taps], 0)
        term = dot_plain(left, h_full[:, :, :, kind].reshape(total, ins))
        for n, (kx, ky, kz) in enumerate(taps):
            found2[(kx * 3 + ky) * 3 + kz] = term[n * outs : (n + 1) * outs]
    for kx in range(3):
        wait(found1.at[kx, :, core], found1.at[kx, :, 1 - core], 16 + kx)
    x_line.sent()
    e_line.sent()
    h_line.sent()
    f_line.sent()
    for copy, cond in started:
        if cond is None:
            copy.wait_send()
        else:
            pl.when(cond)(copy.wait_send)


def chain(x, w1, w2, cot):
    count = lax.axis_size("sp")
    planes, high, wide, ins = x.shape
    high = high * 2
    outs = w1.shape[1]
    flat = high * wide
    nh, nw = high // 2, wide // 2
    cells = nh * nw
    deep = count // 4
    dma = pltpu.SemaphoreType.DMA
    bf, f32 = jnp.bfloat16, jnp.float32
    anywhere = pl.BlockSpec(memory_space=pl.ANY)
    shape = jax.ShapeDtypeStruct
    return pl.pallas_call(
        functools.partial(chain_kernel, (count, high, wide, ins, outs)),
        out_shape=[
            shape(cot.shape, f32),
            shape((planes, flat // 2, ins), f32),
            pltpu.VMEM((3, 9, 2, outs // 2, ins), f32),
            pltpu.VMEM((27, outs, ins), f32),
        ],
        in_specs=[anywhere] * 4,
        out_specs=[anywhere, VMEM, VMEM, VMEM],
        scratch_shapes=[
            pltpu.VMEM(w1.shape, bf),
            pltpu.VMEM(w2.shape, bf),
            pltpu.VMEM((4, flat, ins), bf),
            pltpu.VMEM((nh, nw, outs), bf),
            pltpu.VMEM((nh, nw, outs), f32),
            pltpu.VMEM((2, flat, 3 * outs), f32),
            pltpu.VMEM((2 * flat, outs), f32),
            pltpu.VMEM((8, cells, outs), f32),
            pltpu.VMEM((8, cells, outs), f32),
            pltpu.VMEM((8, cells, outs), bf),
            pltpu.VMEM((12, cells, ins), bf),
            pltpu.VMEM((nh, nw, outs), f32),
            pltpu.VMEM((cells, outs), bf),
            pltpu.VMEM((cells, outs), bf),
            pltpu.VMEM((2, 8, cells, outs), f32),
            pltpu.VMEM((2, 8, cells, outs), bf),
            pltpu.VMEM((8, cells, outs), bf),
            pltpu.VMEM((4, flat, outs), bf),
            pltpu.VMEM((2, outs // 2, 2 * flat), bf),
            pltpu.VMEM((3, 2, flat, ins), f32),
            pltpu.VMEM((2, flat, ins), bf),
            pltpu.VMEM((2, flat // 2, ins), bf),
            pltpu.VMEM((planes * count + 2, flat, ins), bf),
            pltpu.VMEM((deep, 2, 2, 8, cells, ins), bf),
            pltpu.VMEM((deep, 2, 2, cells, outs), bf),
            pltpu.VMEM((deep, 2, 2, outs // 2, planes * flat), bf),
            pltpu.VMEM((2, outs // 2, planes * flat), bf),
            pltpu.VMEM((9 * outs // 2, 8 * flat), bf),
            dma((7,)),
            dma((19,)),
            dma((19,)),
            dma((4,)),
            dma((4, spread_sends(deep))),
            dma((4, spread_slots(deep))),
        ],
        compiler_params=pltpu.CompilerParams(
            collective_id=1, has_side_effects=True, vmem_limit_bytes=40 * 1024 * 1024
        ),
    )(*(pltpu.with_memory_space_constraint(a, pltpu.HBM) for a in (x.reshape(planes, flat // 2, ins), w1, w2, cot)))


def write_kernel(*refs):
    sources, places, sem = refs[:4], refs[4:8], refs[8]
    copies = [pltpu.make_async_copy(src, dst, sem.at[n]) for n, (src, dst) in enumerate(zip(sources, places))]
    for copy in copies:
        copy.start()
    for copy in copies:
        copy.wait()


def write(*arrays):
    anywhere = pl.BlockSpec(memory_space=pl.ANY)
    return pl.pallas_call(
        write_kernel,
        out_shape=[jax.ShapeDtypeStruct(a.shape, a.dtype) for a in arrays],
        in_specs=[anywhere] * 4,
        out_specs=[anywhere] * 4,
        scratch_shapes=[pltpu.SemaphoreType.DMA((4,))],
        compiler_params=pltpu.CompilerParams(vmem_limit_bytes=GRANT),
    )(*arrays)


def taps_first(kernel):
    moved = jnp.transpose(kernel, (1, 2, 3, 0, 4))
    return moved.reshape((27,) + moved.shape[3:])


def per_device_pair(activations, w_first, w_second, cotangent):
    planes, part, wide, ins = activations.shape
    outs = w_first.shape[0]

    def home(found):
        return jnp.transpose(found.reshape(3, 3, 3, outs, ins), (3, 0, 1, 2, 4))

    found = chain(activations, taps_first(w_first), taps_first(w_second), cotangent[0])
    sec, gin, grad_first, grad_second = write(*found)
    grad_first, grad_second = home(grad_first), home(grad_second)
    return sec[None], gin.reshape(activations.shape), grad_first, grad_second


def per_device_any(activations, w_first, w_second, cotangent):
    planes, part, wide, ins = activations.shape
    outs = w_first.shape[0]
    pair = (
        lax.axis_size("flt") == 2
        and planes == 2
        and wide == 8
        and part % 8 == 0
        and outs % 128 == 0
        and cotangent.shape[0] == 1
    )
    run = per_device_pair if pair else per_device
    return run(activations, w_first, w_second, cotangent)


def solution(mesh):
    placed = (
        P("sp", "flt", None, None),
        P("flt", None, None, None, None),
        P("flt", None, None, None, None),
        P("sp", "flt", None, None),
    )
    return jax.shard_map(
        per_device_any,
        mesh=mesh,
        in_specs=placed,
        out_specs=(
            P("sp", "flt", None, None),
            P("sp", "flt", None, None),
            P("flt", None, None, None, None),
            P("flt", None, None, None, None),
        ),
        check_vma=False,
    )
```
